32 devices in a mesh: groups: 2 (over y), rows: 4 (over z), tm: 2 (over x), cols: 2 (over core).
Axes of the slice: x: 2, y: 2, z: 4, core: 2. Of those that a mesh axis runs over, the one named last changes fastest.
Arguments:
- latents: bfloat16 [20, 4, 80, 384], P(('groups', 'tm'), 'rows', 'cols'), parts along dimension 0, may hold values from -16 to 16
- gain_one: float32 [384], replicated, may hold values from 0.1 to 1.9
- conv_one: bfloat16 [27, 384, 384], P(None, 'rows'), may hold values from -0.0625 to 0.0625
- bias_one: float32 [384], replicated, may hold values from -3 to 3
- gain_two: float32 [384], replicated, may hold values from 0.1 to 1.9
- conv_two: bfloat16 [27, 384, 384], P(None, 'rows'), may hold values from -0.0625 to 0.0625
- bias_two: float32 [384], replicated, may hold values from -3 to 3
Outputs:
- block_out: bfloat16 [20, 4, 80, 384], P(('groups', 'tm'), 'rows', 'cols'), parts along dimension 0
The draws below stay inside these ranges and needn't reach their ends.
There are 2 independent parts, one for each index of `groups`. The reference program is written for one: setup_inputs(seed, part) draws one part's arguments, and reference() takes and returns one part's arrays. A program takes and returns all parts, laid end to end along the dimension named above; an argument that names none is the same for every part. Nothing has to cross between parts.
All inputs are finite; a program needn't handle non-finite values.
Results may differ from the reference program's by a relative error of at most 0.006.
Values may be sent and summed in bfloat16 or wider, within the bound.
No kernel may reach another device: no remote copies, remote signals or barrier semaphores. Data moves between devices by JAX's collectives and lax.ppermute only.
A program may use at most 64 MiB of HBM per device.

```python
import math
import jax
import jax.numpy as jnp
from jax import lax

C = 384
FRAMES = 10
HEIGHT = 4
WIDTH = 80


def draw_latents(key, part):
    first_key = jax.random.fold_in(key, 11)
    second_key = jax.random.fold_in(key, 12)
    normal_part = jnp.clip(jax.random.normal(first_key, (FRAMES, HEIGHT, WIDTH, C), jnp.float32), -5.0, 5.0)
    channel_scale = jnp.exp(jax.random.uniform(second_key, (C,), jnp.float32, math.log(0.3), math.log(3.0)))
    values = normal_part * channel_scale
    return jnp.clip(values, -16.0, 16.0).astype(jnp.bfloat16)


def block_scale(stream_key, shape, pieces, least, largest):
    level, own = 1.0, jax.random.fold_in(stream_key, 6)
    for dim, parts in pieces:
        draws = jnp.exp(jax.random.uniform(jax.random.fold_in(own, dim), (parts,), jnp.float32, least / len(pieces), largest / len(pieces)))
        level = level * jnp.repeat(draws, shape[dim] // parts).reshape([-1 if axis == dim else 1 for axis in range(len(shape))])
    return level


def gaussian(rng, shape, scale, limit, shards=(), kind=jnp.bfloat16):
    drawn = jax.random.normal(rng, shape, jnp.float32) * scale
    if len(shards) > 0:
        drawn = block_scale(rng, shape, shards, -0.22, 0.18) * drawn
    return jnp.clip(drawn, min=-limit, max=limit).astype(kind)


def setup_inputs(seed: int = 0, part: int = 0) -> dict:
    seeds = jax.random.split(jax.random.key(seed), 8)
    part_splits = jax.random.split(jax.random.fold_in(seeds[7], part), 8)
    return {
        "latents": draw_latents(jax.random.fold_in(jax.random.fold_in(seeds[7], part), 71), part),
        "gain_one": jnp.clip(1.0 + 0.18 * jax.random.normal(seeds[1], (C,), jnp.float32), 0.1, 1.9),
        "conv_one": gaussian(seeds[2], (27, C, C), (27 * C) ** -0.5, 0.0625, ((1, 4),)),
        "bias_one": gaussian(seeds[3], (C,), 0.5, 3.0, (), jnp.float32),
        "gain_two": jnp.clip(1.0 + 0.18 * jax.random.normal(seeds[4], (C,), jnp.float32), 0.1, 1.9),
        "conv_two": gaussian(seeds[5], (27, C, C), (27 * C) ** -0.5, 0.0625, ((1, 4),)),
        "bias_two": gaussian(seeds[6], (C,), 0.5, 3.0, (), jnp.float32),
    }


def activate(values, gain_values):
    values = values.astype(jnp.float32)
    mean_square = lax.optimization_barrier(jnp.mean(values * values, axis=-1, keepdims=True))
    return jax.nn.silu(values * lax.rsqrt(mean_square + 1e-06) * gain_values).astype(jnp.bfloat16)

def convolve(inputs, weight, bias_values):
    frames, height, breadth, channels = inputs.shape
    padded = jnp.pad(inputs, ((2, 0), (1, 1), (1, 1), (0, 0)))
    summed = jnp.zeros((frames * height * breadth, weight.shape[1]), jnp.float32)
    for depth_tap in range(3):
        for row_tap in range(3):
            for col_tap in range(3):
                window = padded[depth_tap:depth_tap + frames, row_tap:row_tap + height, col_tap:col_tap + breadth]
                window = window.reshape(frames * height * breadth, channels)
                kernel = weight[9 * depth_tap + 3 * row_tap + col_tap]
                summed = summed + lax.dot_general(window, kernel, (((1,), (1,)), ((), ())), preferred_element_type=jnp.float32)
    return summed.reshape(frames, height, breadth, weight.shape[1]) + bias_values

def reference(latents, gain_one, conv_one, bias_one, gain_two, conv_two, bias_two):
    first_act = activate(latents, gain_one)
    first_out = convolve(first_act, conv_one, bias_one).astype(jnp.bfloat16)
    second_act = activate(first_out, gain_two)
    branch = convolve(second_act, conv_two, bias_two)
    return (latents.astype(jnp.float32) + branch).astype(jnp.bfloat16)
```

```python
import functools

import jax
import jax.numpy as jnp
from jax import lax
from jax.experimental import pallas as pl
from jax.experimental.pallas import tpu as pltpu
from jax.sharding import PartitionSpec as P


AXES = ("rows", "tm", "cols")
EDGE = 2
PAST = 2
TAPS = 3
VMEM = pltpu.VMEM


def activate(values, gain_values):
    values = values.astype(jnp.float32)
    mean_square = jnp.mean(values * values, axis=-1, keepdims=True)
    return jax.nn.silu(values * lax.rsqrt(mean_square + 1e-06) * gain_values)


def call(body, name, out_shape, scratch, flops, moved, *operands):
    return pl.pallas_call(
        body,
        name=name,
        out_shape=out_shape,
        in_specs=[pl.BlockSpec(memory_space=VMEM)] * len(operands),
        out_specs=jax.tree.map(lambda _: pl.BlockSpec(memory_space=VMEM), out_shape),
        scratch_shapes=scratch,
        cost_estimate=pl.CostEstimate(flops=flops, bytes_accessed=moved, transcendentals=0),
        compiler_params=pltpu.CompilerParams(vmem_limit_bytes=48 << 20),
    )(*operands)


def act_body(own_ref, other_ref, gain_ref, out_ref):
    frames, breadth, channels = own_ref.shape
    ring = out_ref.shape[1]
    gain_values = gain_ref[...]
    half = lax.axis_index("cols")
    right = activate(other_ref[:, 0:EDGE], gain_values)
    left = activate(other_ref[:, breadth - EDGE : breadth], gain_values)
    right = jnp.where(half == 0, right, 0.0)
    left = jnp.where(half == 1, left, 0.0)
    gap = jnp.zeros((frames, ring - breadth - 2 * EDGE, channels), jnp.float32)
    own = activate(own_ref[...], gain_values)
    out_ref[...] = jnp.concatenate([own, right, gap, left], axis=1).astype(jnp.bfloat16)


def conv_sum(padded, weight_ref, bias_row):
    frames, height, ring, channels = padded.shape[0] - PAST, padded.shape[1] - 2, padded.shape[2], padded.shape[3]
    width = weight_ref.shape[1] // TAPS
    count = frames * height * ring
    windows = [
        padded[t : t + frames, r : r + height].reshape(count, channels) for t in range(TAPS) for r in range(TAPS)
    ]
    kernels = [weight_ref[i] for i in range(TAPS * TAPS)]
    product = lax.dot_general(
        jnp.concatenate(windows, axis=1),
        jnp.concatenate(kernels, axis=1),
        (((1,), (1,)), ((), ())),
        preferred_element_type=jnp.float32,
    )
    product = product.reshape(frames * height, ring, TAPS * width)
    before = pltpu.roll(product[:, :, 0:width], 1, 1)
    after = pltpu.roll(product[:, :, 2 * width : 3 * width], ring - 1, 1)
    summed = before + product[:, :, width : 2 * width] + after + bias_row
    return summed.reshape(frames, height, ring, width)


def fill(padded, pieces, past_ref, order):
    block = lax.axis_index("tm") // 2 * 2 + lax.axis_index("cols")
    height = padded.shape[1] - 2
    edge = jnp.zeros((padded.shape[0],) + padded.shape[2:], padded.dtype)
    padded[:, 0] = edge
    padded[:, height + 1] = edge
    for k, piece in enumerate(pieces):
        row = order(k) + 1
        padded[PAST:, row] = piece[...]
        past = past_ref[k]
        padded[0:PAST, row] = jnp.where(block > 0, past, jnp.zeros_like(past))


def first_body(*refs):
    *pieces, past_ref, weight_ref, bias_ref, out_ref, padded = refs
    row = lax.axis_index("rows")
    fill(padded, pieces, past_ref, lambda k: row ^ k)
    summed = conv_sum(padded, weight_ref, bias_ref[pl.ds(row, 1), :])
    frames, height, ring, width = summed.shape
    packed = [summed[:, h].reshape(frames * ring, width) for h in range(height)]
    out_ref[...] = jnp.concatenate(packed, axis=1).astype(jnp.bfloat16)


def regroup_body(*refs):
    *pieces, gain_ref, out_ref, held = refs
    row = lax.axis_index("rows")
    half = lax.axis_index("tm") % 2
    height, frames, ring, channels = out_ref.shape
    width = channels // height
    for k, piece in enumerate(pieces):
        held[row ^ k] = piece[...].astype(jnp.float32)
    gain_values = gain_ref[...]
    column = lax.broadcasted_iota(jnp.int32, (frames, ring, channels), 1)
    breadth = ring - 8
    kept = jnp.where(half == 0, breadth, ring - 1)
    inside = (column < breadth) | (column == kept)
    for h in range(height):
        joined = [held[s, :, h * width : (h + 1) * width] for s in range(height)]
        values = activate(jnp.concatenate(joined, axis=1), gain_values).reshape(frames, ring, channels)
        out_ref[h] = jnp.where(inside, values, 0.0).astype(jnp.bfloat16)


def second_body(act_ref, past_ref, weight_ref, bias_ref, *refs):
    *outs, padded, held = refs
    row = lax.axis_index("rows")
    height = act_ref.shape[0]
    fill(padded, [act_ref.at[h] for h in range(height)], past_ref, lambda k: k)
    summed = conv_sum(padded, weight_ref, bias_ref[pl.ds(row, 1), :])
    breadth = summed.shape[2] - 8
    for h in range(height):
        held[h] = summed[:, h, 0:breadth]
    for k, out_ref in enumerate(outs):
        out_ref[...] = held[row ^ k].astype(jnp.bfloat16)


def last_body(latents_ref, *refs):
    *pieces, out_ref, held = refs
    row = lax.axis_index("rows")
    for k, piece in enumerate(pieces):
        held[row ^ k] = piece[...].astype(jnp.float32)
    branch = jnp.concatenate([held[s] for s in range(len(pieces))], axis=2)
    out_ref[...] = (latents_ref[...].astype(jnp.float32) + branch).astype(jnp.bfloat16)


def shards(shape, latents, gain_one, conv_one, bias_one, gain_two, conv_two, bias_two):
    rows, tm, cols = (shape[name] for name in AXES)
    frames, height, breadth, channels = latents.shape
    width = channels // rows
    ring = breadth + 8
    bf16, f32 = jnp.bfloat16, jnp.float32
    own = latents.reshape(frames, breadth, channels)
    every = [(z, x, c) for z in range(rows) for x in range(tm) for c in range(cols)]
    place = {device: i for i, device in enumerate(every)}

    def moved(values, target):
        pairs = [(place[device], place[target(*device)]) for device in every if target(*device) in place]
        return lax.ppermute(values, AXES, pairs)

    def turned(values, k):
        return moved(values, lambda z, x, c: (z ^ k, x // 2 * 2 + c, x % 2))

    def following(values):
        return moved(values, lambda z, x, c: (z, x, 1) if c == 0 else (z, (x + 2) % tm, 0))

    other = lax.ppermute(own, "cols", [(0, 1), (1, 0)])
    gains = [g.reshape(1, channels) for g in (gain_one, gain_two)]
    biases = [b.reshape(rows, width) for b in (bias_one, bias_two)]
    weights = [w.reshape(TAPS * TAPS, TAPS * width, channels) for w in (conv_one, conv_two)]
    sds = jax.ShapeDtypeStruct
    size = frames * ring * channels
    work = 2 * size * rows * 27 * width
    padded = VMEM((frames + PAST, rows + 2, ring, channels), bf16)

    act = call(act_body, "act", sds((frames, ring, channels), bf16), [], 10 * size, 6 * size, own, other, gains[0])
    pieces = [turned(act, k) for k in range(rows)]
    past = following(jnp.stack([piece[frames - PAST :] for piece in pieces]))
    part = call(
        first_body, "first", sds((frames * ring, rows * width), bf16), [padded], work, 20 * size,
        *pieces, past, weights[0], biases[0],
    )
    parts = [part] + [lax.ppermute(part, "rows", [(z, z ^ k) for z in range(rows)]) for k in range(1, rows)]
    second = call(
        regroup_body, "regroup", sds((rows, frames, ring, channels), bf16),
        [VMEM((rows, frames * ring, channels), f32)], 10 * size * rows, 4 * size * rows, *parts, gains[1],
    )
    past = following(second[:, frames - PAST :])
    branch = call(
        second_body, "second", [sds((frames, breadth, width), bf16)] * rows,
        [padded, VMEM((rows, frames, breadth, width), f32)], work, 20 * size,
        second, past, weights[1], biases[1],
    )
    branch = [turned(piece, k) for k, piece in enumerate(branch)]
    result = call(
        last_body, "last", sds((frames, breadth, channels), bf16), [VMEM((rows, frames, breadth, width), f32)],
        2 * size, 6 * size, own, *branch,
    )
    return result.reshape(frames, height, breadth, channels)


def solution(mesh):
    shape = dict(mesh.shape)
    return jax.shard_map(
        functools.partial(shards, shape),
        mesh=mesh,
        in_specs=(
            P(("groups", "tm"), "rows", "cols", None),
            P(),
            P(None, "rows", None),
            P(),
            P(),
            P(None, "rows", None),
            P(),
        ),
        out_specs=P(("groups", "tm"), "rows", "cols", None),
        check_vma=False,
    )
```

```python
import functools

import jax
import jax.numpy as jnp
from jax import lax
from jax.experimental import pallas as pl
from jax.experimental.pallas import tpu as pltpu
from jax.sharding import PartitionSpec as P


AXES = ("rows", "tm", "cols")
EDGE = 2
PAST = 2
TAPS = 3
VMEM = pltpu.VMEM


def activate(values, gain_values):
    values = values.astype(jnp.float32)
    mean_square = jnp.mean(values * values, axis=-1, keepdims=True)
    return jax.nn.silu(values * lax.rsqrt(mean_square + 1e-06) * gain_values)


def call(body, name, out_shape, scratch, flops, moved, *operands):
    return pl.pallas_call(
        body,
        name=name,
        out_shape=out_shape,
        in_specs=[pl.BlockSpec(memory_space=VMEM)] * len(operands),
        out_specs=jax.tree.map(lambda _: pl.BlockSpec(memory_space=VMEM), out_shape),
        scratch_shapes=scratch,
        cost_estimate=pl.CostEstimate(flops=flops, bytes_accessed=moved, transcendentals=0),
        compiler_params=pltpu.CompilerParams(vmem_limit_bytes=48 << 20),
    )(*operands)


def ring_of(center, right, left):
    gap = jnp.zeros((8 - right.shape[0] - left.shape[0], center.shape[1]), center.dtype)
    return jnp.concatenate([center, right, gap, left], axis=0)


def padded_rows(count):
    return -(-count // 8) * 8


def own_part(vector, row, width):
    parts = vector.shape[1] // width
    return sum(jnp.where(row == s, vector[:, s * width : (s + 1) * width], 0.0) for s in range(parts))


def act_body(own_ref, other_ref, gain_ref, out_ref):
    frames, breadth, channels = own_ref.shape
    gain_values = gain_ref[...].reshape(1, channels)
    half = lax.axis_index("cols")
    right = jnp.where(half == 0, activate(other_ref[:, 0:EDGE], gain_values), 0.0)
    left = jnp.where(half == 1, activate(other_ref[:, breadth - EDGE : breadth], gain_values), 0.0)
    own = activate(own_ref[...], gain_values).reshape(frames * breadth, channels)
    ends = [edge[f] for f in range(frames) for edge in (right, left)]
    rest = out_ref.shape[0] - own.shape[0] - 2 * EDGE * frames
    ends.append(jnp.zeros((rest, channels), jnp.float32))
    out_ref[...] = jnp.concatenate([own] + ends, axis=0).astype(jnp.bfloat16)


def clear_ends(padded):
    edge = jnp.zeros((padded.shape[0],) + padded.shape[2:], padded.dtype)
    padded[:, 0] = edge
    padded[:, padded.shape[1] - 1] = edge


def fill_first(padded, at, rows_values, breadth, picks, ends):
    values = rows_values.astype(jnp.float32)
    for i, (frame, end) in enumerate(zip(picks, ends)):
        center = values[frame * breadth : (frame + 1) * breadth]
        right, left = values[end : end + EDGE], values[end + EDGE : end + 2 * EDGE]
        padded[i + at[0], at[1]] = ring_of(center, right, left).astype(jnp.bfloat16)


def conv_sum(padded, weight_ref, bias_row):
    frames, height, ring, channels = padded.shape[0] - PAST, padded.shape[1] - 2, padded.shape[2], padded.shape[3]
    width = weight_ref.shape[1] // TAPS
    count = frames * height * ring
    windows = [
        padded[t : t + frames, r : r + height].reshape(count, channels) for t in range(TAPS) for r in range(TAPS)
    ]
    kernels = [weight_ref[i] for i in range(TAPS * TAPS)]
    product = lax.dot_general(
        jnp.concatenate(windows, axis=1),
        jnp.concatenate(kernels, axis=1),
        (((1,), (1,)), ((), ())),
        preferred_element_type=jnp.float32,
    )
    product = product.reshape(frames * height, ring, TAPS * width)
    before = pltpu.roll(product[:, :, 0:width], 1, 1)
    after = pltpu.roll(product[:, :, 2 * width : 3 * width], ring - 1, 1)
    summed = before + product[:, :, width : 2 * width] + after + bias_row
    return summed.reshape(frames, height, ring, width)


def block_number():
    return lax.axis_index("tm") // 2 * 2 + lax.axis_index("cols")


def pack_first(summed, out_ref, breadth):
    frames, height, ring, width = summed.shape
    rest = out_ref.shape[0] - frames * (breadth + 2)
    packed = []
    for h in range(height):
        centers = [summed[f, h, 0:breadth] for f in range(frames)]
        ends = [summed[f, h, w : w + 1] for f in range(frames) for w in (breadth, ring - 1)]
        if rest:
            ends.append(jnp.zeros((rest, width), jnp.float32))
        packed.append(jnp.concatenate(centers + ends, axis=0))
    out_ref[...] = jnp.concatenate(packed, axis=1).astype(jnp.bfloat16)


def first_late_body(breadth, *refs):
    *pieces, weight_ref, bias_ref, out_ref, padded = refs
    row = lax.axis_index("rows")
    clear_ends(padded)
    frames = padded.shape[0]
    ends = [frames * breadth + 2 * EDGE * f for f in range(frames)]
    for k, piece in enumerate(pieces):
        fill_first(padded, (0, (row ^ k) + 1), piece[...], breadth, range(frames), ends)
    bias_row = own_part(bias_ref[...].reshape(1, -1), row, weight_ref.shape[1] // TAPS)
    pack_first(conv_sum(padded, weight_ref, bias_row), out_ref, breadth)


def first_early_body(breadth, frames, *refs):
    *pieces, past_ref, weight_ref, bias_ref, out_ref, padded = refs
    row = lax.axis_index("rows")
    clear_ends(padded)
    total = frames * breadth
    skipped = (frames - PAST) * breadth
    for k, piece in enumerate(pieces):
        past = past_ref[k]
        past = jnp.where(block_number() > 0, past, jnp.zeros_like(past))
        ends = [total + 2 * EDGE * (frames - PAST + j) - skipped for j in range(PAST)]
        fill_first(padded, (0, (row ^ k) + 1), past, breadth, range(PAST), ends)
        ends = [total + 2 * EDGE * j for j in range(PAST)]
        fill_first(padded, (PAST, (row ^ k) + 1), piece[...], breadth, range(PAST), ends)
    bias_row = own_part(bias_ref[...].reshape(1, -1), row, weight_ref.shape[1] // TAPS)
    pack_first(conv_sum(padded, weight_ref, bias_row), out_ref, breadth)


def regroup(pieces, gain_ref, held, breadth, frames, store):
    row = lax.axis_index("rows")
    half = lax.axis_index("tm") % 2
    height, channels = len(pieces), pieces[0].shape[1]
    width = channels // height
    for k, piece in enumerate(pieces):
        held[row ^ k] = piece[...].astype(jnp.float32)
    gain_values = gain_ref[...].reshape(1, channels)
    for h in range(height):
        joined = [held[s, :, h * width : (h + 1) * width] for s in range(height)]
        values = activate(jnp.concatenate(joined, axis=1), gain_values)
        for f in range(frames):
            end = frames * breadth + 2 * f
            right = jnp.where(half == 0, values[end : end + 1], 0.0)
            left = jnp.where(half == 1, values[end + 1 : end + 2], 0.0)
            ring = ring_of(values[f * breadth : (f + 1) * breadth], right, left)
            store(h, f, ring.astype(jnp.bfloat16))


def regroup_body(breadth, *refs):
    *pieces, gain_ref, out_ref, last_ref, held = refs
    middle, late = out_ref.shape[1], last_ref.shape[1]

    def store(h, f, ring):
        if f < middle:
            out_ref[h, f] = ring
        else:
            last_ref[h, f - middle] = ring

    regroup(pieces, gain_ref, held, breadth, middle + late, store)


def second_body(breadth, *refs):
    height = (len(refs) - 9) // 2
    pieces, refs = refs[:height], refs[height:]
    middle_ref, last_ref, past_ref, gain_ref, weight_ref, bias_ref = refs[:6]
    outs, (padded, held, branch) = refs[6 : 6 + height], refs[6 + height :]
    row = lax.axis_index("rows")
    clear_ends(padded)

    def store(h, f, ring):
        padded[PAST + f, h + 1] = ring

    regroup(pieces, gain_ref, held, breadth, PAST, store)
    middle, late = middle_ref.shape[1], last_ref.shape[1]
    for h in range(height):
        past = past_ref[h]
        padded[0:PAST, h + 1] = jnp.where(block_number() > 0, past, jnp.zeros_like(past))
        padded[2 * PAST : 2 * PAST + middle, h + 1] = middle_ref[h]
        padded[2 * PAST + middle : 2 * PAST + middle + late, h + 1] = last_ref[h]
    bias_row = own_part(bias_ref[...].reshape(1, -1), row, weight_ref.shape[1] // TAPS)
    summed = conv_sum(padded, weight_ref, bias_row)
    frames, width = summed.shape[0], summed.shape[3]
    for h in range(height):
        branch[h, 0 : frames * breadth] = summed[:, h, 0:breadth].reshape(frames * breadth, width)
    for k, out_ref in enumerate(outs):
        chosen = branch[row ^ k]
        rows = out_ref.shape[0]
        parts = [chosen[i * rows : (i + 1) * rows] for i in range(height)]
        out_ref[...] = jnp.concatenate(parts, axis=1).astype(jnp.bfloat16)


def last_body(latents_ref, *refs):
    *pieces, out_ref, held = refs
    row = lax.axis_index("rows")
    height = len(pieces)
    frames, breadth, channels = latents_ref.shape
    width = channels // height
    for k, piece in enumerate(pieces):
        values = piece[...].astype(jnp.float32)
        parts = [values[:, i * width : (i + 1) * width] for i in range(height)]
        held[row ^ k] = jnp.concatenate(parts, axis=0)
    branch = jnp.concatenate([held[s] for s in range(height)], axis=1)
    branch = branch[0 : frames * breadth].reshape(frames, breadth, channels)
    out_ref[...] = (latents_ref[...].astype(jnp.float32) + branch).astype(jnp.bfloat16)


def shards(shape, latents, gain_one, conv_one, bias_one, gain_two, conv_two, bias_two):
    rows, tm, cols = (shape[name] for name in AXES)
    frames, height, breadth, channels = latents.shape
    width = channels // rows
    ring = breadth + 8
    late, middle = frames - PAST, frames - 2 * PAST
    bf16, f32 = jnp.bfloat16, jnp.float32
    own = latents.reshape(frames, breadth, channels)
    every = [(z, x, c) for z in range(rows) for x in range(tm) for c in range(cols)]
    place = {device: i for i, device in enumerate(every)}

    def moved(values, target):
        return lax.ppermute(values, AXES, [(place[device], place[target(*device)]) for device in every])

    def turned(values, k):
        return moved(values, lambda z, x, c: (z ^ k, x // 2 * 2 + c, x % 2))

    def following(values):
        return moved(values, lambda z, x, c: (z, x, 1) if c == 0 else (z, (x + 2) % tm, 0))

    def spread(values):
        return [values] + [lax.ppermute(values, "rows", [(z, z ^ k) for z in range(rows)]) for k in range(1, rows)]

    other = lax.ppermute(own, "cols", [(0, 1), (1, 0)])
    weights = [w.reshape(TAPS * TAPS, TAPS * width, channels) for w in (conv_one, conv_two)]
    sds = jax.ShapeDtypeStruct
    size = frames * ring * channels
    work = 2 * ring * channels * rows * 27 * width

    def padded(count):
        return VMEM((count, rows + 2, ring, channels), bf16)

    total = padded_rows(frames * (breadth + 2 * EDGE))
    act = call(act_body, "act", sds((total, channels), bf16), [], 10 * size, 6 * size, own, other, gain_one)
    pieces = [turned(act, k) for k in range(rows)]
    past = following(jnp.stack([piece[late * breadth :] for piece in pieces]))
    late_rows, early_rows = padded_rows(late * (breadth + 2)), padded_rows(PAST * (breadth + 2))
    part = call(
        functools.partial(first_late_body, breadth), "first_late", sds((late_rows, channels), bf16), [padded(frames)],
        late * work, 20 * size, *pieces, weights[0], bias_one,
    )
    late_parts = spread(part)
    part = call(
        functools.partial(first_early_body, breadth, frames), "first_early", sds((early_rows, channels), bf16),
        [padded(2 * PAST)], PAST * work, 20 * size, *pieces, past, weights[0], bias_one,
    )
    early_parts = spread(part)
    second, last = call(
        functools.partial(regroup_body, breadth), "regroup",
        [sds((rows, middle, ring, channels), bf16), sds((rows, PAST, ring, channels), bf16)],
        [VMEM((rows, late_rows, channels), f32)], 10 * size * rows, 4 * size * rows, *late_parts, gain_two,
    )
    past = following(last)
    back_rows = padded_rows(-(-frames * breadth // rows))
    branch = call(
        functools.partial(second_body, breadth), "second", [sds((back_rows, channels), bf16)] * rows,
        [padded(frames + PAST), VMEM((rows, early_rows, channels), f32), VMEM((rows, back_rows * rows, width), f32)],
        frames * work, 20 * size, *early_parts, second, last, past, gain_two, weights[1], bias_two,
    )
    branch = [turned(piece, k) for k, piece in enumerate(branch)]
    result = call(
        last_body, "last", sds((frames, breadth, channels), bf16), [VMEM((rows, back_rows * rows, width), f32)],
        2 * size, 6 * size, own, *branch,
    )
    return result.reshape(frames, height, breadth, channels)


def solution(mesh):
    shape = dict(mesh.shape)
    return jax.shard_map(
        functools.partial(shards, shape),
        mesh=mesh,
        in_specs=(
            P(("groups", "tm"), "rows", "cols", None),
            P(),
            P(None, "rows", None),
            P(),
            P(),
            P(None, "rows", None),
            P(),
        ),
        out_specs=P(("groups", "tm"), "rows", "cols", None),
        check_vma=False,
    )
```

```python
import functools

import jax
import jax.numpy as jnp
from jax import lax
from jax.experimental import pallas as pl
from jax.experimental.pallas import tpu as pltpu
from jax.sharding import PartitionSpec as P


AXES = ("rows", "tm", "cols")
EDGE = 2
PAST = 2
TAPS = 3
VMEM = pltpu.VMEM


def activate(values, gain_values):
    values = values.astype(jnp.float32)
    mean_square = jnp.mean(values * values, axis=-1, keepdims=True)
    return jax.nn.silu(values * lax.rsqrt(mean_square + 1e-06) * gain_values)


def call(body, out_shape, scratch, flops, moved, *operands, far=()):
    operands = [pltpu.with_memory_space_constraint(v, pltpu.HBM) if i in far else v for i, v in enumerate(operands)]
    spaces = [pltpu.HBM if i in far else VMEM for i in range(len(operands))]
    return pl.pallas_call(
        body,
        out_shape=out_shape,
        in_specs=[pl.BlockSpec(memory_space=space) for space in spaces],
        out_specs=jax.tree.map(lambda _: pl.BlockSpec(memory_space=VMEM), out_shape),
        scratch_shapes=scratch,
        cost_estimate=pl.CostEstimate(flops=flops, bytes_accessed=moved, transcendentals=0),
        compiler_params=pltpu.CompilerParams(vmem_limit_bytes=48 << 20),
    )(*operands)


def ring_of(center, right, left):
    gap = jnp.zeros((8 - right.shape[0] - left.shape[0], center.shape[1]), center.dtype)
    return jnp.concatenate([center, right, gap, left], axis=0)


def padded_rows(count):
    return -(-count // 8) * 8


def own_part(vector, row, width):
    parts = vector.shape[1] // width
    return sum(jnp.where(row == s, vector[:, s * width : (s + 1) * width], 0.0) for s in range(parts))


def own_body(own_ref, *refs):
    count = (len(refs) - 3) // 2
    far, out_ref, near, (held, sems) = refs[:count], refs[count], refs[count + 1 : 2 * count + 1], refs[2 * count + 1 :]
    copies = [pltpu.make_async_copy(a, b, sems.at[i]) for i, (a, b) in enumerate(zip((own_ref, *far), (held, *near)))]
    for copy in copies:
        copy.start()
    copies[0].wait()
    copies[1].wait()
    frames, breadth, channels = held.shape
    values = activate(held[...], near[0][...].reshape(1, channels))
    out_ref[...] = values.reshape(frames * breadth, channels).astype(jnp.bfloat16)
    for copy in copies[2:]:
        copy.wait()


def ends_body(center_ref, other_ref, gain_ref, out_ref):
    frames, breadth, channels = other_ref.shape
    gain_values = gain_ref[...].reshape(1, channels)
    half = lax.axis_index("cols")
    right = jnp.where(half == 0, activate(other_ref[:, 0:EDGE], gain_values), 0.0)
    left = jnp.where(half == 1, activate(other_ref[:, breadth - EDGE : breadth], gain_values), 0.0)
    ends = [edge[f] for f in range(frames) for edge in (right, left)]
    count = frames * breadth
    rest = out_ref.shape[0] - count - 2 * EDGE * frames
    ends.append(jnp.zeros((rest, channels), jnp.float32))
    out_ref[0:count] = center_ref[...]
    out_ref[count:] = jnp.concatenate(ends, axis=0).astype(jnp.bfloat16)


def clear_ends(padded):
    edge = jnp.zeros((padded.shape[0],) + padded.shape[2:], padded.dtype)
    padded[:, 0] = edge
    padded[:, padded.shape[1] - 1] = edge


def fill_first(padded, at, rows_values, breadth, picks, ends):
    values = rows_values.astype(jnp.float32)
    for i, (frame, end) in enumerate(zip(picks, ends)):
        center = values[frame * breadth : (frame + 1) * breadth]
        right, left = values[end : end + EDGE], values[end + EDGE : end + 2 * EDGE]
        padded[i + at[0], at[1]] = ring_of(center, right, left).astype(jnp.bfloat16)


def conv_sum(padded, weight_ref, bias_row):
    frames, height, ring, channels = padded.shape[0] - PAST, padded.shape[1] - 2, padded.shape[2], padded.shape[3]
    width = weight_ref.shape[1] // TAPS
    count = frames * height * ring
    windows = [
        padded[t : t + frames, r : r + height].reshape(count, channels) for t in range(TAPS) for r in range(TAPS)
    ]
    kernels = [weight_ref[i] for i in range(TAPS * TAPS)]
    product = lax.dot_general(
        jnp.concatenate(windows, axis=1),
        jnp.concatenate(kernels, axis=1),
        (((1,), (1,)), ((), ())),
        preferred_element_type=jnp.float32,
    )
    product = product.reshape(frames * height, ring, TAPS * width)
    before = pltpu.roll(product[:, :, 0:width], 1, 1)
    after = pltpu.roll(product[:, :, 2 * width : 3 * width], ring - 1, 1)
    summed = before + product[:, :, width : 2 * width] + after + bias_row
    return summed.reshape(frames, height, ring, width)


def block_number():
    return lax.axis_index("tm") // 2 * 2 + lax.axis_index("cols")


def pack_first(summed, out_ref, breadth):
    frames, height, ring, width = summed.shape
    rest = out_ref.shape[0] - frames * (breadth + 2)
    packed = []
    for h in range(height):
        centers = [summed[f, h, 0:breadth] for f in range(frames)]
        ends = [summed[f, h, w : w + 1] for f in range(frames) for w in (breadth, ring - 1)]
        if rest:
            ends.append(jnp.zeros((rest, width), jnp.float32))
        packed.append(jnp.concatenate(centers + ends, axis=0))
    out_ref[...] = jnp.concatenate(packed, axis=1).astype(jnp.bfloat16)


def first_late_body(breadth, *refs):
    *pieces, weight_ref, bias_ref, out_ref, padded = refs
    row = lax.axis_index("rows")
    clear_ends(padded)
    frames = padded.shape[0]
    ends = [frames * breadth + 2 * EDGE * f for f in range(frames)]
    for k, piece in enumerate(pieces):
        fill_first(padded, (0, (row ^ k) + 1), piece[...], breadth, range(frames), ends)
    bias_row = own_part(bias_ref[...].reshape(1, -1), row, weight_ref.shape[1] // TAPS)
    pack_first(conv_sum(padded, weight_ref, bias_row), out_ref, breadth)


def first_early_body(breadth, frames, *refs):
    *pieces, past_ref, weight_ref, bias_ref, out_ref, padded = refs
    row = lax.axis_index("rows")
    clear_ends(padded)
    total = frames * breadth
    skipped = (frames - PAST) * breadth
    for k, piece in enumerate(pieces):
        past = past_ref[k]
        past = jnp.where(block_number() > 0, past, jnp.zeros_like(past))
        ends = [total + 2 * EDGE * (frames - PAST + j) - skipped for j in range(PAST)]
        fill_first(padded, (0, (row ^ k) + 1), past, breadth, range(PAST), ends)
        ends = [total + 2 * EDGE * j for j in range(PAST)]
        fill_first(padded, (PAST, (row ^ k) + 1), piece[...], breadth, range(PAST), ends)
    bias_row = own_part(bias_ref[...].reshape(1, -1), row, weight_ref.shape[1] // TAPS)
    pack_first(conv_sum(padded, weight_ref, bias_row), out_ref, breadth)


def regroup(pieces, gain_ref, held, breadth, frames, store):
    row = lax.axis_index("rows")
    half = lax.axis_index("tm") % 2
    height, channels = len(pieces), pieces[0].shape[1]
    width = channels // height
    for k, piece in enumerate(pieces):
        held[row ^ k] = piece[...].astype(jnp.float32)
    gain_values = gain_ref[...].reshape(1, channels)
    for h in range(height):
        joined = [held[s, :, h * width : (h + 1) * width] for s in range(height)]
        values = activate(jnp.concatenate(joined, axis=1), gain_values)
        for f in range(frames):
            end = frames * breadth + 2 * f
            right = jnp.where(half == 0, values[end : end + 1], 0.0)
            left = jnp.where(half == 1, values[end + 1 : end + 2], 0.0)
            ring = ring_of(values[f * breadth : (f + 1) * breadth], right, left)
            store(h, f, ring.astype(jnp.bfloat16))


def regroup_body(breadth, *refs):
    *pieces, gain_ref, out_ref, last_ref, held = refs
    middle, late = out_ref.shape[1], last_ref.shape[1]

    def store(h, f, ring):
        if f < middle:
            out_ref[h, f] = ring
        else:
            last_ref[h, f - middle] = ring

    regroup(pieces, gain_ref, held, breadth, middle + late, store)


def second_body(breadth, *refs):
    height = (len(refs) - 9) // 2
    pieces, refs = refs[:height], refs[height:]
    middle_ref, last_ref, past_ref, gain_ref, weight_ref, bias_ref = refs[:6]
    outs, (padded, held, branch) = refs[6 : 6 + height], refs[6 + height :]
    row = lax.axis_index("rows")
    clear_ends(padded)

    def store(h, f, ring):
        padded[PAST + f, h + 1] = ring

    regroup(pieces, gain_ref, held, breadth, PAST, store)
    middle, late = middle_ref.shape[1], last_ref.shape[1]
    for h in range(height):
        past = past_ref[h]
        padded[0:PAST, h + 1] = jnp.where(block_number() > 0, past, jnp.zeros_like(past))
        padded[2 * PAST : 2 * PAST + middle, h + 1] = middle_ref[h]
        padded[2 * PAST + middle : 2 * PAST + middle + late, h + 1] = last_ref[h]
    bias_row = own_part(bias_ref[...].reshape(1, -1), row, weight_ref.shape[1] // TAPS)
    summed = conv_sum(padded, weight_ref, bias_row)
    frames, width = summed.shape[0], summed.shape[3]
    for h in range(height):
        branch[h, 0 : frames * breadth] = summed[:, h, 0:breadth].reshape(frames * breadth, width)
    for k, out_ref in enumerate(outs):
        chosen = branch[row ^ k]
        rows = out_ref.shape[0]
        parts = [chosen[i * rows : (i + 1) * rows] for i in range(height)]
        out_ref[...] = jnp.concatenate(parts, axis=1).astype(jnp.bfloat16)


def last_body(latents_ref, *refs):
    *pieces, out_ref, held = refs
    row = lax.axis_index("rows")
    height = len(pieces)
    frames, breadth, channels = latents_ref.shape
    width = channels // height
    for k, piece in enumerate(pieces):
        values = piece[...].astype(jnp.float32)
        parts = [values[:, i * width : (i + 1) * width] for i in range(height)]
        held[row ^ k] = jnp.concatenate(parts, axis=0)
    branch = jnp.concatenate([held[s] for s in range(height)], axis=1)
    branch = branch[0 : frames * breadth].reshape(frames, breadth, channels)
    out_ref[...] = (latents_ref[...].astype(jnp.float32) + branch).astype(jnp.bfloat16)


def shards(shape, latents, gain_one, conv_one, bias_one, gain_two, conv_two, bias_two):
    rows, tm, cols = (shape[name] for name in AXES)
    frames, height, breadth, channels = latents.shape
    width = channels // rows
    ring = breadth + 8
    late, middle = frames - PAST, frames - 2 * PAST
    bf16, f32 = jnp.bfloat16, jnp.float32
    own = latents.reshape(frames, breadth, channels)
    every = [(z, x, c) for z in range(rows) for x in range(tm) for c in range(cols)]
    place = {device: i for i, device in enumerate(every)}

    def moved(values, target):
        return lax.ppermute(values, AXES, [(place[device], place[target(*device)]) for device in every])

    def turned(values, k):
        return moved(values, lambda z, x, c: (z ^ k, x // 2 * 2 + c, x % 2))

    def following(values):
        return moved(values, lambda z, x, c: (z, x, 1) if c == 0 else (z, (x + 2) % tm, 0))

    def spread(values):
        return [values] + [lax.ppermute(values, "rows", [(z, z ^ k) for z in range(rows)]) for k in range(1, rows)]

    other = lax.ppermute(own, "cols", [(0, 1), (1, 0)])
    weights = [w.reshape(TAPS * TAPS, TAPS * width, channels) for w in (conv_one, conv_two)]
    sds = jax.ShapeDtypeStruct
    size = frames * ring * channels
    work = 2 * ring * channels * rows * 27 * width

    def padded(count):
        return VMEM((count, rows + 2, ring, channels), bf16)

    total = padded_rows(frames * (breadth + 2 * EDGE))
    small = (gain_one, bias_one, gain_two, bias_two, weights[0])
    center, gain_one, bias_one, gain_two, bias_two, near = call(
        own_body, [sds((frames * breadth, channels), bf16)] + [sds(v.shape, v.dtype) for v in small],
        [VMEM((frames, breadth, channels), bf16), pltpu.SemaphoreType.DMA((1 + len(small),))],
        10 * size, 6 * size, own, *small, far=range(1 + len(small)),
    )
    act = call(ends_body, sds((total, channels), bf16), [], size, 4 * size, center, other, gain_one)
    pieces = [turned(act, k) for k in range(rows)]
    past = following(jnp.stack([piece[late * breadth :] for piece in pieces]))
    late_rows, early_rows = padded_rows(late * (breadth + 2)), padded_rows(PAST * (breadth + 2))
    part = call(
        functools.partial(first_late_body, breadth), sds((late_rows, channels), bf16), [padded(frames)],
        late * work, 20 * size, *pieces, near, bias_one,
    )
    late_parts = spread(part)
    part = call(
        functools.partial(first_early_body, breadth, frames), sds((early_rows, channels), bf16),
        [padded(2 * PAST)], PAST * work, 20 * size, *pieces, past, near, bias_one,
    )
    early_parts = spread(part)
    second, last = call(
        functools.partial(regroup_body, breadth),
        [sds((rows, middle, ring, channels), bf16), sds((rows, PAST, ring, channels), bf16)],
        [VMEM((rows, late_rows, channels), f32)], 10 * size * rows, 4 * size * rows, *late_parts, gain_two,
    )
    past = following(last)
    back_rows = padded_rows(-(-frames * breadth // rows))
    branch = call(
        functools.partial(second_body, breadth), [sds((back_rows, channels), bf16)] * rows,
        [padded(frames + PAST), VMEM((rows, early_rows, channels), f32), VMEM((rows, back_rows * rows, width), f32)],
        frames * work, 20 * size, *early_parts, second, last, past, gain_two, weights[1], bias_two,
    )
    branch = [turned(piece, k) for k, piece in enumerate(branch)]
    result = call(
        last_body, sds((frames, breadth, channels), bf16), [VMEM((rows, back_rows * rows, width), f32)],
        2 * size, 6 * size, own, *branch,
    )
    return result.reshape(frames, height, breadth, channels)


def solution(mesh):
    shape = dict(mesh.shape)
    return jax.shard_map(
        functools.partial(shards, shape),
        mesh=mesh,
        in_specs=(
            P(("groups", "tm"), "rows", "cols", None),
            P(),
            P(None, "rows", None),
            P(),
            P(),
            P(None, "rows", None),
            P(),
        ),
        out_specs=P(("groups", "tm"), "rows", "cols", None),
        check_vma=False,
    )
```

```python
import functools

import jax
import jax.numpy as jnp
from jax import lax
from jax.experimental import pallas as pl
from jax.experimental.pallas import tpu as pltpu
from jax.sharding import PartitionSpec as P


AXES = ("rows", "tm", "cols")
EDGE = 2
PAST = 2
TAPS = 3
VMEM = pltpu.VMEM


def activate(values, gain_values):
    values = values.astype(jnp.float32)
    mean_square = jnp.mean(values * values, axis=-1, keepdims=True)
    return jax.nn.silu(values * lax.rsqrt(mean_square + 1e-06) * gain_values)


def call(body, out_shape, scratch, flops, moved, *operands, far=()):
    operands = [pltpu.with_memory_space_constraint(v, pltpu.HBM) if i in far else v for i, v in enumerate(operands)]
    spaces = [pltpu.HBM if i in far else VMEM for i in range(len(operands))]
    return pl.pallas_call(
        body,
        out_shape=out_shape,
        in_specs=[pl.BlockSpec(memory_space=space) for space in spaces],
        out_specs=jax.tree.map(lambda _: pl.BlockSpec(memory_space=VMEM), out_shape),
        scratch_shapes=scratch,
        cost_estimate=pl.CostEstimate(flops=flops, bytes_accessed=moved, transcendentals=0),
        compiler_params=pltpu.CompilerParams(vmem_limit_bytes=48 << 20),
    )(*operands)


def ring_of(center, end, half):
    gap = jnp.zeros((8 - end.shape[0], center.shape[1]), center.dtype)
    after = jnp.concatenate([end, gap], axis=0)
    before = jnp.concatenate([gap, end], axis=0)
    return jnp.concatenate([center, jnp.where(half == 0, after, before)], axis=0)


def padded_rows(count):
    return -(-count // 8) * 8


def own_part(vector, row, width):
    parts = vector.shape[1] // width
    return sum(jnp.where(row == s, vector[:, s * width : (s + 1) * width], 0.0) for s in range(parts))


def own_body(own_ref, far_gain_ref, out_ref, gain_ref, held, sems):
    copies = [
        pltpu.make_async_copy(own_ref, held, sems.at[0]),
        pltpu.make_async_copy(far_gain_ref, gain_ref, sems.at[1]),
    ]
    for copy in copies:
        copy.start()
    for copy in copies:
        copy.wait()
    frames, breadth, channels = held.shape
    values = activate(held[...], gain_ref[...].reshape(1, channels))
    out_ref[...] = values.reshape(frames * breadth, channels).astype(jnp.bfloat16)


def ends_body(other_ref, gain_ref, *refs):
    count = (len(refs) - 2) // 2
    far, out_ref, near, sems = refs[:count], refs[count], refs[count + 1 : 2 * count + 1], refs[2 * count + 1]
    copies = [pltpu.make_async_copy(a, b, sems.at[i]) for i, (a, b) in enumerate(zip(far, near))]
    for copy in copies:
        copy.start()
    frames, breadth, channels = other_ref.shape
    half = lax.axis_index("cols")
    chosen = jnp.where(half == 0, other_ref[:, 0:8].astype(jnp.float32), other_ref[:, breadth - 8 :].astype(jnp.float32))
    values = activate(chosen, gain_ref[...].reshape(1, channels))
    ends = [jnp.where(half == 0, values[f, 0:EDGE], values[f, 8 - EDGE : 8]) for f in range(frames)]
    rest = out_ref.shape[0] - EDGE * frames
    if rest:
        ends.append(jnp.zeros((rest, channels), jnp.float32))
    out_ref[...] = jnp.concatenate(ends, axis=0).astype(jnp.bfloat16)
    for copy in copies:
        copy.wait()


def fill_first(padded, at, centers, ends, picks, breadth):
    half = lax.axis_index("tm") % 2
    for i, (frame, end) in enumerate(picks):
        center = centers[frame * breadth : (frame + 1) * breadth]
        padded[i + at[0], at[1]] = ring_of(center, ends[end * EDGE : (end + 1) * EDGE], half).astype(jnp.bfloat16)


def conv_sum(padded, weight_ref, bias_row):
    frames, height, ring, channels = padded.shape[0] - PAST, padded.shape[1], padded.shape[2], padded.shape[3]
    wide = weight_ref.shape[1] // TAPS
    width = wide // TAPS
    windows = [padded[t : t + frames].reshape(frames * height * ring, channels) for t in range(TAPS)]
    product = lax.dot_general(
        jnp.concatenate(windows, axis=1),
        jnp.concatenate([weight_ref[t] for t in range(TAPS)], axis=1),
        (((1,), (1,)), ((), ())),
        preferred_element_type=jnp.float32,
    )
    product = product.reshape(frames, height, ring, TAPS * wide)
    rows = []
    for h in range(height):
        near = [
            product[:, h + r - 1, :, r * wide : (r + 1) * wide] for r in range(TAPS) if 0 <= h + r - 1 < height
        ]
        row = sum(near[1:], near[0])
        before = pltpu.roll(row[:, :, 0:width], 1, 1)
        after = pltpu.roll(row[:, :, 2 * width : 3 * width], ring - 1, 1)
        rows.append(before + row[:, :, width : 2 * width] + after + bias_row)
    return rows


def block_number():
    return lax.axis_index("tm") // 2 * 2 + lax.axis_index("cols")


def pack_first(rows, out_ref, breadth):
    half = lax.axis_index("tm") % 2
    frames, ring, width = rows[0].shape
    rest = out_ref.shape[0] - frames * (breadth + 1)
    packed = []
    for row in rows:
        centers = [row[f, 0:breadth] for f in range(frames)]
        ends = [jnp.where(half == 0, row[f, breadth : breadth + 1], row[f, ring - 1 : ring]) for f in range(frames)]
        if rest:
            ends.append(jnp.zeros((rest, width), jnp.float32))
        packed.append(jnp.concatenate(centers + ends, axis=0))
    out_ref[...] = jnp.concatenate(packed, axis=1).astype(jnp.bfloat16)


def bias_part(bias_ref, row, weight_ref):
    return own_part(bias_ref[...].reshape(1, -1), row, weight_ref.shape[1] // TAPS // TAPS)


def first_late_body(breadth, height, *refs):
    centers, ends = refs[:height], refs[height : 2 * height]
    weight_ref, bias_ref, out_ref, padded = refs[2 * height :]
    row = lax.axis_index("rows")
    picks = [(f, f) for f in range(padded.shape[0])]
    for k in range(height):
        center, end = centers[k][...].astype(jnp.float32), ends[k][...].astype(jnp.float32)
        fill_first(padded, (0, row ^ k), center, end, picks, breadth)
    pack_first(conv_sum(padded, weight_ref, bias_part(bias_ref, row, weight_ref)), out_ref, breadth)


def first_early_body(breadth, height, frames, *refs):
    centers, ends = refs[:height], refs[height : 2 * height]
    past_ref, weight_ref, bias_ref, out_ref, padded = refs[2 * height :]
    row = lax.axis_index("rows")
    for k in range(height):
        past = past_ref[k].astype(jnp.float32)
        past = jnp.where(block_number() > 0, past, jnp.zeros_like(past))
        picks = [(j, frames - PAST + j) for j in range(PAST)]
        fill_first(padded, (0, row ^ k), past[0 : PAST * breadth], past[PAST * breadth :], picks, breadth)
        center, end = centers[k][0 : PAST * breadth].astype(jnp.float32), ends[k][...].astype(jnp.float32)
        fill_first(padded, (PAST, row ^ k), center, end, [(j, j) for j in range(PAST)], breadth)
    pack_first(conv_sum(padded, weight_ref, bias_part(bias_ref, row, weight_ref)), out_ref, breadth)


def regroup(pieces, gain_ref, held, breadth, frames, store):
    row = lax.axis_index("rows")
    half = lax.axis_index("tm") % 2
    height, channels = len(pieces), pieces[0].shape[1]
    width = channels // height
    for k, piece in enumerate(pieces):
        held[row ^ k] = piece[...].astype(jnp.float32)
    gain_values = gain_ref[...].reshape(1, channels)
    for h in range(height):
        joined = [held[s, :, h * width : (h + 1) * width] for s in range(height)]
        values = activate(jnp.concatenate(joined, axis=1), gain_values)
        for f in range(frames):
            end = frames * breadth + f
            ring = ring_of(values[f * breadth : (f + 1) * breadth], values[end : end + 1], half)
            store(h, f, ring.astype(jnp.bfloat16))


def regroup_body(breadth, *refs):
    *pieces, gain_ref, out_ref, last_ref, held = refs
    middle, late = out_ref.shape[1], last_ref.shape[1]

    def store(h, f, ring):
        if f < middle:
            out_ref[h, f] = ring
        else:
            last_ref[h, f - middle] = ring

    regroup(pieces, gain_ref, held, breadth, middle + late, store)


def second_body(breadth, *refs):
    height = (len(refs) - 9) // 2
    pieces, refs = refs[:height], refs[height:]
    middle_ref, last_ref, past_ref, gain_ref, weight_ref, bias_ref = refs[:6]
    outs, (padded, held, branch) = refs[6 : 6 + height], refs[6 + height :]
    row = lax.axis_index("rows")

    def store(h, f, ring):
        padded[PAST + f, h] = ring

    regroup(pieces, gain_ref, held, breadth, PAST, store)
    middle, late = middle_ref.shape[1], last_ref.shape[1]
    for h in range(height):
        past = past_ref[h]
        padded[0:PAST, h] = jnp.where(block_number() > 0, past, jnp.zeros_like(past))
        padded[2 * PAST : 2 * PAST + middle, h] = middle_ref[h]
        padded[2 * PAST + middle : 2 * PAST + middle + late, h] = last_ref[h]
    summed = conv_sum(padded, weight_ref, bias_part(bias_ref, row, weight_ref))
    frames, _, width = summed[0].shape
    for h in range(height):
        branch[h, 0 : frames * breadth] = summed[h][:, 0:breadth].reshape(frames * breadth, width)
    for k, out_ref in enumerate(outs):
        chosen = branch[row ^ k]
        rows = out_ref.shape[0]
        parts = [chosen[i * rows : (i + 1) * rows] for i in range(height)]
        out_ref[...] = jnp.concatenate(parts, axis=1).astype(jnp.bfloat16)


def last_body(latents_ref, *refs):
    *pieces, out_ref, held = refs
    row = lax.axis_index("rows")
    height = len(pieces)
    frames, breadth, channels = latents_ref.shape
    width = channels // height
    for k, piece in enumerate(pieces):
        values = piece[...].astype(jnp.float32)
        parts = [values[:, i * width : (i + 1) * width] for i in range(height)]
        held[row ^ k] = jnp.concatenate(parts, axis=0)
    branch = jnp.concatenate([held[s] for s in range(height)], axis=1)
    branch = branch[0 : frames * breadth].reshape(frames, breadth, channels)
    out_ref[...] = (latents_ref[...].astype(jnp.float32) + branch).astype(jnp.bfloat16)


def shards(shape, latents, gain_one, conv_one, bias_one, gain_two, conv_two, bias_two):
    rows, tm, cols = (shape[name] for name in AXES)
    frames, height, breadth, channels = latents.shape
    width = channels // rows
    ring = breadth + 8
    late, middle = frames - PAST, frames - 2 * PAST
    bf16, f32 = jnp.bfloat16, jnp.float32
    own = latents.reshape(frames, breadth, channels)
    every = [(z, x, c) for z in range(rows) for x in range(tm) for c in range(cols)]
    place = {device: i for i, device in enumerate(every)}

    def moved(values, target):
        return lax.ppermute(values, AXES, [(place[device], place[target(*device)]) for device in every])

    def turned(values, k):
        return moved(values, lambda z, x, c: (z ^ k, x // 2 * 2 + c, x % 2))

    def following(values):
        return moved(values, lambda z, x, c: (z, x, 1) if c == 0 else (z, (x + 2) % tm, 0))

    def spread(values):
        parts = [values]
        for k in range(1, rows):
            parts.append(lax.ppermute(values, "rows", [(z, z ^ k) for z in range(rows)]))
        return parts

    def turn(values):
        parts = []
        for k in range(rows):
            parts.append(turned(values[k], k))
        return parts

    other = lax.ppermute(own, "cols", [(0, 1), (1, 0)])
    weights = [w.reshape(TAPS, TAPS * TAPS * width, channels) for w in (conv_one, conv_two)]
    sds = jax.ShapeDtypeStruct
    size = frames * ring * channels
    work = 2 * ring * channels * rows * 27 * width

    def padded(count):
        return VMEM((count, rows, ring, channels), bf16)

    center, gain_one = call(
        own_body, [sds((frames * breadth, channels), bf16), sds(gain_one.shape, f32)],
        [VMEM((frames, breadth, channels), bf16), pltpu.SemaphoreType.DMA((2,))],
        10 * size, 6 * size, own, gain_one, far=(0, 1),
    )
    centers = turn([center] * rows)
    small = (bias_one, gain_two, bias_two, weights[0])
    end, bias_one, gain_two, bias_two, near = call(
        ends_body, [sds((padded_rows(EDGE * frames), channels), bf16)] + [sds(v.shape, v.dtype) for v in small],
        [pltpu.SemaphoreType.DMA((len(small),))], size, 4 * size, other, gain_one, *small, far=range(2, 2 + len(small)),
    )
    ends = turn([end] * rows)
    past = following(
        jnp.stack([jnp.concatenate([a[late * breadth :], b], axis=0) for a, b in zip(centers, ends)])
    )
    late_rows, early_rows = padded_rows(late * (breadth + 1)), padded_rows(PAST * (breadth + 1))
    part = call(
        functools.partial(first_late_body, breadth, rows), sds((late_rows, channels), bf16),
        [padded(frames)], late * work, 20 * size, *centers, *ends, near, bias_one,
    )
    late_parts = spread(part)
    part = call(
        functools.partial(first_early_body, breadth, rows, frames), sds((early_rows, channels), bf16),
        [padded(2 * PAST)], PAST * work, 20 * size, *centers, *ends, past, near, bias_one,
    )
    early_parts = spread(part)
    second, last = call(
        functools.partial(regroup_body, breadth),
        [sds((rows, middle, ring, channels), bf16), sds((rows, PAST, ring, channels), bf16)],
        [VMEM((rows, late_rows, channels), f32)], 10 * size * rows, 4 * size * rows, *late_parts, gain_two,
    )
    past = following(last)
    back_rows = padded_rows(-(-frames * breadth // rows))
    branch = call(
        functools.partial(second_body, breadth), [sds((back_rows, channels), bf16)] * rows,
        [padded(frames + PAST), VMEM((rows, early_rows, channels), f32), VMEM((rows, back_rows * rows, width), f32)],
        frames * work, 20 * size, *early_parts, second, last, past, gain_two, weights[1], bias_two,
    )
    branch = turn(branch)
    result = call(
        last_body, sds((frames, breadth, channels), bf16), [VMEM((rows, back_rows * rows, width), f32)],
        2 * size, 6 * size, own, *branch,
    )
    return result.reshape(frames, height, breadth, channels)


def solution(mesh):
    shape = dict(mesh.shape)
    return jax.shard_map(
        functools.partial(shards, shape),
        mesh=mesh,
        in_specs=(
            P(("groups", "tm"), "rows", "cols", None),
            P(),
            P(None, "rows", None),
            P(),
            P(),
            P(None, "rows", None),
            P(),
        ),
        out_specs=P(("groups", "tm"), "rows", "cols", None),
        check_vma=False,
    )
```

```python
import functools

import jax
import jax.numpy as jnp
from jax import lax
from jax.experimental import pallas as pl
from jax.experimental.pallas import tpu as pltpu
from jax.sharding import PartitionSpec as P


AXES = ("rows", "tm", "cols")
EDGE = 2
PAST = 2
TAPS = 3
VMEM = pltpu.VMEM


def activate(values, gain_values):
    values = values.astype(jnp.float32)
    mean_square = jnp.mean(values * values, axis=-1, keepdims=True)
    return jax.nn.silu(values * lax.rsqrt(mean_square + 1e-06) * gain_values)


def call(body, out_shape, scratch, flops, moved, *operands, far=()):
    operands = [pltpu.with_memory_space_constraint(v, pltpu.HBM) if i in far else v for i, v in enumerate(operands)]
    spaces = [pltpu.HBM if i in far else VMEM for i in range(len(operands))]
    return pl.pallas_call(
        body,
        out_shape=out_shape,
        in_specs=[pl.BlockSpec(memory_space=space) for space in spaces],
        out_specs=jax.tree.map(lambda _: pl.BlockSpec(memory_space=VMEM), out_shape),
        scratch_shapes=scratch,
        cost_estimate=pl.CostEstimate(flops=flops, bytes_accessed=moved, transcendentals=0),
        compiler_params=pltpu.CompilerParams(vmem_limit_bytes=48 << 20),
    )(*operands)


def ring_of(center, end, half):
    gap = jnp.zeros((8 - end.shape[0], center.shape[1]), center.dtype)
    after = jnp.concatenate([end, gap], axis=0)
    before = jnp.concatenate([gap, end], axis=0)
    return jnp.concatenate([center, jnp.where(half == 0, after, before)], axis=0)


def padded_rows(count):
    return -(-count // 8) * 8


def own_part(vector, row, width):
    parts = vector.shape[1] // width
    return sum(jnp.where(row == s, vector[:, s * width : (s + 1) * width], 0.0) for s in range(parts))


def own_body(own_ref, far_gain_ref, out_ref, gain_ref, held, sems):
    copies = [
        pltpu.make_async_copy(own_ref, held, sems.at[0]),
        pltpu.make_async_copy(far_gain_ref, gain_ref, sems.at[1]),
    ]
    for copy in copies:
        copy.start()
    for copy in copies:
        copy.wait()
    frames, breadth, channels = held.shape
    values = activate(held[...], gain_ref[...].reshape(1, channels))
    out_ref[...] = values.reshape(frames * breadth, channels).astype(jnp.bfloat16)


def ends_body(center_ref, other_ref, gain_ref, out_ref):
    frames, breadth, channels = other_ref.shape
    half = lax.axis_index("cols")
    chosen = jnp.where(half == 0, other_ref[:, 0:8].astype(jnp.float32), other_ref[:, breadth - 8 :].astype(jnp.float32))
    values = activate(chosen, gain_ref[...].reshape(1, channels))
    ends = [jnp.where(half == 0, values[f, 0:EDGE], values[f, 8 - EDGE : 8]) for f in range(frames)]
    count = frames * breadth
    rest = out_ref.shape[0] - count - EDGE * frames
    if rest:
        ends.append(jnp.zeros((rest, channels), jnp.float32))
    out_ref[0:count] = center_ref[...]
    out_ref[count:] = jnp.concatenate(ends, axis=0).astype(jnp.bfloat16)


def stage_body(*refs):
    count = len(refs) // 2
    far, near, sems = refs[:count], refs[count : 2 * count], refs[2 * count]
    copies = [pltpu.make_async_copy(a, b, sems.at[i]) for i, (a, b) in enumerate(zip(far, near))]
    for copy in copies:
        copy.start()
    for copy in copies:
        copy.wait()


def fill_first(padded, at, centers, ends, picks, breadth):
    half = lax.axis_index("tm") % 2
    for i, (frame, end) in enumerate(picks):
        center = centers[frame * breadth : (frame + 1) * breadth]
        padded[i + at[0], at[1]] = ring_of(center, ends[end * EDGE : (end + 1) * EDGE], half).astype(jnp.bfloat16)


def conv_sum(padded, weight_ref, bias_row):
    frames, height, ring, channels = padded.shape[0] - PAST, padded.shape[1], padded.shape[2], padded.shape[3]
    wide = weight_ref.shape[1] // TAPS
    width = wide // TAPS
    windows = [padded[t : t + frames].reshape(frames * height * ring, channels) for t in range(TAPS)]
    product = lax.dot_general(
        jnp.concatenate(windows, axis=1),
        jnp.concatenate([weight_ref[t] for t in range(TAPS)], axis=1),
        (((1,), (1,)), ((), ())),
        preferred_element_type=jnp.float32,
    )
    product = product.reshape(frames, height, ring, TAPS * wide)
    rows = []
    for h in range(height):
        near = [
            product[:, h + r - 1, :, r * wide : (r + 1) * wide] for r in range(TAPS) if 0 <= h + r - 1 < height
        ]
        row = sum(near[1:], near[0])
        before = pltpu.roll(row[:, :, 0:width], 1, 1)
        after = pltpu.roll(row[:, :, 2 * width : 3 * width], ring - 1, 1)
        rows.append(before + row[:, :, width : 2 * width] + after + bias_row)
    return rows


def block_number():
    return lax.axis_index("tm") // 2 * 2 + lax.axis_index("cols")


def pack_first(rows, out_ref, breadth):
    half = lax.axis_index("tm") % 2
    frames, ring, width = rows[0].shape
    rest = out_ref.shape[0] - frames * (breadth + 1)
    packed = []
    for row in rows:
        centers = [row[f, 0:breadth] for f in range(frames)]
        ends = [jnp.where(half == 0, row[f, breadth : breadth + 1], row[f, ring - 1 : ring]) for f in range(frames)]
        if rest:
            ends.append(jnp.zeros((rest, width), jnp.float32))
        packed.append(jnp.concatenate(centers + ends, axis=0))
    out_ref[...] = jnp.concatenate(packed, axis=1).astype(jnp.bfloat16)


def bias_part(bias_ref, row, weight_ref):
    return own_part(bias_ref[...].reshape(1, -1), row, weight_ref.shape[1] // TAPS // TAPS)


def first_late_body(breadth, height, *refs):
    *pieces, weight_ref, bias_ref, out_ref, padded = refs
    row = lax.axis_index("rows")
    frames = padded.shape[0]
    picks = [(f, f) for f in range(frames)]
    for k in range(height):
        values = pieces[k][...].astype(jnp.float32)
        fill_first(padded, (0, row ^ k), values, values[frames * breadth :], picks, breadth)
    pack_first(conv_sum(padded, weight_ref, bias_part(bias_ref, row, weight_ref)), out_ref, breadth)


def first_early_body(breadth, height, frames, *refs):
    *pieces, past_ref, weight_ref, bias_ref, out_ref, padded = refs
    row = lax.axis_index("rows")
    for k in range(height):
        past = past_ref[k].astype(jnp.float32)
        past = jnp.where(block_number() > 0, past, jnp.zeros_like(past))
        picks = [(j, frames - PAST + j) for j in range(PAST)]
        fill_first(padded, (0, row ^ k), past[0 : PAST * breadth], past[PAST * breadth :], picks, breadth)
        center = pieces[k][0 : PAST * breadth].astype(jnp.float32)
        end = pieces[k][frames * breadth :].astype(jnp.float32)
        fill_first(padded, (PAST, row ^ k), center, end, [(j, j) for j in range(PAST)], breadth)
    pack_first(conv_sum(padded, weight_ref, bias_part(bias_ref, row, weight_ref)), out_ref, breadth)


def regroup(pieces, gain_ref, held, breadth, frames, store):
    row = lax.axis_index("rows")
    half = lax.axis_index("tm") % 2
    height, channels = len(pieces), pieces[0].shape[1]
    width = channels // height
    for k, piece in enumerate(pieces):
        held[row ^ k] = piece[...].astype(jnp.float32)
    gain_values = gain_ref[...].reshape(1, channels)
    for h in range(height):
        joined = [held[s, :, h * width : (h + 1) * width] for s in range(height)]
        values = activate(jnp.concatenate(joined, axis=1), gain_values)
        for f in range(frames):
            end = frames * breadth + f
            ring = ring_of(values[f * breadth : (f + 1) * breadth], values[end : end + 1], half)
            store(h, f, ring.astype(jnp.bfloat16))


def regroup_body(breadth, *refs):
    *pieces, gain_ref, out_ref, last_ref, held = refs
    middle, late = out_ref.shape[1], last_ref.shape[1]

    def store(h, f, ring):
        if f < middle:
            out_ref[h, f] = ring
        else:
            last_ref[h, f - middle] = ring

    regroup(pieces, gain_ref, held, breadth, middle + late, store)


def second_body(breadth, *refs):
    height = (len(refs) - 9) // 2
    pieces, refs = refs[:height], refs[height:]
    middle_ref, last_ref, past_ref, gain_ref, weight_ref, bias_ref = refs[:6]
    outs, (padded, held, branch) = refs[6 : 6 + height], refs[6 + height :]
    row = lax.axis_index("rows")

    def store(h, f, ring):
        padded[PAST + f, h] = ring

    regroup(pieces, gain_ref, held, breadth, PAST, store)
    middle, late = middle_ref.shape[1], last_ref.shape[1]
    for h in range(height):
        past = past_ref[h]
        padded[0:PAST, h] = jnp.where(block_number() > 0, past, jnp.zeros_like(past))
        padded[2 * PAST : 2 * PAST + middle, h] = middle_ref[h]
        padded[2 * PAST + middle : 2 * PAST + middle + late, h] = last_ref[h]
    summed = conv_sum(padded, weight_ref, bias_part(bias_ref, row, weight_ref))
    frames, _, width = summed[0].shape
    for h in range(height):
        branch[h, 0 : frames * breadth] = summed[h][:, 0:breadth].reshape(frames * breadth, width)
    for k, out_ref in enumerate(outs):
        chosen = branch[row ^ k]
        rows = out_ref.shape[0]
        parts = [chosen[i * rows : (i + 1) * rows] for i in range(height)]
        out_ref[...] = jnp.concatenate(parts, axis=1).astype(jnp.bfloat16)


def last_body(latents_ref, *refs):
    *pieces, out_ref, held = refs
    row = lax.axis_index("rows")
    height = len(pieces)
    frames, breadth, channels = latents_ref.shape
    width = channels // height
    for k, piece in enumerate(pieces):
        values = piece[...].astype(jnp.float32)
        parts = [values[:, i * width : (i + 1) * width] for i in range(height)]
        held[row ^ k] = jnp.concatenate(parts, axis=0)
    branch = jnp.concatenate([held[s] for s in range(height)], axis=1)
    branch = branch[0 : frames * breadth].reshape(frames, breadth, channels)
    out_ref[...] = (latents_ref[...].astype(jnp.float32) + branch).astype(jnp.bfloat16)


def shards(shape, latents, gain_one, conv_one, bias_one, gain_two, conv_two, bias_two):
    rows, tm, cols = (shape[name] for name in AXES)
    frames, height, breadth, channels = latents.shape
    width = channels // rows
    ring = breadth + 8
    late, middle = frames - PAST, frames - 2 * PAST
    bf16, f32 = jnp.bfloat16, jnp.float32
    own = latents.reshape(frames, breadth, channels)
    every = [(z, x, c) for z in range(rows) for x in range(tm) for c in range(cols)]
    place = {device: i for i, device in enumerate(every)}

    def moved(values, target):
        return lax.ppermute(values, AXES, [(place[device], place[target(*device)]) for device in every])

    def turned(values, k):
        return moved(values, lambda z, x, c: (z ^ k, x // 2 * 2 + c, x % 2))

    def following(values):
        return moved(values, lambda z, x, c: (z, x, 1) if c == 0 else (z, (x + 2) % tm, 0))

    def spread(values):
        parts = [values]
        for k in range(1, rows):
            parts.append(lax.ppermute(values, "rows", [(z, z ^ k) for z in range(rows)]))
        return parts

    def turn(values):
        parts = []
        for k in range(rows):
            parts.append(turned(values[k], k))
        return parts

    other = lax.ppermute(own, "cols", [(0, 1), (1, 0)])
    weights = [w.reshape(TAPS, TAPS * TAPS * width, channels) for w in (conv_one, conv_two)]
    sds = jax.ShapeDtypeStruct
    size = frames * ring * channels
    work = 2 * ring * channels * rows * 27 * width

    def padded(count):
        return VMEM((count, rows, ring, channels), bf16)

    center, gain_one = call(
        own_body, [sds((frames * breadth, channels), bf16), sds(gain_one.shape, f32)],
        [VMEM((frames, breadth, channels), bf16), pltpu.SemaphoreType.DMA((2,))],
        10 * size, 6 * size, own, gain_one, far=(0, 1),
    )
    total = frames * breadth + padded_rows(EDGE * frames)
    band = call(ends_body, sds((total, channels), bf16), [], size, 4 * size, center, other, gain_one)
    pieces = turn([band] * rows)
    small = (bias_one, gain_two, bias_two, weights[0])
    bias_one, gain_two, bias_two, near = call(
        stage_body, [sds(v.shape, v.dtype) for v in small], [pltpu.SemaphoreType.DMA((len(small),))],
        size, 4 * size, *small, far=range(len(small)),
    )
    past = following(jnp.stack([piece[late * breadth :] for piece in pieces]))
    late_rows, early_rows = padded_rows(late * (breadth + 1)), padded_rows(PAST * (breadth + 1))
    part = call(
        functools.partial(first_late_body, breadth, rows), sds((late_rows, channels), bf16),
        [padded(frames)], late * work, 20 * size, *pieces, near, bias_one,
    )
    late_parts = spread(part)
    part = call(
        functools.partial(first_early_body, breadth, rows, frames), sds((early_rows, channels), bf16),
        [padded(2 * PAST)], PAST * work, 20 * size, *pieces, past, near, bias_one,
    )
    early_parts = spread(part)
    second, last = call(
        functools.partial(regroup_body, breadth),
        [sds((rows, middle, ring, channels), bf16), sds((rows, PAST, ring, channels), bf16)],
        [VMEM((rows, late_rows, channels), f32)], 10 * size * rows, 4 * size * rows, *late_parts, gain_two,
    )
    past = following(last)
    back_rows = padded_rows(-(-frames * breadth // rows))
    branch = call(
        functools.partial(second_body, breadth), [sds((back_rows, channels), bf16)] * rows,
        [padded(frames + PAST), VMEM((rows, early_rows, channels), f32), VMEM((rows, back_rows * rows, width), f32)],
        frames * work, 20 * size, *early_parts, second, last, past, gain_two, weights[1], bias_two,
    )
    branch = turn(branch)
    result = call(
        last_body, sds((frames, breadth, channels), bf16), [VMEM((rows, back_rows * rows, width), f32)],
        2 * size, 6 * size, own, *branch,
    )
    return result.reshape(frames, height, breadth, channels)


def solution(mesh):
    shape = dict(mesh.shape)
    return jax.shard_map(
        functools.partial(shards, shape),
        mesh=mesh,
        in_specs=(
            P(("groups", "tm"), "rows", "cols", None),
            P(),
            P(None, "rows", None),
            P(),
            P(),
            P(None, "rows", None),
            P(),
        ),
        out_specs=P(("groups", "tm"), "rows", "cols", None),
        check_vma=False,
    )
```

```python
import functools

import jax
import jax.numpy as jnp
from jax import lax
from jax.experimental import pallas as pl
from jax.experimental.pallas import tpu as pltpu
from jax.sharding import PartitionSpec as P


AXES = ("rows", "tm", "cols")
EDGE = 2
PAST = 2
TAPS = 3
VMEM = pltpu.VMEM


def activate(values, gain_values):
    values = values.astype(jnp.float32)
    mean_square = jnp.mean(values * values, axis=-1, keepdims=True)
    return jax.nn.silu(values * lax.rsqrt(mean_square + 1e-06) * gain_values)


def call(body, out_shape, scratch, flops, moved, *operands, far=()):
    operands = [pltpu.with_memory_space_constraint(v, pltpu.HBM) if i in far else v for i, v in enumerate(operands)]
    spaces = [pltpu.HBM if i in far else VMEM for i in range(len(operands))]
    return pl.pallas_call(
        body,
        out_shape=out_shape,
        in_specs=[pl.BlockSpec(memory_space=space) for space in spaces],
        out_specs=jax.tree.map(lambda _: pl.BlockSpec(memory_space=VMEM), out_shape),
        scratch_shapes=scratch,
        cost_estimate=pl.CostEstimate(flops=flops, bytes_accessed=moved, transcendentals=0),
        compiler_params=pltpu.CompilerParams(vmem_limit_bytes=48 << 20),
    )(*operands)


def ring_of(center, end, half):
    gap = jnp.zeros((8 - end.shape[0], center.shape[1]), center.dtype)
    after = jnp.concatenate([end, gap], axis=0)
    before = jnp.concatenate([gap, end], axis=0)
    return jnp.concatenate([center, jnp.where(half == 0, after, before)], axis=0)


def padded_rows(count):
    return -(-count // 8) * 8


def own_part(vector, row, width):
    parts = vector.shape[1] // width
    return sum(jnp.where(row == s, vector[:, s * width : (s + 1) * width], 0.0) for s in range(parts))


def own_body(own_ref, far_gain_ref, out_ref, gain_ref, held, sems):
    copies = [
        pltpu.make_async_copy(own_ref, held, sems.at[0]),
        pltpu.make_async_copy(far_gain_ref, gain_ref, sems.at[1]),
    ]
    for copy in copies:
        copy.start()
    for copy in copies:
        copy.wait()
    frames, breadth, channels = held.shape
    values = activate(held[...], gain_ref[...].reshape(1, channels))
    out_ref[...] = values.reshape(frames * breadth, channels).astype(jnp.bfloat16)


def ends_body(center_ref, other_ref, gain_ref, out_ref):
    frames, breadth, channels = other_ref.shape
    half = lax.axis_index("cols")
    chosen = jnp.where(half == 0, other_ref[:, 0:8].astype(jnp.float32), other_ref[:, breadth - 8 :].astype(jnp.float32))
    values = activate(chosen, gain_ref[...].reshape(1, channels))
    ends = [jnp.where(half == 0, values[f, 0:EDGE], values[f, 8 - EDGE : 8]) for f in range(frames)]
    count = frames * breadth
    rest = out_ref.shape[0] - count - EDGE * frames
    if rest:
        ends.append(jnp.zeros((rest, channels), jnp.float32))
    out_ref[0:count] = center_ref[...]
    out_ref[count:] = jnp.concatenate(ends, axis=0).astype(jnp.bfloat16)


def stage_body(*refs):
    count = len(refs) // 2
    far, near, sems = refs[:count], refs[count : 2 * count], refs[2 * count]
    copies = [pltpu.make_async_copy(a, b, sems.at[i]) for i, (a, b) in enumerate(zip(far, near))]
    for copy in copies:
        copy.start()
    for copy in copies:
        copy.wait()


def fill_first(padded, at, centers, ends, picks, breadth):
    half = lax.axis_index("tm") % 2
    for i, (frame, end) in enumerate(picks):
        center = centers[frame * breadth : (frame + 1) * breadth]
        padded[i + at[0], at[1]] = ring_of(center, ends[end * EDGE : (end + 1) * EDGE], half).astype(jnp.bfloat16)


def multiply(windows, weight_ref, taps):
    return lax.dot_general(
        jnp.concatenate(windows, axis=1),
        jnp.concatenate([weight_ref[t] for t in taps], axis=1),
        (((1,), (1,)), ((), ())),
        preferred_element_type=jnp.float32,
    )


def row_sums(product):
    height, wide = product.shape[1], product.shape[3] // TAPS
    rows = []
    for h in range(height):
        near = [product[:, h + r - 1, :, r * wide : (r + 1) * wide] for r in range(TAPS) if 0 <= h + r - 1 < height]
        rows.append(sum(near[1:], near[0]))
    return rows


def column_sum(row, bias_row):
    ring, width = row.shape[1], row.shape[2] // TAPS
    before = pltpu.roll(row[:, :, 0:width], 1, 1)
    after = pltpu.roll(row[:, :, 2 * width : 3 * width], ring - 1, 1)
    return before + row[:, :, width : 2 * width] + after + bias_row


def conv_sum(padded, weight_ref, bias_row):
    frames, height, ring, channels = padded.shape[0] - PAST, padded.shape[1], padded.shape[2], padded.shape[3]
    windows = [padded[t : t + frames].reshape(frames * height * ring, channels) for t in range(TAPS)]
    product = multiply(windows, weight_ref, range(TAPS)).reshape(frames, height, ring, -1)
    return [column_sum(row, bias_row) for row in row_sums(product)]


def pair_sums(padded, base, weight_ref, total):
    frames, ring, channels = padded.shape[0] - PAST, padded.shape[2], padded.shape[3]
    windows = [padded[t : t + frames, pl.ds(base, 2)].reshape(frames * 2 * ring, channels) for t in range(TAPS)]
    product = multiply(windows, weight_ref, range(TAPS)).reshape(frames, 2, ring, -1)
    wide = product.shape[3] // TAPS
    taps = [[product[:, i, :, r * wide : (r + 1) * wide] for r in range(TAPS)] for i in range(2)]
    total[base] += taps[0][2]
    total[base + 1] += taps[0][1] + taps[1][2]
    total[base + 2] += taps[0][0] + taps[1][1]
    total[base + 3] += taps[1][0]


def frame_terms(frames, early):
    groups = {}
    for f in range(frames):
        taps = tuple(t for t in range(TAPS) if (PAST <= f + t < 2 * PAST) == early)
        groups.setdefault(taps, []).append(f)
    return [(taps, outs) for taps, outs in groups.items() if taps]


def frame_sums(frame_of, frames, early, weight_ref, height, ring, add):
    for taps, outs in frame_terms(frames, early):
        windows = [jnp.concatenate([frame_of(f + t) for f in outs], axis=0) for t in taps]
        product = multiply(windows, weight_ref, taps).reshape(len(outs), height, ring, -1)
        for h, row in enumerate(row_sums(product)):
            for i, f in enumerate(outs):
                add(f, h, row[i])


def block_number():
    return lax.axis_index("tm") // 2 * 2 + lax.axis_index("cols")


def pack_first(rows, out_ref, breadth):
    half = lax.axis_index("tm") % 2
    frames, ring, width = rows[0].shape
    rest = out_ref.shape[0] - frames * (breadth + 1)
    packed = []
    for row in rows:
        centers = [row[f, 0:breadth] for f in range(frames)]
        ends = [jnp.where(half == 0, row[f, breadth : breadth + 1], row[f, ring - 1 : ring]) for f in range(frames)]
        if rest:
            ends.append(jnp.zeros((rest, width), jnp.float32))
        packed.append(jnp.concatenate(centers + ends, axis=0))
    out_ref[...] = jnp.concatenate(packed, axis=1).astype(jnp.bfloat16)


def bias_part(bias_ref, row, weight_ref):
    return own_part(bias_ref[...].reshape(1, -1), row, weight_ref.shape[1] // TAPS // TAPS)


def fill_pair(padded, pieces, base, row, breadth):
    frames = padded.shape[0]
    for i, piece in enumerate(pieces):
        values = piece[...].astype(jnp.float32)
        picks = [(f, f) for f in range(frames)]
        fill_first(padded, (0, row ^ (base + i)), values, values[frames * breadth :], picks, breadth)


def first_near_body(breadth, *refs):
    *pieces, weight_ref, total, padded = refs
    row = lax.axis_index("rows")
    fill_pair(padded, pieces, 0, row, breadth)
    total[...] = jnp.zeros_like(total)
    pair_sums(padded, row // 2 * 2, weight_ref, total)


def first_late_body(breadth, *refs):
    *pieces, near_ref, weight_ref, bias_ref, out_ref, padded, total = refs
    row = lax.axis_index("rows")
    fill_pair(padded, pieces, 2, row, breadth)
    total[...] = near_ref[...]
    for pair in range(1, len(pieces) // 2 + 1):
        pair_sums(padded, (row // 2 ^ pair) * 2, weight_ref, total)
    bias_row = bias_part(bias_ref, row, weight_ref)
    pack_first([column_sum(total[h + 1], bias_row) for h in range(len(pieces) + 2)], out_ref, breadth)


def first_early_body(breadth, height, frames, *refs):
    *pieces, past_ref, weight_ref, bias_ref, out_ref, padded = refs
    row = lax.axis_index("rows")
    for k in range(height):
        past = past_ref[k].astype(jnp.float32)
        past = jnp.where(block_number() > 0, past, jnp.zeros_like(past))
        picks = [(j, frames - PAST + j) for j in range(PAST)]
        fill_first(padded, (0, row ^ k), past[0 : PAST * breadth], past[PAST * breadth :], picks, breadth)
        center = pieces[k][0 : PAST * breadth].astype(jnp.float32)
        end = pieces[k][frames * breadth :].astype(jnp.float32)
        fill_first(padded, (PAST, row ^ k), center, end, [(j, j) for j in range(PAST)], breadth)
    pack_first(conv_sum(padded, weight_ref, bias_part(bias_ref, row, weight_ref)), out_ref, breadth)


def regroup(pieces, gain_ref, held, breadth, frames, store):
    row = lax.axis_index("rows")
    half = lax.axis_index("tm") % 2
    height, channels = len(pieces), pieces[0].shape[1]
    width = channels // height
    for k, piece in enumerate(pieces):
        held[row ^ k] = piece[...].astype(jnp.float32)
    gain_values = gain_ref[...].reshape(1, channels)
    for h in range(height):
        joined = [held[s, :, h * width : (h + 1) * width] for s in range(height)]
        values = activate(jnp.concatenate(joined, axis=1), gain_values)
        for f in range(frames):
            end = frames * breadth + f
            ring = ring_of(values[f * breadth : (f + 1) * breadth], values[end : end + 1], half)
            store(h, f, ring.astype(jnp.bfloat16))


def regroup_body(breadth, *refs):
    *pieces, gain_ref, out_ref, last_ref, held = refs
    middle, late = out_ref.shape[1], last_ref.shape[1]

    def store(h, f, ring):
        if f < middle:
            out_ref[h, f] = ring
        else:
            last_ref[h, f - middle] = ring

    regroup(pieces, gain_ref, held, breadth, middle + late, store)


def second_part_body(frames, middle_ref, last_ref, past_ref, weight_ref, total):
    height, middle, ring, channels = middle_ref.shape
    done = set()

    def frame_of(p):
        if p < PAST:
            values = past_ref[:, p]
            values = jnp.where(block_number() > 0, values, jnp.zeros_like(values))
        elif p < 2 * PAST + middle:
            values = middle_ref[:, p - 2 * PAST]
        else:
            values = last_ref[:, p - 2 * PAST - middle]
        return values.reshape(height * ring, channels)

    def add(f, h, values):
        done.add(f)
        total[h, f] = values

    frame_sums(frame_of, frames, False, weight_ref, height, ring, add)
    for f in range(frames):
        if f not in done:
            total[:, f] = jnp.zeros((height,) + total.shape[2:], jnp.float32)


def second_body(breadth, *refs):
    height = (len(refs) - 7) // 2
    pieces, refs = refs[:height], refs[height:]
    part_ref, gain_ref, weight_ref, bias_ref = refs[:4]
    outs, (early, held, branch) = refs[4 : 4 + height], refs[4 + height :]
    row = lax.axis_index("rows")

    def store(h, f, ring):
        early[f, h] = ring

    regroup(pieces, gain_ref, held, breadth, PAST, store)
    _, frames, ring, _ = part_ref.shape
    channels = early.shape[3]
    sums = {}

    def add(f, h, values):
        sums[f, h] = part_ref[h, f] + values

    def frame_of(p):
        return early[p - PAST].reshape(height * ring, channels)

    frame_sums(frame_of, frames, True, weight_ref, height, ring, add)
    bias_row = bias_part(bias_ref, row, weight_ref)
    for h in range(height):
        for f in range(frames):
            values = sums[f, h] if (f, h) in sums else part_ref[h, f]
            values = column_sum(values[None], bias_row)[0]
            branch[h, f * breadth : (f + 1) * breadth] = values[0:breadth]
    for k, out_ref in enumerate(outs):
        chosen = branch[row ^ k]
        rows = out_ref.shape[0]
        parts = [chosen[i * rows : (i + 1) * rows] for i in range(height)]
        out_ref[...] = jnp.concatenate(parts, axis=1).astype(jnp.bfloat16)


def last_body(latents_ref, *refs):
    *pieces, out_ref, held = refs
    row = lax.axis_index("rows")
    height = len(pieces)
    frames, breadth, channels = latents_ref.shape
    width = channels // height
    for k, piece in enumerate(pieces):
        values = piece[...].astype(jnp.float32)
        parts = [values[:, i * width : (i + 1) * width] for i in range(height)]
        held[row ^ k] = jnp.concatenate(parts, axis=0)
    branch = jnp.concatenate([held[s] for s in range(height)], axis=1)
    branch = branch[0 : frames * breadth].reshape(frames, breadth, channels)
    out_ref[...] = (latents_ref[...].astype(jnp.float32) + branch).astype(jnp.bfloat16)


def shards(shape, latents, gain_one, conv_one, bias_one, gain_two, conv_two, bias_two):
    rows, tm, cols = (shape[name] for name in AXES)
    frames, height, breadth, channels = latents.shape
    width = channels // rows
    ring = breadth + 8
    late, middle = frames - PAST, frames - 2 * PAST
    bf16, f32 = jnp.bfloat16, jnp.float32
    own = latents.reshape(frames, breadth, channels)
    every = [(z, x, c) for z in range(rows) for x in range(tm) for c in range(cols)]
    place = {device: i for i, device in enumerate(every)}

    def moved(values, target):
        return lax.ppermute(values, AXES, [(place[device], place[target(*device)]) for device in every])

    def turned(values, k):
        return moved(values, lambda z, x, c: (z ^ k, x // 2 * 2 + c, x % 2))

    def following(values):
        return moved(values, lambda z, x, c: (z, x, 1) if c == 0 else (z, (x + 2) % tm, 0))

    def spread(values):
        parts = [values]
        for k in range(1, rows):
            parts.append(lax.ppermute(values, "rows", [(z, z ^ k) for z in range(rows)]))
        return parts

    def turn(values):
        parts = []
        for k in range(rows):
            parts.append(turned(values[k], k))
        return parts

    other = lax.ppermute(own, "cols", [(0, 1), (1, 0)])
    weights = [w.reshape(TAPS, TAPS * TAPS * width, channels) for w in (conv_one, conv_two)]
    sds = jax.ShapeDtypeStruct
    size = frames * ring * channels
    work = 2 * ring * channels * rows * 27 * width

    def padded(count):
        return VMEM((count, rows, ring, channels), bf16)

    center, gain_one = call(
        own_body, [sds((frames * breadth, channels), bf16), sds(gain_one.shape, f32)],
        [VMEM((frames, breadth, channels), bf16), pltpu.SemaphoreType.DMA((2,))],
        10 * size, 6 * size, own, gain_one, far=(0, 1),
    )
    total = frames * breadth + padded_rows(EDGE * frames)
    band = call(ends_body, sds((total, channels), bf16), [], size, 4 * size, center, other, gain_one)
    pieces = turn([band] * rows)
    small = (bias_one, gain_two, bias_two, weights[0])
    bias_one, gain_two, bias_two, near = call(
        stage_body, [sds(v.shape, v.dtype) for v in small], [pltpu.SemaphoreType.DMA((len(small),))],
        size, 4 * size, *small, far=range(len(small)),
    )
    past = following(jnp.stack([piece[late * breadth :] for piece in pieces]))
    late_rows, early_rows = padded_rows(late * (breadth + 1)), padded_rows(PAST * (breadth + 1))
    near_sums = call(
        functools.partial(first_near_body, breadth), sds((rows + 2, late, ring, TAPS * width), f32),
        [padded(frames)], late * work // 2, 10 * size, *pieces[:2], near,
    )
    part = call(
        functools.partial(first_late_body, breadth), sds((late_rows, channels), bf16),
        [padded(frames), VMEM((rows + 2, late, ring, TAPS * width), f32)],
        late * work // 2, 10 * size, *pieces[2:], near_sums, near, bias_one,
    )
    late_parts = spread(part)
    part = call(
        functools.partial(first_early_body, breadth, rows, frames), sds((early_rows, channels), bf16),
        [padded(2 * PAST)], PAST * work, 20 * size, *pieces, past, near, bias_one,
    )
    early_parts = spread(part)
    second, last = call(
        functools.partial(regroup_body, breadth),
        [sds((rows, middle, ring, channels), bf16), sds((rows, PAST, ring, channels), bf16)],
        [VMEM((rows, late_rows, channels), f32)], 10 * size * rows, 4 * size * rows, *late_parts, gain_two,
    )
    past = following(last)
    back_rows = padded_rows(-(-frames * breadth // rows))
    part = call(
        functools.partial(second_part_body, frames), sds((rows, frames, ring, TAPS * width), f32), [],
        frames * work // 2, 20 * size, second, last, past, weights[1],
    )
    branch = call(
        functools.partial(second_body, breadth), [sds((back_rows, channels), bf16)] * rows,
        [padded(PAST), VMEM((rows, early_rows, channels), f32), VMEM((rows, back_rows * rows, width), f32)],
        frames * work // 2, 20 * size, *early_parts, part, gain_two, weights[1], bias_two,
    )
    branch = turn(branch)
    result = call(
        last_body, sds((frames, breadth, channels), bf16), [VMEM((rows, back_rows * rows, width), f32)],
        2 * size, 6 * size, own, *branch,
    )
    return result.reshape(frames, height, breadth, channels)


def solution(mesh):
    shape = dict(mesh.shape)
    return jax.shard_map(
        functools.partial(shards, shape),
        mesh=mesh,
        in_specs=(
            P(("groups", "tm"), "rows", "cols", None),
            P(),
            P(None, "rows", None),
            P(),
            P(),
            P(None, "rows", None),
            P(),
        ),
        out_specs=P(("groups", "tm"), "rows", "cols", None),
        check_vma=False,
    )
```

```python
import functools

import jax
import jax.numpy as jnp
from jax import lax
from jax.experimental import pallas as pl
from jax.experimental.pallas import tpu as pltpu
from jax.sharding import PartitionSpec as P


AXES = ("rows", "tm", "cols")
EDGE = 2
PAST = 2
TAPS = 3
VMEM = pltpu.VMEM


def activate(values, gain_values):
    values = values.astype(jnp.float32)
    mean_square = jnp.mean(values * values, axis=-1, keepdims=True)
    return jax.nn.silu(values * lax.rsqrt(mean_square + 1e-06) * gain_values)


def call(body, out_shape, scratch, flops, moved, *operands, far=(), aliases=None):
    operands = [pltpu.with_memory_space_constraint(v, pltpu.HBM) if i in far else v for i, v in enumerate(operands)]
    spaces = [pltpu.HBM if i in far else VMEM for i in range(len(operands))]
    return pl.pallas_call(
        body,
        out_shape=out_shape,
        in_specs=[pl.BlockSpec(memory_space=space) for space in spaces],
        out_specs=jax.tree.map(lambda _: pl.BlockSpec(memory_space=VMEM), out_shape),
        scratch_shapes=scratch,
        input_output_aliases=aliases or {},
        cost_estimate=pl.CostEstimate(flops=flops, bytes_accessed=moved, transcendentals=0),
        compiler_params=pltpu.CompilerParams(vmem_limit_bytes=48 << 20),
    )(*operands)


def ring_of(center, end, half):
    gap = jnp.zeros((8 - end.shape[0], center.shape[1]), center.dtype)
    after = jnp.concatenate([end, gap], axis=0)
    before = jnp.concatenate([gap, end], axis=0)
    return jnp.concatenate([center, jnp.where(half == 0, after, before)], axis=0)


def padded_rows(count):
    return -(-count // 8) * 8


def own_part(vector, row, width):
    parts = vector.shape[1] // width
    return sum(jnp.where(row == s, vector[:, s * width : (s + 1) * width], 0.0) for s in range(parts))


def own_body(own_ref, far_gain_ref, out_ref, gain_ref, held, sems):
    copies = [
        pltpu.make_async_copy(own_ref, held, sems.at[0]),
        pltpu.make_async_copy(far_gain_ref, gain_ref, sems.at[1]),
    ]
    for copy in copies:
        copy.start()
    for copy in copies:
        copy.wait()
    frames, breadth, channels = held.shape
    values = activate(held[...], gain_ref[...].reshape(1, channels))
    out_ref[...] = values.reshape(frames * breadth, channels).astype(jnp.bfloat16)


def ends_body(center_ref, other_ref, gain_ref, out_ref):
    frames, breadth, channels = other_ref.shape
    half = lax.axis_index("cols")
    chosen = jnp.where(half == 0, other_ref[:, 0:8].astype(jnp.float32), other_ref[:, breadth - 8 :].astype(jnp.float32))
    values = activate(chosen, gain_ref[...].reshape(1, channels))
    ends = [jnp.where(half == 0, values[f, 0:EDGE], values[f, 8 - EDGE : 8]) for f in range(frames)]
    count = frames * breadth
    rest = out_ref.shape[0] - count - EDGE * frames
    if rest:
        ends.append(jnp.zeros((rest, channels), jnp.float32))
    out_ref[0:count] = center_ref[...]
    out_ref[count:] = jnp.concatenate(ends, axis=0).astype(jnp.bfloat16)


def stage_body(*refs):
    count = len(refs) // 2
    far, near, sems = refs[:count], refs[count : 2 * count], refs[2 * count]
    copies = [pltpu.make_async_copy(a, b, sems.at[i]) for i, (a, b) in enumerate(zip(far, near))]
    for copy in copies:
        copy.start()
    for copy in copies:
        copy.wait()


def fill_first(padded, at, centers, ends, picks, breadth):
    half = lax.axis_index("tm") % 2
    for i, (frame, end) in enumerate(picks):
        center = centers[frame * breadth : (frame + 1) * breadth]
        padded[i + at[0], at[1]] = ring_of(center, ends[end * EDGE : (end + 1) * EDGE], half).astype(jnp.bfloat16)


def multiply(windows, weight_ref, taps):
    return lax.dot_general(
        jnp.concatenate(windows, axis=1),
        jnp.concatenate([weight_ref[t] for t in taps], axis=1),
        (((1,), (1,)), ((), ())),
        preferred_element_type=jnp.float32,
    )


def row_sums(product):
    height, wide = product.shape[1], product.shape[3] // TAPS
    rows = []
    for h in range(height):
        near = [product[:, h + r - 1, :, r * wide : (r + 1) * wide] for r in range(TAPS) if 0 <= h + r - 1 < height]
        rows.append(sum(near[1:], near[0]))
    return rows


def column_sum(row, bias_row):
    ring, width = row.shape[1], row.shape[2] // TAPS
    before = pltpu.roll(row[:, :, 0:width], 1, 1)
    after = pltpu.roll(row[:, :, 2 * width : 3 * width], ring - 1, 1)
    return before + row[:, :, width : 2 * width] + after + bias_row


def conv_sum(padded, weight_ref, bias_row):
    frames, height, ring, channels = padded.shape[0] - PAST, padded.shape[1], padded.shape[2], padded.shape[3]
    windows = [padded[t : t + frames].reshape(frames * height * ring, channels) for t in range(TAPS)]
    product = multiply(windows, weight_ref, range(TAPS)).reshape(frames, height, ring, -1)
    return [column_sum(row, bias_row) for row in row_sums(product)]


def add_rows(padded, rows, weight_ref, total):
    frames, height, ring, channels = padded.shape[0] - PAST, padded.shape[1], padded.shape[2], padded.shape[3]
    windows = [padded[t : t + frames].reshape(frames * height * ring, channels) for t in range(TAPS)]
    product = multiply(windows, weight_ref, range(TAPS)).reshape(frames, height, ring, -1)
    wide = product.shape[3] // TAPS
    for i, row in enumerate(rows):
        for r in range(TAPS):
            total[row + 2 - r] += product[:, i, :, r * wide : (r + 1) * wide]


def frame_terms(frames, wanted):
    groups = {}
    for f in range(frames):
        taps = tuple(t for t in range(TAPS) if wanted(f + t))
        groups.setdefault(taps, []).append(f)
    return [(taps, outs) for taps, outs in groups.items() if taps]


def frame_sums(frame_of, frames, wanted, weight_ref, height, ring, add):
    for taps, outs in frame_terms(frames, wanted):
        windows = [jnp.concatenate([frame_of(f + t) for f in outs], axis=0) for t in taps]
        product = multiply(windows, weight_ref, taps).reshape(len(outs), height, ring, -1)
        for h, row in enumerate(row_sums(product)):
            for i, f in enumerate(outs):
                add(f, h, row[i])


def block_number():
    return lax.axis_index("tm") // 2 * 2 + lax.axis_index("cols")


def pack_first(rows, out_ref, breadth):
    half = lax.axis_index("tm") % 2
    frames, ring, width = rows[0].shape
    rest = out_ref.shape[0] - frames * (breadth + 1)
    packed = []
    for row in rows:
        centers = [row[f, 0:breadth] for f in range(frames)]
        ends = [jnp.where(half == 0, row[f, breadth : breadth + 1], row[f, ring - 1 : ring]) for f in range(frames)]
        if rest:
            ends.append(jnp.zeros((rest, width), jnp.float32))
        packed.append(jnp.concatenate(centers + ends, axis=0))
    out_ref[...] = jnp.concatenate(packed, axis=1).astype(jnp.bfloat16)


def bias_part(bias_ref, row, weight_ref):
    return own_part(bias_ref[...].reshape(1, -1), row, weight_ref.shape[1] // TAPS // TAPS)


def fill_slots(padded, pieces, breadth):
    frames = padded.shape[0]
    picks = [(f, f) for f in range(frames)]
    for i, piece in enumerate(pieces):
        values = piece[...].astype(jnp.float32)
        fill_first(padded, (0, i), values, values[frames * breadth :], picks, breadth)


def first_near_body(breadth, ks, *refs):
    *pieces, weight_ref, total, padded = refs
    row = lax.axis_index("rows")
    fill_slots(padded, pieces, breadth)
    total[...] = jnp.zeros_like(total)
    add_rows(padded, [row ^ k for k in ks], weight_ref, total)


def first_late_body(breadth, k, piece_ref, near_ref, weight_ref, bias_ref, out_ref, total, padded):
    row = lax.axis_index("rows")
    fill_slots(padded, [piece_ref], breadth)
    add_rows(padded, [row ^ k], weight_ref, total)
    bias_row = bias_part(bias_ref, row, weight_ref)
    pack_first([column_sum(total[h + 1], bias_row) for h in range(total.shape[0] - 2)], out_ref, breadth)


def first_early_body(breadth, height, frames, *refs):
    *pieces, past_ref, weight_ref, bias_ref, out_ref, padded = refs
    row = lax.axis_index("rows")
    for k in range(height):
        past = past_ref[k].astype(jnp.float32)
        past = jnp.where(block_number() > 0, past, jnp.zeros_like(past))
        picks = [(j, frames - PAST + j) for j in range(PAST)]
        fill_first(padded, (0, row ^ k), past[0 : PAST * breadth], past[PAST * breadth :], picks, breadth)
        center = pieces[k][0 : PAST * breadth].astype(jnp.float32)
        end = pieces[k][frames * breadth :].astype(jnp.float32)
        fill_first(padded, (PAST, row ^ k), center, end, [(j, j) for j in range(PAST)], breadth)
    pack_first(conv_sum(padded, weight_ref, bias_part(bias_ref, row, weight_ref)), out_ref, breadth)


def regroup(pieces, gain_ref, held, breadth, frames, store):
    row = lax.axis_index("rows")
    half = lax.axis_index("tm") % 2
    height, channels = len(pieces), pieces[0].shape[1]
    width = channels // height
    for k, piece in enumerate(pieces):
        held[row ^ k] = piece[...].astype(jnp.float32)
    gain_values = gain_ref[...].reshape(1, channels)
    for h in range(height):
        joined = [held[s, :, h * width : (h + 1) * width] for s in range(height)]
        values = activate(jnp.concatenate(joined, axis=1), gain_values)
        for f in range(frames):
            end = frames * breadth + f
            ring = ring_of(values[f * breadth : (f + 1) * breadth], values[end : end + 1], half)
            store(h, f, ring.astype(jnp.bfloat16))


def regroup_body(breadth, *refs):
    *pieces, gain_ref, out_ref, last_ref, held = refs
    middle, late = out_ref.shape[1], last_ref.shape[1]

    def store(h, f, ring):
        if f < middle:
            out_ref[h, f] = ring
        else:
            last_ref[h, f - middle] = ring

    regroup(pieces, gain_ref, held, breadth, middle + late, store)


def second_late_body(frames, middle_ref, last_ref, weight_ref, total):
    height, middle, ring, channels = middle_ref.shape

    def frame_of(p):
        p -= 2 * PAST
        values = middle_ref[:, p] if p < middle else last_ref[:, p - middle]
        return values.reshape(height * ring, channels)

    def add(f, h, values):
        total[h, f - PAST] = values

    frame_sums(frame_of, frames, lambda p: p >= 2 * PAST, weight_ref, height, ring, add)


def second_past_body(past_ref, weight_ref, total):
    height, _, ring, channels = past_ref.shape

    def frame_of(p):
        values = past_ref[:, p]
        return jnp.where(block_number() > 0, values, jnp.zeros_like(values)).reshape(height * ring, channels)

    def add(f, h, values):
        total[h, f] = values

    frame_sums(frame_of, PAST, lambda p: p < PAST, weight_ref, height, ring, add)


def second_body(breadth, *refs):
    height = (len(refs) - 8) // 2
    pieces, refs = refs[:height], refs[height:]
    late_ref, past_ref, gain_ref, weight_ref, bias_ref = refs[:5]
    outs, (early, held, branch) = refs[5 : 5 + height], refs[5 + height :]
    row = lax.axis_index("rows")

    def store(h, f, ring):
        early[f, h] = ring

    regroup(pieces, gain_ref, held, breadth, PAST, store)
    _, frames, ring, _ = late_ref.shape
    frames += PAST
    channels = early.shape[3]
    sums = {}

    def held_sum(f, h):
        return past_ref[h, f] if f < PAST else late_ref[h, f - PAST]

    def add(f, h, values):
        sums[f, h] = held_sum(f, h) + values

    def frame_of(p):
        return early[p - PAST].reshape(height * ring, channels)

    frame_sums(frame_of, frames, lambda p: PAST <= p < 2 * PAST, weight_ref, height, ring, add)
    bias_row = bias_part(bias_ref, row, weight_ref)
    for h in range(height):
        for f in range(frames):
            values = sums[f, h] if (f, h) in sums else held_sum(f, h)
            values = column_sum(values[None], bias_row)[0]
            branch[h, f * breadth : (f + 1) * breadth] = values[0:breadth]
    for k, out_ref in enumerate(outs):
        chosen = branch[row ^ k]
        rows = out_ref.shape[0]
        parts = [chosen[i * rows : (i + 1) * rows] for i in range(height)]
        out_ref[...] = jnp.concatenate(parts, axis=1).astype(jnp.bfloat16)


def last_body(latents_ref, *refs):
    *pieces, out_ref, held = refs
    row = lax.axis_index("rows")
    height = len(pieces)
    frames, breadth, channels = latents_ref.shape
    width = channels // height
    for k, piece in enumerate(pieces):
        values = piece[...].astype(jnp.float32)
        parts = [values[:, i * width : (i + 1) * width] for i in range(height)]
        held[row ^ k] = jnp.concatenate(parts, axis=0)
    branch = jnp.concatenate([held[s] for s in range(height)], axis=1)
    branch = branch[0 : frames * breadth].reshape(frames, breadth, channels)
    out_ref[...] = (latents_ref[...].astype(jnp.float32) + branch).astype(jnp.bfloat16)


def shards(shape, latents, gain_one, conv_one, bias_one, gain_two, conv_two, bias_two):
    rows, tm, cols = (shape[name] for name in AXES)
    frames, height, breadth, channels = latents.shape
    width = channels // rows
    ring = breadth + 8
    late, middle = frames - PAST, frames - 2 * PAST
    bf16, f32 = jnp.bfloat16, jnp.float32
    own = latents.reshape(frames, breadth, channels)
    every = [(z, x, c) for z in range(rows) for x in range(tm) for c in range(cols)]
    place = {device: i for i, device in enumerate(every)}

    def moved(values, target):
        return lax.ppermute(values, AXES, [(place[device], place[target(*device)]) for device in every])

    def turned(values, k):
        return moved(values, lambda z, x, c: (z ^ k, x // 2 * 2 + c, x % 2))

    def following(values):
        return moved(values, lambda z, x, c: (z, x, 1) if c == 0 else (z, (x + 2) % tm, 0))

    def spread(values):
        parts = [values]
        for k in range(1, rows):
            parts.append(lax.ppermute(values, "rows", [(z, z ^ k) for z in range(rows)]))
        return parts

    def turn(values):
        parts = []
        for k in range(rows):
            parts.append(turned(values[k], k))
        return parts

    other = lax.ppermute(own, "cols", [(0, 1), (1, 0)])
    weights = [w.reshape(TAPS, TAPS * TAPS * width, channels) for w in (conv_one, conv_two)]
    sds = jax.ShapeDtypeStruct
    size = frames * ring * channels
    work = 2 * ring * channels * rows * 27 * width

    def padded(count):
        return VMEM((count, rows, ring, channels), bf16)

    center, gain_one = call(
        own_body, [sds((frames * breadth, channels), bf16), sds(gain_one.shape, f32)],
        [VMEM((frames, breadth, channels), bf16), pltpu.SemaphoreType.DMA((2,))],
        10 * size, 6 * size, own, gain_one, far=(0, 1),
    )
    total = frames * breadth + padded_rows(EDGE * frames)
    band = call(ends_body, sds((total, channels), bf16), [], size, 4 * size, center, other, gain_one)
    pieces = turn([band] * rows)
    small = (bias_one, gain_two, bias_two, weights[0])
    bias_one, gain_two, bias_two, near = call(
        stage_body, [sds(v.shape, v.dtype) for v in small], [pltpu.SemaphoreType.DMA((len(small),))],
        size, 4 * size, *small, far=range(len(small)),
    )
    past = following(jnp.stack([piece[late * breadth :] for piece in pieces]))
    late_rows, early_rows = padded_rows(late * (breadth + 1)), padded_rows(PAST * (breadth + 1))
    *ks, last_k = band_order(rows)
    sums = sds((rows + 2, late, ring, TAPS * width), f32)
    near_sums = call(
        functools.partial(first_near_body, breadth, ks), sums,
        [VMEM((frames, rows - 1, ring, channels), bf16)], late * work * (rows - 1) // rows, 10 * size,
        *[pieces[k] for k in ks], near,
    )
    part, _ = call(
        functools.partial(first_late_body, breadth, last_k), [sds((late_rows, channels), bf16), sums],
        [VMEM((frames, 1, ring, channels), bf16)], late * work // rows, 10 * size,
        pieces[last_k], near_sums, near, bias_one, aliases={1: 1},
    )
    late_parts = spread(part)
    part = call(
        functools.partial(first_early_body, breadth, rows, frames), sds((early_rows, channels), bf16),
        [padded(2 * PAST)], PAST * work, 20 * size, *pieces, past, near, bias_one,
    )
    early_parts = spread(part)
    second, last = call(
        functools.partial(regroup_body, breadth),
        [sds((rows, middle, ring, channels), bf16), sds((rows, PAST, ring, channels), bf16)],
        [VMEM((rows, late_rows, channels), f32)], 10 * size * rows, 4 * size * rows, *late_parts, gain_two,
    )
    past = following(last)
    back_rows = padded_rows(-(-frames * breadth // rows))
    late_sums = call(
        functools.partial(second_late_body, frames), sds((rows, late, ring, TAPS * width), f32), [],
        frames * work // 3, 10 * size, second, last, weights[1],
    )
    past_sums = call(
        second_past_body, sds((rows, PAST, ring, TAPS * width), f32), [],
        frames * work // 5, 10 * size, past, weights[1],
    )
    branch = call(
        functools.partial(second_body, breadth), [sds((back_rows, channels), bf16)] * rows,
        [padded(PAST), VMEM((rows, early_rows, channels), f32), VMEM((rows, back_rows * rows, width), f32)],
        frames * work // 2, 20 * size, *early_parts, late_sums, past_sums, gain_two, weights[1], bias_two,
    )
    branch = turn(branch)
    result = call(
        last_body, sds((frames, breadth, channels), bf16), [VMEM((rows, back_rows * rows, width), f32)],
        2 * size, 6 * size, own, *branch,
    )
    return result.reshape(frames, height, breadth, channels)


def band_order(rows):
    first = [k for k in range(rows - 1, 0, -1) if k != 2]
    return first + [0] + [k for k in (2,) if k < rows]


def solution(mesh):
    shape = dict(mesh.shape)
    return jax.shard_map(
        functools.partial(shards, shape),
        mesh=mesh,
        in_specs=(
            P(("groups", "tm"), "rows", "cols", None),
            P(),
            P(None, "rows", None),
            P(),
            P(),
            P(None, "rows", None),
            P(),
        ),
        out_specs=P(("groups", "tm"), "rows", "cols", None),
        check_vma=False,
    )
```

```python
import functools

import jax
import jax.numpy as jnp
from jax import lax
from jax.experimental import pallas as pl
from jax.experimental.pallas import tpu as pltpu
from jax.sharding import PartitionSpec as P


AXES = ("rows", "tm", "cols")
EDGE = 2
PAST = 2
TAPS = 3
VMEM = pltpu.VMEM


def activate(values, gain_values):
    values = values.astype(jnp.float32)
    mean_square = jnp.mean(values * values, axis=-1, keepdims=True)
    return jax.nn.silu(values * lax.rsqrt(mean_square + 1e-06) * gain_values)


def call(body, out_shape, scratch, flops, moved, *operands, far=(), aliases=None):
    operands = [pltpu.with_memory_space_constraint(v, pltpu.HBM) if i in far else v for i, v in enumerate(operands)]
    spaces = [pltpu.HBM if i in far else VMEM for i in range(len(operands))]
    return pl.pallas_call(
        body,
        out_shape=out_shape,
        in_specs=[pl.BlockSpec(memory_space=space) for space in spaces],
        out_specs=jax.tree.map(lambda _: pl.BlockSpec(memory_space=VMEM), out_shape),
        scratch_shapes=scratch,
        input_output_aliases=aliases or {},
        cost_estimate=pl.CostEstimate(flops=flops, bytes_accessed=moved, transcendentals=0),
        compiler_params=pltpu.CompilerParams(vmem_limit_bytes=48 << 20),
    )(*operands)


def ring_of(center, end, half):
    gap = jnp.zeros((8 - end.shape[0], center.shape[1]), center.dtype)
    after = jnp.concatenate([end, gap], axis=0)
    before = jnp.concatenate([gap, end], axis=0)
    return jnp.concatenate([center, jnp.where(half == 0, after, before)], axis=0)


def padded_rows(count):
    return -(-count // 8) * 8


def own_part(vector, row, width):
    parts = vector.shape[1] // width
    return sum(jnp.where(row == s, vector[:, s * width : (s + 1) * width], 0.0) for s in range(parts))


def own_body(own_ref, far_gain_ref, out_ref, gain_ref, held, sems):
    copies = [
        pltpu.make_async_copy(own_ref, held, sems.at[0]),
        pltpu.make_async_copy(far_gain_ref, gain_ref, sems.at[1]),
    ]
    for copy in copies:
        copy.start()
    for copy in copies:
        copy.wait()
    frames, breadth, channels = held.shape
    values = activate(held[...], gain_ref[...].reshape(1, channels))
    out_ref[...] = values.reshape(frames * breadth, channels).astype(jnp.bfloat16)


def ends_body(center_ref, other_ref, gain_ref, out_ref):
    frames, breadth, channels = other_ref.shape
    half = lax.axis_index("cols")
    chosen = jnp.where(half == 0, other_ref[:, 0:8].astype(jnp.float32), other_ref[:, breadth - 8 :].astype(jnp.float32))
    values = activate(chosen, gain_ref[...].reshape(1, channels))
    ends = [jnp.where(half == 0, values[f, 0:EDGE], values[f, 8 - EDGE : 8]) for f in range(frames)]
    count = frames * breadth
    rest = out_ref.shape[0] - count - EDGE * frames
    if rest:
        ends.append(jnp.zeros((rest, channels), jnp.float32))
    out_ref[0:count] = center_ref[...]
    out_ref[count:] = jnp.concatenate(ends, axis=0).astype(jnp.bfloat16)


def stage_body(*refs):
    count = len(refs) // 2
    far, near, sems = refs[:count], refs[count : 2 * count], refs[2 * count]
    copies = [pltpu.make_async_copy(a, b, sems.at[i]) for i, (a, b) in enumerate(zip(far, near))]
    for copy in copies:
        copy.start()
    for copy in copies:
        copy.wait()


def fill_first(padded, at, centers, ends, picks, breadth):
    half = lax.axis_index("tm") % 2
    for i, (frame, end) in enumerate(picks):
        center = centers[frame * breadth : (frame + 1) * breadth]
        padded[i + at[0], at[1]] = ring_of(center, ends[end * EDGE : (end + 1) * EDGE], half).astype(jnp.bfloat16)


def multiply(windows, weight_ref, taps):
    return lax.dot_general(
        jnp.concatenate(windows, axis=1),
        jnp.concatenate([weight_ref[t] for t in taps], axis=1),
        (((1,), (1,)), ((), ())),
        preferred_element_type=jnp.float32,
    )


def row_sums(product):
    height, wide = product.shape[1], product.shape[3] // TAPS
    rows = []
    for h in range(height):
        near = [product[:, h + r - 1, :, r * wide : (r + 1) * wide] for r in range(TAPS) if 0 <= h + r - 1 < height]
        rows.append(sum(near[1:], near[0]))
    return rows


def column_sum(row, bias_row):
    ring, width = row.shape[1], row.shape[2] // TAPS
    before = pltpu.roll(row[:, :, 0:width], 1, 1)
    after = pltpu.roll(row[:, :, 2 * width : 3 * width], ring - 1, 1)
    return before + row[:, :, width : 2 * width] + after + bias_row


def conv_sum(padded, weight_ref, bias_row):
    frames, height, ring, channels = padded.shape[0] - PAST, padded.shape[1], padded.shape[2], padded.shape[3]
    windows = [padded[t : t + frames].reshape(frames * height * ring, channels) for t in range(TAPS)]
    product = multiply(windows, weight_ref, range(TAPS)).reshape(frames, height, ring, -1)
    return [column_sum(row, bias_row) for row in row_sums(product)]


def add_rows(padded, rows, weight_ref, total):
    frames, height, ring, channels = padded.shape[0] - PAST, padded.shape[1], padded.shape[2], padded.shape[3]
    windows = [padded[t : t + frames].reshape(frames * height * ring, channels) for t in range(TAPS)]
    product = multiply(windows, weight_ref, range(TAPS)).reshape(frames, height, ring, -1)
    wide = product.shape[3] // TAPS
    for i, row in enumerate(rows):
        for r in range(TAPS):
            total[row + 2 - r] += product[:, i, :, r * wide : (r + 1) * wide]


def frame_terms(frames, wanted):
    groups = {}
    for f in range(frames):
        taps = tuple(t for t in range(TAPS) if wanted(f + t))
        groups.setdefault(taps, []).append(f)
    return [(taps, outs) for taps, outs in groups.items() if taps]


def frame_sums(frame_of, frames, wanted, weight_ref, height, ring, add):
    for taps, outs in frame_terms(frames, wanted):
        windows = [jnp.concatenate([frame_of(f + t) for f in outs], axis=0) for t in taps]
        product = multiply(windows, weight_ref, taps).reshape(len(outs), height, ring, -1)
        for h, row in enumerate(row_sums(product)):
            for i, f in enumerate(outs):
                add(f, h, row[i])


def block_number():
    return lax.axis_index("tm") // 2 * 2 + 1 - lax.axis_index("cols")


def pack_first(rows, out_ref, breadth):
    half = lax.axis_index("tm") % 2
    frames, ring, width = rows[0].shape
    rest = out_ref.shape[0] - frames * (breadth + 1)
    packed = []
    for row in rows:
        centers = [row[f, 0:breadth] for f in range(frames)]
        ends = [jnp.where(half == 0, row[f, breadth : breadth + 1], row[f, ring - 1 : ring]) for f in range(frames)]
        if rest:
            ends.append(jnp.zeros((rest, width), jnp.float32))
        packed.append(jnp.concatenate(centers + ends, axis=0))
    out_ref[...] = jnp.concatenate(packed, axis=1).astype(jnp.bfloat16)


def bias_part(bias_ref, row, weight_ref):
    return own_part(bias_ref[...].reshape(1, -1), row, weight_ref.shape[1] // TAPS // TAPS)


def fill_slots(padded, pieces, breadth):
    frames = padded.shape[0]
    picks = [(f, f) for f in range(frames)]
    for i, piece in enumerate(pieces):
        values = piece[...].astype(jnp.float32)
        fill_first(padded, (0, i), values, values[frames * breadth :], picks, breadth)


def first_near_body(breadth, ks, *refs):
    *pieces, weight_ref, total, padded = refs
    row = lax.axis_index("rows")
    fill_slots(padded, pieces, breadth)
    total[...] = jnp.zeros_like(total)
    add_rows(padded, [row ^ k for k in ks], weight_ref, total)


def first_late_body(breadth, k, piece_ref, near_ref, weight_ref, bias_ref, out_ref, total, padded):
    row = lax.axis_index("rows")
    fill_slots(padded, [piece_ref], breadth)
    add_rows(padded, [row ^ k], weight_ref, total)
    bias_row = bias_part(bias_ref, row, weight_ref)
    pack_first([column_sum(total[h + 1], bias_row) for h in range(total.shape[0] - 2)], out_ref, breadth)


def first_early_body(breadth, height, frames, *refs):
    *pieces, past_ref, weight_ref, bias_ref, out_ref, padded = refs
    row = lax.axis_index("rows")
    for k in range(height):
        past = past_ref[k].astype(jnp.float32)
        past = jnp.where(block_number() > 0, past, jnp.zeros_like(past))
        picks = [(j, frames - PAST + j) for j in range(PAST)]
        fill_first(padded, (0, row ^ k), past[0 : PAST * breadth], past[PAST * breadth :], picks, breadth)
        center = pieces[k][0 : PAST * breadth].astype(jnp.float32)
        end = pieces[k][frames * breadth :].astype(jnp.float32)
        fill_first(padded, (PAST, row ^ k), center, end, [(j, j) for j in range(PAST)], breadth)
    pack_first(conv_sum(padded, weight_ref, bias_part(bias_ref, row, weight_ref)), out_ref, breadth)


def regroup(pieces, gain_ref, held, breadth, frames, store):
    row = lax.axis_index("rows")
    half = lax.axis_index("tm") % 2
    height, channels = len(pieces), pieces[0].shape[1]
    width = channels // height
    for k, piece in enumerate(pieces):
        held[row ^ k] = piece[...].astype(jnp.float32)
    gain_values = gain_ref[...].reshape(1, channels)
    for h in range(height):
        joined = [held[s, :, h * width : (h + 1) * width] for s in range(height)]
        values = activate(jnp.concatenate(joined, axis=1), gain_values)
        for f in range(frames):
            end = frames * breadth + f
            ring = ring_of(values[f * breadth : (f + 1) * breadth], values[end : end + 1], half)
            store(h, f, ring.astype(jnp.bfloat16))


def regroup_body(breadth, *refs):
    *pieces, gain_ref, out_ref, last_ref, held = refs
    middle, late = out_ref.shape[1], last_ref.shape[1]

    def store(h, f, ring):
        if f < middle:
            out_ref[h, f] = ring
        else:
            last_ref[h, f - middle] = ring

    regroup(pieces, gain_ref, held, breadth, middle + late, store)


def second_late_body(frames, middle_ref, last_ref, weight_ref, total):
    height, middle, ring, channels = middle_ref.shape

    def frame_of(p):
        p -= 2 * PAST
        values = middle_ref[:, p] if p < middle else last_ref[:, p - middle]
        return values.reshape(height * ring, channels)

    def add(f, h, values):
        total[h, f - PAST] = values

    frame_sums(frame_of, frames, lambda p: p >= 2 * PAST, weight_ref, height, ring, add)


def second_past_body(past_ref, weight_ref, total):
    height, _, ring, channels = past_ref.shape

    def frame_of(p):
        values = past_ref[:, p]
        return jnp.where(block_number() > 0, values, jnp.zeros_like(values)).reshape(height * ring, channels)

    def add(f, h, values):
        total[h, f] = values

    frame_sums(frame_of, PAST, lambda p: p < PAST, weight_ref, height, ring, add)


def second_body(breadth, *refs):
    height = (len(refs) - 8) // 2
    pieces, refs = refs[:height], refs[height:]
    late_ref, past_ref, gain_ref, weight_ref, bias_ref = refs[:5]
    outs, (early, held, branch) = refs[5 : 5 + height], refs[5 + height :]
    row = lax.axis_index("rows")

    def store(h, f, ring):
        early[f, h] = ring

    regroup(pieces, gain_ref, held, breadth, PAST, store)
    _, frames, ring, _ = late_ref.shape
    frames += PAST
    channels = early.shape[3]
    sums = {}

    def held_sum(f, h):
        return past_ref[h, f] if f < PAST else late_ref[h, f - PAST]

    def add(f, h, values):
        sums[f, h] = held_sum(f, h) + values

    def frame_of(p):
        return early[p - PAST].reshape(height * ring, channels)

    frame_sums(frame_of, frames, lambda p: PAST <= p < 2 * PAST, weight_ref, height, ring, add)
    bias_row = bias_part(bias_ref, row, weight_ref)
    for h in range(height):
        for f in range(frames):
            values = sums[f, h] if (f, h) in sums else held_sum(f, h)
            values = column_sum(values[None], bias_row)[0]
            branch[h, f * breadth : (f + 1) * breadth] = values[0:breadth]
    for k, out_ref in enumerate(outs):
        chosen = branch[row ^ k]
        rows = out_ref.shape[0]
        parts = [chosen[i * rows : (i + 1) * rows] for i in range(height)]
        out_ref[...] = jnp.concatenate(parts, axis=1).astype(jnp.bfloat16)


def last_body(latents_ref, *refs):
    *pieces, out_ref, held = refs
    row = lax.axis_index("rows")
    height = len(pieces)
    frames, breadth, channels = latents_ref.shape
    width = channels // height
    for k, piece in enumerate(pieces):
        values = piece[...].astype(jnp.float32)
        parts = [values[:, i * width : (i + 1) * width] for i in range(height)]
        held[row ^ k] = jnp.concatenate(parts, axis=0)
    branch = jnp.concatenate([held[s] for s in range(height)], axis=1)
    branch = branch[0 : frames * breadth].reshape(frames, breadth, channels)
    out_ref[...] = (latents_ref[...].astype(jnp.float32) + branch).astype(jnp.bfloat16)


def shards(shape, latents, gain_one, conv_one, bias_one, gain_two, conv_two, bias_two):
    rows, tm, cols = (shape[name] for name in AXES)
    frames, height, breadth, channels = latents.shape
    width = channels // rows
    ring = breadth + 8
    late, middle = frames - PAST, frames - 2 * PAST
    bf16, f32 = jnp.bfloat16, jnp.float32
    own = latents.reshape(frames, breadth, channels)
    every = [(z, x, c) for z in range(rows) for x in range(tm) for c in range(cols)]
    place = {device: i for i, device in enumerate(every)}

    def moved(values, target):
        return lax.ppermute(values, AXES, [(place[device], place[target(*device)]) for device in every])

    def turned(values, k):
        return moved(values, lambda z, x, c: (z ^ k, x // 2 * 2 + c, 1 - x % 2))

    def returned(values, k):
        return moved(values, lambda z, x, c: (z ^ k, x // 2 * 2 + 1 - c, x % 2))

    def following(values):
        return moved(values, lambda z, x, c: (z, x, 0) if c == 1 else (z, (x + 2) % tm, 1))

    def spread(values):
        parts = [values]
        for k in range(1, rows):
            parts.append(lax.ppermute(values, "rows", [(z, z ^ k) for z in range(rows)]))
        return parts

    def turn(values, way):
        parts = []
        for k in range(rows):
            parts.append(way(values[k], k))
        return parts

    other = lax.ppermute(own, "cols", [(0, 1), (1, 0)])
    weights = [w.reshape(TAPS, TAPS * TAPS * width, channels) for w in (conv_one, conv_two)]
    sds = jax.ShapeDtypeStruct
    size = frames * ring * channels
    work = 2 * ring * channels * rows * 27 * width

    def padded(count):
        return VMEM((count, rows, ring, channels), bf16)

    center, gain_one = call(
        own_body, [sds((frames * breadth, channels), bf16), sds(gain_one.shape, f32)],
        [VMEM((frames, breadth, channels), bf16), pltpu.SemaphoreType.DMA((2,))],
        10 * size, 6 * size, own, gain_one, far=(0, 1),
    )
    total = frames * breadth + padded_rows(EDGE * frames)
    band = call(ends_body, sds((total, channels), bf16), [], size, 4 * size, center, other, gain_one)
    pieces = turn([band] * rows, turned)
    small = (bias_one, gain_two, bias_two, weights[0])
    bias_one, gain_two, bias_two, near = call(
        stage_body, [sds(v.shape, v.dtype) for v in small], [pltpu.SemaphoreType.DMA((len(small),))],
        size, 4 * size, *small, far=range(len(small)),
    )
    past = following(jnp.stack([piece[late * breadth :] for piece in pieces]))
    late_rows, early_rows = padded_rows(late * (breadth + 1)), padded_rows(PAST * (breadth + 1))
    *ks, last_k = band_order(rows)
    sums = sds((rows + 2, late, ring, TAPS * width), f32)
    near_sums = call(
        functools.partial(first_near_body, breadth, ks), sums,
        [VMEM((frames, rows - 1, ring, channels), bf16)], late * work * (rows - 1) // rows, 10 * size,
        *[pieces[k] for k in ks], near,
    )
    part, _ = call(
        functools.partial(first_late_body, breadth, last_k), [sds((late_rows, channels), bf16), sums],
        [VMEM((frames, 1, ring, channels), bf16)], late * work // rows, 10 * size,
        pieces[last_k], near_sums, near, bias_one, aliases={1: 1},
    )
    late_parts = spread(part)
    part = call(
        functools.partial(first_early_body, breadth, rows, frames), sds((early_rows, channels), bf16),
        [padded(2 * PAST)], PAST * work, 20 * size, *pieces, past, near, bias_one,
    )
    early_parts = spread(part)
    second, last = call(
        functools.partial(regroup_body, breadth),
        [sds((rows, middle, ring, channels), bf16), sds((rows, PAST, ring, channels), bf16)],
        [VMEM((rows, late_rows, channels), f32)], 10 * size * rows, 4 * size * rows, *late_parts, gain_two,
    )
    past = following(last)
    back_rows = padded_rows(-(-frames * breadth // rows))
    late_sums = call(
        functools.partial(second_late_body, frames), sds((rows, late, ring, TAPS * width), f32), [],
        frames * work // 3, 10 * size, second, last, weights[1],
    )
    past_sums = call(
        second_past_body, sds((rows, PAST, ring, TAPS * width), f32), [],
        frames * work // 5, 10 * size, past, weights[1],
    )
    branch = call(
        functools.partial(second_body, breadth), [sds((back_rows, channels), bf16)] * rows,
        [padded(PAST), VMEM((rows, early_rows, channels), f32), VMEM((rows, back_rows * rows, width), f32)],
        frames * work // 2, 20 * size, *early_parts, late_sums, past_sums, gain_two, weights[1], bias_two,
    )
    branch = turn(branch, returned)
    result = call(
        last_body, sds((frames, breadth, channels), bf16), [VMEM((rows, back_rows * rows, width), f32)],
        2 * size, 6 * size, own, *branch,
    )
    return result.reshape(frames, height, breadth, channels)


def band_order(rows):
    first = [k for k in range(rows - 1, 0, -1) if k != 2]
    return first + [0] + [k for k in (2,) if k < rows]


def solution(mesh):
    shape = dict(mesh.shape)
    return jax.shard_map(
        functools.partial(shards, shape),
        mesh=mesh,
        in_specs=(
            P(("groups", "tm"), "rows", "cols", None),
            P(),
            P(None, "rows", None),
            P(),
            P(),
            P(None, "rows", None),
            P(),
        ),
        out_specs=P(("groups", "tm"), "rows", "cols", None),
        check_vma=False,
    )
```

```python
import functools

import jax
import jax.numpy as jnp
from jax import lax
from jax.experimental import pallas as pl
from jax.experimental.pallas import tpu as pltpu
from jax.sharding import PartitionSpec as P


AXES = ("rows", "tm", "cols")
EDGE = 2
LANES = 128
PAST = 2
TAPS = 3
VMEM = pltpu.VMEM


def activate(values, gain_values):
    values = values.astype(jnp.float32)
    mean_square = jnp.mean(values * values, axis=-1, keepdims=True)
    return jax.nn.silu(values * lax.rsqrt(mean_square + 1e-06) * gain_values)


def call(body, out_shape, scratch, flops, moved, *operands, far=(), aliases=None):
    operands = [pltpu.with_memory_space_constraint(v, pltpu.HBM) if i in far else v for i, v in enumerate(operands)]
    spaces = [pltpu.HBM if i in far else VMEM for i in range(len(operands))]
    return pl.pallas_call(
        body,
        out_shape=out_shape,
        in_specs=[pl.BlockSpec(memory_space=space) for space in spaces],
        out_specs=jax.tree.map(lambda _: pl.BlockSpec(memory_space=VMEM), out_shape),
        scratch_shapes=scratch,
        input_output_aliases=aliases or {},
        cost_estimate=pl.CostEstimate(flops=flops, bytes_accessed=moved, transcendentals=0),
        compiler_params=pltpu.CompilerParams(vmem_limit_bytes=48 << 20),
    )(*operands)


def ring_of(center, end, half):
    gap = jnp.zeros((8 - end.shape[0], center.shape[1]), center.dtype)
    after = jnp.concatenate([end, gap], axis=0)
    before = jnp.concatenate([gap, end], axis=0)
    return jnp.concatenate([center, jnp.where(half == 0, after, before)], axis=0)


def padded_rows(count):
    return -(-count // 8) * 8


def packed_rows(count, ends, channels):
    blocks = channels // LANES
    return count * blocks + padded_rows(ends * blocks)


def lane_blocks(values):
    return [values[:, i : i + LANES] for i in range(0, values.shape[1], LANES)]


def pack(center, ends, out_ref):
    parts = lane_blocks(center) + lane_blocks(ends)
    rest = out_ref.shape[0] - sum(part.shape[0] for part in parts)
    if rest:
        parts.append(jnp.zeros((rest, LANES), jnp.float32))
    out_ref[...] = jnp.concatenate(parts, axis=0).astype(jnp.bfloat16)


def unpack(values, count, ends, channels):
    blocks = channels // LANES
    center = jnp.concatenate([values[i * count : (i + 1) * count] for i in range(blocks)], axis=1)
    start = blocks * count
    return center, jnp.concatenate([values[start + i * ends : start + (i + 1) * ends] for i in range(blocks)], axis=1)


def own_part(vector, row, width):
    parts = vector.shape[1] // width
    return sum(jnp.where(row == s, vector[:, s * width : (s + 1) * width], 0.0) for s in range(parts))


def own_body(own_ref, far_gain_ref, out_ref, gain_ref, held, sems):
    copies = [
        pltpu.make_async_copy(own_ref, held, sems.at[0]),
        pltpu.make_async_copy(far_gain_ref, gain_ref, sems.at[1]),
    ]
    for copy in copies:
        copy.start()
    for copy in copies:
        copy.wait()
    frames, breadth, channels = held.shape
    values = activate(held[...], gain_ref[...].reshape(1, channels))
    blocks = lane_blocks(values.reshape(frames * breadth, channels))
    out_ref[...] = jnp.concatenate(blocks, axis=0).astype(jnp.bfloat16)


def ends_body(center_ref, other_ref, gain_ref, out_ref):
    frames, breadth, channels = other_ref.shape
    half = lax.axis_index("cols")
    chosen = jnp.where(half == 0, other_ref[:, 0:8].astype(jnp.float32), other_ref[:, breadth - 8 :].astype(jnp.float32))
    values = activate(chosen, gain_ref[...].reshape(1, channels))
    ends = [jnp.where(half == 0, values[f, 0:EDGE], values[f, 8 - EDGE : 8]) for f in range(frames)]
    blocks = lane_blocks(jnp.concatenate(ends, axis=0))
    count = center_ref.shape[0]
    rest = out_ref.shape[0] - count - len(blocks) * EDGE * frames
    if rest:
        blocks.append(jnp.zeros((rest, LANES), jnp.float32))
    out_ref[0:count] = center_ref[...]
    out_ref[count:] = jnp.concatenate(blocks, axis=0).astype(jnp.bfloat16)


def stage_body(*refs):
    count = len(refs) // 2
    far, near, sems = refs[:count], refs[count : 2 * count], refs[2 * count]
    copies = [pltpu.make_async_copy(a, b, sems.at[i]) for i, (a, b) in enumerate(zip(far, near))]
    for copy in copies:
        copy.start()
    for copy in copies:
        copy.wait()


def fill_first(padded, at, centers, ends, picks, breadth):
    half = lax.axis_index("tm") % 2
    for i, (frame, end) in enumerate(picks):
        center = centers[frame * breadth : (frame + 1) * breadth]
        padded[i + at[0], at[1]] = ring_of(center, ends[end * EDGE : (end + 1) * EDGE], half).astype(jnp.bfloat16)


def multiply(windows, weight_ref, taps):
    return lax.dot_general(
        jnp.concatenate(windows, axis=1),
        jnp.concatenate([weight_ref[t] for t in taps], axis=1),
        (((1,), (1,)), ((), ())),
        preferred_element_type=jnp.float32,
    )


def row_sums(product):
    height, wide = product.shape[1], product.shape[3] // TAPS
    rows = []
    for h in range(height):
        near = [product[:, h + r - 1, :, r * wide : (r + 1) * wide] for r in range(TAPS) if 0 <= h + r - 1 < height]
        rows.append(sum(near[1:], near[0]))
    return rows


def column_sum(row):
    ring, width = row.shape[1], row.shape[2] // TAPS
    before = pltpu.roll(row[:, :, 0:width], 1, 1)
    after = pltpu.roll(row[:, :, 2 * width : 3 * width], ring - 1, 1)
    return before + row[:, :, width : 2 * width] + after


def conv_sum(padded, weight_ref, bias_row):
    frames, height, ring, channels = padded.shape[0] - PAST, padded.shape[1], padded.shape[2], padded.shape[3]
    windows = [padded[t : t + frames].reshape(frames * height * ring, channels) for t in range(TAPS)]
    product = multiply(windows, weight_ref, range(TAPS)).reshape(frames, height, ring, -1)
    return [column_sum(row) + bias_row for row in row_sums(product)]


def add_rows(padded, rows, weight_ref, total):
    frames, height, ring, channels = padded.shape[0] - PAST, padded.shape[1], padded.shape[2], padded.shape[3]
    windows = [padded[t : t + frames].reshape(frames * height * ring, channels) for t in range(TAPS)]
    product = multiply(windows, weight_ref, range(TAPS)).reshape(frames, height, ring, -1)
    wide = product.shape[3] // TAPS
    for i, row in enumerate(rows):
        for r in range(TAPS):
            total[row + 2 - r] += column_sum(product[:, i, :, r * wide : (r + 1) * wide])


def frame_terms(frames, wanted):
    groups = {}
    for f in range(frames):
        taps = tuple(t for t in range(TAPS) if wanted(f + t))
        groups.setdefault(taps, []).append(f)
    return [(taps, outs) for taps, outs in groups.items() if taps]


def frame_sums(frame_of, frames, wanted, weight_ref, height, ring, add):
    for taps, outs in frame_terms(frames, wanted):
        windows = [jnp.concatenate([frame_of(f + t) for f in outs], axis=0) for t in taps]
        product = multiply(windows, weight_ref, taps).reshape(len(outs), height, ring, -1)
        for h, row in enumerate(row_sums(product)):
            shifted = column_sum(row)
            for i, f in enumerate(outs):
                add(f, h, shifted[i])


def block_number():
    return lax.axis_index("tm") // 2 * 2 + 1 - lax.axis_index("cols")


def pack_first(rows, out_ref, breadth):
    half = lax.axis_index("tm") % 2
    frames, ring, width = rows[0].shape
    centers = [row[:, 0:breadth].reshape(frames * breadth, width) for row in rows]
    ends = [
        jnp.concatenate(
            [jnp.where(half == 0, row[f, breadth : breadth + 1], row[f, ring - 1 : ring]) for f in range(frames)], axis=0
        )
        for row in rows
    ]
    pack(jnp.concatenate(centers, axis=1), jnp.concatenate(ends, axis=1), out_ref)


def bias_part(bias_ref, row, weight_ref):
    return own_part(bias_ref[...].reshape(1, -1), row, weight_ref.shape[1] // TAPS // TAPS)


def fill_slots(padded, pieces, breadth):
    frames = padded.shape[0]
    picks = [(f, f) for f in range(frames)]
    for i, piece in enumerate(pieces):
        values = piece[...].astype(jnp.float32)
        center, ends = unpack(values, frames * breadth, frames * EDGE, padded.shape[3])
        fill_first(padded, (0, i), center, ends, picks, breadth)


def first_near_body(breadth, ks, *refs):
    *pieces, weight_ref, total, padded = refs
    row = lax.axis_index("rows")
    fill_slots(padded, pieces, breadth)
    total[...] = jnp.zeros_like(total)
    add_rows(padded, [row ^ k for k in ks], weight_ref, total)


def first_late_body(breadth, k, piece_ref, near_ref, weight_ref, bias_ref, out_ref, total, padded):
    row = lax.axis_index("rows")
    fill_slots(padded, [piece_ref], breadth)
    add_rows(padded, [row ^ k], weight_ref, total)
    bias_row = bias_part(bias_ref, row, weight_ref)
    pack_first([total[h + 1] + bias_row for h in range(total.shape[0] - 2)], out_ref, breadth)


def cut_body(count, kept, *refs):
    *pieces, out_ref = refs
    for k, piece in enumerate(pieces):
        blocks = piece.shape[0] // count
        for i in range(blocks):
            out_ref[k, i * kept : (i + 1) * kept] = piece[(i + 1) * count - kept : (i + 1) * count]
        out_ref[k, blocks * kept :] = piece[blocks * count :]


def first_early_body(breadth, height, frames, *refs):
    *pieces, past_ref, weight_ref, bias_ref, out_ref, padded = refs
    row = lax.axis_index("rows")
    for k in range(height):
        past = past_ref[k].astype(jnp.float32)
        past = jnp.where(block_number() > 0, past, jnp.zeros_like(past))
        picks = [(j, frames - PAST + j) for j in range(PAST)]
        center, ends = unpack(past, PAST * breadth, frames * EDGE, padded.shape[3])
        fill_first(padded, (0, row ^ k), center, ends, picks, breadth)
        center, ends = unpack(pieces[k][...].astype(jnp.float32), frames * breadth, frames * EDGE, padded.shape[3])
        fill_first(padded, (PAST, row ^ k), center, ends, [(j, j) for j in range(PAST)], breadth)
    pack_first(conv_sum(padded, weight_ref, bias_part(bias_ref, row, weight_ref)), out_ref, breadth)


def regroup(pieces, gain_ref, held, breadth, frames, store):
    row = lax.axis_index("rows")
    half = lax.axis_index("tm") % 2
    height, channels = len(pieces), held.shape[2]
    width = channels // height
    count = frames * breadth
    for k, piece in enumerate(pieces):
        center, ends = unpack(piece[...].astype(jnp.float32), count, frames, channels)
        held[row ^ k, 0:count] = center
        held[row ^ k, count : count + frames] = ends
    gain_values = gain_ref[...].reshape(1, channels)
    for h in range(height):
        joined = [held[s, :, h * width : (h + 1) * width] for s in range(height)]
        values = activate(jnp.concatenate(joined, axis=1), gain_values)
        for f in range(frames):
            end = frames * breadth + f
            ring = ring_of(values[f * breadth : (f + 1) * breadth], values[end : end + 1], half)
            store(h, f, ring.astype(jnp.bfloat16))


def regroup_body(breadth, *refs):
    *pieces, gain_ref, out_ref, last_ref, held = refs
    middle, late = out_ref.shape[1], last_ref.shape[1]

    def store(h, f, ring):
        if f < middle:
            out_ref[h, f] = ring
        else:
            last_ref[h, f - middle] = ring

    regroup(pieces, gain_ref, held, breadth, middle + late, store)


def second_late_body(frames, middle_ref, last_ref, weight_ref, total):
    height, middle, ring, channels = middle_ref.shape

    def frame_of(p):
        p -= 2 * PAST
        values = middle_ref[:, p] if p < middle else last_ref[:, p - middle]
        return values.reshape(height * ring, channels)

    def add(f, h, values):
        total[h, f - PAST] = values

    frame_sums(frame_of, frames, lambda p: p >= 2 * PAST, weight_ref, height, ring, add)


def second_past_body(past_ref, weight_ref, total):
    height, _, ring, channels = past_ref.shape

    def frame_of(p):
        values = past_ref[:, p]
        return jnp.where(block_number() > 0, values, jnp.zeros_like(values)).reshape(height * ring, channels)

    def add(f, h, values):
        total[h, f] = values

    frame_sums(frame_of, PAST, lambda p: p < PAST, weight_ref, height, ring, add)


def second_body(breadth, *refs):
    height = (len(refs) - 8) // 2
    pieces, refs = refs[:height], refs[height:]
    late_ref, past_ref, gain_ref, weight_ref, bias_ref = refs[:5]
    outs, (early, held, branch) = refs[5 : 5 + height], refs[5 + height :]
    row = lax.axis_index("rows")

    def store(h, f, ring):
        early[f, h] = ring

    regroup(pieces, gain_ref, held, breadth, PAST, store)
    _, frames, ring, _ = late_ref.shape
    frames += PAST
    channels = early.shape[3]
    sums = {}

    def held_sum(f, h):
        return past_ref[h, f] if f < PAST else late_ref[h, f - PAST]

    def add(f, h, values):
        sums[f, h] = held_sum(f, h) + values

    def frame_of(p):
        return early[p - PAST].reshape(height * ring, channels)

    frame_sums(frame_of, frames, lambda p: PAST <= p < 2 * PAST, weight_ref, height, ring, add)
    bias_row = bias_part(bias_ref, row, weight_ref)
    for h in range(height):
        for f in range(frames):
            values = sums[f, h] if (f, h) in sums else held_sum(f, h)
            branch[h, f * breadth : (f + 1) * breadth] = values[0:breadth] + bias_row
    for k, out_ref in enumerate(outs):
        chosen = branch[row ^ k]
        rows = out_ref.shape[0]
        parts = [chosen[i * rows : (i + 1) * rows] for i in range(height)]
        out_ref[...] = jnp.concatenate(parts, axis=1).astype(jnp.bfloat16)


def last_body(latents_ref, *refs):
    *pieces, out_ref, held = refs
    row = lax.axis_index("rows")
    height = len(pieces)
    frames, breadth, channels = latents_ref.shape
    width = channels // height
    for k, piece in enumerate(pieces):
        values = piece[...].astype(jnp.float32)
        parts = [values[:, i * width : (i + 1) * width] for i in range(height)]
        held[row ^ k] = jnp.concatenate(parts, axis=0)
    branch = jnp.concatenate([held[s] for s in range(height)], axis=1)
    branch = branch[0 : frames * breadth].reshape(frames, breadth, channels)
    out_ref[...] = (latents_ref[...].astype(jnp.float32) + branch).astype(jnp.bfloat16)


def shards(shape, latents, gain_one, conv_one, bias_one, gain_two, conv_two, bias_two):
    rows, tm, cols = (shape[name] for name in AXES)
    frames, height, breadth, channels = latents.shape
    width = channels // rows
    ring = breadth + 8
    late, middle = frames - PAST, frames - 2 * PAST
    bf16, f32 = jnp.bfloat16, jnp.float32
    own = latents.reshape(frames, breadth, channels)
    every = [(z, x, c) for z in range(rows) for x in range(tm) for c in range(cols)]
    place = {device: i for i, device in enumerate(every)}

    def moved(values, target):
        return lax.ppermute(values, AXES, [(place[device], place[target(*device)]) for device in every])

    def turned(values, k):
        return moved(values, lambda z, x, c: (z ^ k, x // 2 * 2 + c, 1 - x % 2))

    def returned(values, k):
        return moved(values, lambda z, x, c: (z ^ k, x // 2 * 2 + 1 - c, x % 2))

    def following(values):
        return moved(values, lambda z, x, c: (z, x, 0) if c == 1 else (z, (x + 2) % tm, 1))

    def spread(values):
        parts = [values]
        for k in range(1, rows):
            parts.append(lax.ppermute(values, "rows", [(z, z ^ k) for z in range(rows)]))
        return parts

    def turn(values, way):
        parts = []
        for k in range(rows):
            parts.append(way(values[k], k))
        return parts

    other = lax.ppermute(own, "cols", [(0, 1), (1, 0)])
    weights = [w.reshape(TAPS, TAPS * TAPS * width, channels) for w in (conv_one, conv_two)]
    sds = jax.ShapeDtypeStruct
    size = frames * ring * channels
    work = 2 * ring * channels * rows * 27 * width

    def padded(count):
        return VMEM((count, rows, ring, channels), bf16)

    center, gain_one = call(
        own_body, [sds((frames * breadth * channels // LANES, LANES), bf16), sds(gain_one.shape, f32)],
        [VMEM((frames, breadth, channels), bf16), pltpu.SemaphoreType.DMA((2,))],
        10 * size, 6 * size, own, gain_one, far=(0, 1),
    )
    total = packed_rows(frames * breadth, EDGE * frames, channels)
    band = call(ends_body, sds((total, LANES), bf16), [], size, 4 * size, center, other, gain_one)
    pieces = turn([band] * rows, turned)
    small = (bias_one, gain_two, bias_two, weights[0])
    bias_one, gain_two, bias_two, near = call(
        stage_body, [sds(v.shape, v.dtype) for v in small], [pltpu.SemaphoreType.DMA((len(small),))],
        size, 4 * size, *small, far=range(len(small)),
    )
    past_rows = packed_rows(PAST * breadth, EDGE * frames, channels)
    past = call(
        functools.partial(cut_body, frames * breadth, PAST * breadth), sds((rows, past_rows, LANES), bf16), [],
        size, 4 * size, *pieces,
    )
    past = following(past)
    late_sent, early_sent = (packed_rows(count * breadth, count, channels) for count in (late, PAST))
    late_rows, early_rows = (padded_rows(count * (breadth + 1)) for count in (late, PAST))
    *ks, last_k = band_order(rows)
    sums = sds((rows + 2, late, ring, width), f32)
    near_sums = call(
        functools.partial(first_near_body, breadth, ks), sums,
        [VMEM((frames, rows - 1, ring, channels), bf16)], late * work * (rows - 1) // rows, 10 * size,
        *[pieces[k] for k in ks], near,
    )
    part, _ = call(
        functools.partial(first_late_body, breadth, last_k), [sds((late_sent, LANES), bf16), sums],
        [VMEM((frames, 1, ring, channels), bf16)], late * work // rows, 10 * size,
        pieces[last_k], near_sums, near, bias_one, aliases={1: 1},
    )
    late_parts = spread(part)
    part = call(
        functools.partial(first_early_body, breadth, rows, frames), sds((early_sent, LANES), bf16),
        [padded(2 * PAST)], PAST * work, 20 * size, *pieces, past, near, bias_one,
    )
    early_parts = spread(part)
    second, last = call(
        functools.partial(regroup_body, breadth),
        [sds((rows, middle, ring, channels), bf16), sds((rows, PAST, ring, channels), bf16)],
        [VMEM((rows, late_rows, channels), f32)], 10 * size * rows, 4 * size * rows, *late_parts, gain_two,
    )
    past = following(last)
    back_rows = padded_rows(-(-frames * breadth // rows))
    late_sums = call(
        functools.partial(second_late_body, frames), sds((rows, late, ring, width), f32), [],
        frames * work // 3, 10 * size, second, last, weights[1],
    )
    past_sums = call(
        second_past_body, sds((rows, PAST, ring, width), f32), [],
        frames * work // 5, 10 * size, past, weights[1],
    )
    branch = call(
        functools.partial(second_body, breadth), [sds((back_rows, channels), bf16)] * rows,
        [padded(PAST), VMEM((rows, early_rows, channels), f32), VMEM((rows, back_rows * rows, width), f32)],
        frames * work // 2, 20 * size, *early_parts, late_sums, past_sums, gain_two, weights[1], bias_two,
    )
    branch = turn(branch, returned)
    result = call(
        last_body, sds((frames, breadth, channels), bf16), [VMEM((rows, back_rows * rows, width), f32)],
        2 * size, 6 * size, own, *branch,
    )
    return result.reshape(frames, height, breadth, channels)


def band_order(rows):
    first = [k for k in range(rows - 1, 0, -1) if k != 2]
    return first + [0] + [k for k in (2,) if k < rows]


def solution(mesh):
    shape = dict(mesh.shape)
    return jax.shard_map(
        functools.partial(shards, shape),
        mesh=mesh,
        in_specs=(
            P(("groups", "tm"), "rows", "cols", None),
            P(),
            P(None, "rows", None),
            P(),
            P(),
            P(None, "rows", None),
            P(),
        ),
        out_specs=P(("groups", "tm"), "rows", "cols", None),
        check_vma=False,
    )
```

```python
import functools

import jax
import jax.numpy as jnp
from jax import lax
from jax.experimental import pallas as pl
from jax.experimental.pallas import tpu as pltpu
from jax.sharding import PartitionSpec as P


AXES = ("rows", "tm", "cols")
EDGE = 2
LANES = 128
PAST = 2
TAPS = 3
VMEM = pltpu.VMEM


def activate(values, gain_values):
    values = values.astype(jnp.float32)
    mean_square = jnp.mean(values * values, axis=-1, keepdims=True)
    return jax.nn.silu(values * lax.rsqrt(mean_square + 1e-06) * gain_values)


def call(body, out_shape, scratch, flops, moved, *operands, far=(), aliases=None):
    operands = [pltpu.with_memory_space_constraint(v, pltpu.HBM) if i in far else v for i, v in enumerate(operands)]
    spaces = [pltpu.HBM if i in far else VMEM for i in range(len(operands))]
    return pl.pallas_call(
        body,
        out_shape=out_shape,
        in_specs=[pl.BlockSpec(memory_space=space) for space in spaces],
        out_specs=jax.tree.map(lambda _: pl.BlockSpec(memory_space=VMEM), out_shape),
        scratch_shapes=scratch,
        input_output_aliases=aliases or {},
        cost_estimate=pl.CostEstimate(flops=flops, bytes_accessed=moved, transcendentals=0),
        compiler_params=pltpu.CompilerParams(vmem_limit_bytes=48 << 20),
    )(*operands)


def ring_of(center, end, half):
    gap = jnp.zeros((8 - end.shape[0], center.shape[1]), center.dtype)
    after = jnp.concatenate([end, gap], axis=0)
    before = jnp.concatenate([gap, end], axis=0)
    return jnp.concatenate([center, jnp.where(half == 0, after, before)], axis=0)


def padded_rows(count):
    return -(-count // 8) * 8


def packed_rows(count, ends, channels):
    blocks = channels // LANES
    return count * blocks + padded_rows(ends * blocks)


def lane_blocks(values):
    return [values[:, i : i + LANES] for i in range(0, values.shape[1], LANES)]


def pack(center, ends, out_ref):
    parts = lane_blocks(center) + lane_blocks(ends)
    rest = out_ref.shape[0] - sum(part.shape[0] for part in parts)
    if rest:
        parts.append(jnp.zeros((rest, LANES), jnp.float32))
    out_ref[...] = jnp.concatenate(parts, axis=0).astype(jnp.bfloat16)


def unpack(values, count, ends, channels):
    blocks = channels // LANES
    center = jnp.concatenate([values[i * count : (i + 1) * count] for i in range(blocks)], axis=1)
    start = blocks * count
    return center, jnp.concatenate([values[start + i * ends : start + (i + 1) * ends] for i in range(blocks)], axis=1)


def own_part(vector, row, width):
    parts = vector.shape[1] // width
    return sum(jnp.where(row == s, vector[:, s * width : (s + 1) * width], 0.0) for s in range(parts))


def own_body(own_ref, far_gain_ref, out_ref, gain_ref, held, sems):
    copies = [
        pltpu.make_async_copy(own_ref, held, sems.at[0]),
        pltpu.make_async_copy(far_gain_ref, gain_ref, sems.at[1]),
    ]
    for copy in copies:
        copy.start()
    for copy in copies:
        copy.wait()
    frames, breadth, channels = held.shape
    values = activate(held[...], gain_ref[...].reshape(1, channels))
    blocks = lane_blocks(values.reshape(frames * breadth, channels))
    out_ref[...] = jnp.concatenate(blocks, axis=0).astype(jnp.bfloat16)


def ends_body(center_ref, other_ref, gain_ref, out_ref):
    frames, breadth, channels = other_ref.shape
    half = lax.axis_index("cols")
    chosen = jnp.where(half == 0, other_ref[:, 0:8].astype(jnp.float32), other_ref[:, breadth - 8 :].astype(jnp.float32))
    values = activate(chosen, gain_ref[...].reshape(1, channels))
    ends = [jnp.where(half == 0, values[f, 0:EDGE], values[f, 8 - EDGE : 8]) for f in range(frames)]
    blocks = lane_blocks(jnp.concatenate(ends, axis=0))
    count = center_ref.shape[0]
    rest = out_ref.shape[0] - count - len(blocks) * EDGE * frames
    if rest:
        blocks.append(jnp.zeros((rest, LANES), jnp.float32))
    out_ref[0:count] = center_ref[...]
    out_ref[count:] = jnp.concatenate(blocks, axis=0).astype(jnp.bfloat16)


def stage_body(*refs):
    count = len(refs) // 2
    far, near, sems = refs[:count], refs[count : 2 * count], refs[2 * count]
    copies = [pltpu.make_async_copy(a, b, sems.at[i]) for i, (a, b) in enumerate(zip(far, near))]
    for copy in copies:
        copy.start()
    for copy in copies:
        copy.wait()


def fill_first(padded, at, centers, ends, picks, breadth):
    half = lax.axis_index("tm") % 2
    for i, (frame, end) in enumerate(picks):
        center = centers[frame * breadth : (frame + 1) * breadth]
        padded[i + at[0], at[1]] = ring_of(center, ends[end * EDGE : (end + 1) * EDGE], half).astype(jnp.bfloat16)


def multiply(windows, weight_ref, taps):
    return lax.dot_general(
        jnp.concatenate(windows, axis=1),
        jnp.concatenate([weight_ref[t] for t in taps], axis=1),
        (((1,), (1,)), ((), ())),
        preferred_element_type=jnp.float32,
    )


def row_sums(product):
    height, wide = product.shape[1], product.shape[3] // TAPS
    rows = []
    for h in range(height):
        near = [product[:, h + r - 1, :, r * wide : (r + 1) * wide] for r in range(TAPS) if 0 <= h + r - 1 < height]
        rows.append(sum(near[1:], near[0]))
    return rows


def column_sum(row):
    ring, width = row.shape[1], row.shape[2] // TAPS
    before = pltpu.roll(row[:, :, 0:width], 1, 1)
    after = pltpu.roll(row[:, :, 2 * width : 3 * width], ring - 1, 1)
    return before + row[:, :, width : 2 * width] + after


def conv_sum(padded, weight_ref, bias_row):
    frames, height, ring, channels = padded.shape[0] - PAST, padded.shape[1], padded.shape[2], padded.shape[3]
    windows = [padded[t : t + frames].reshape(frames * height * ring, channels) for t in range(TAPS)]
    product = multiply(windows, weight_ref, range(TAPS)).reshape(frames, height, ring, -1)
    return [column_sum(row) + bias_row for row in row_sums(product)]


def add_rows(padded, rows, weight_ref, total):
    frames, height, ring, channels = padded.shape[0] - PAST, padded.shape[1], padded.shape[2], padded.shape[3]
    windows = [padded[t : t + frames].reshape(frames * height * ring, channels) for t in range(TAPS)]
    product = multiply(windows, weight_ref, range(TAPS)).reshape(frames, height, ring, -1)
    wide = product.shape[3] // TAPS
    for i, row in enumerate(rows):
        for r in range(TAPS):
            total[row + 2 - r] += column_sum(product[:, i, :, r * wide : (r + 1) * wide])


def frame_terms(frames, wanted):
    groups = {}
    for f in range(frames):
        taps = tuple(t for t in range(TAPS) if wanted(f + t))
        groups.setdefault(taps, []).append(f)
    return [(taps, outs) for taps, outs in groups.items() if taps]


def frame_sums(frame_of, frames, wanted, weight_ref, height, ring, add):
    for taps, outs in frame_terms(frames, wanted):
        windows = [jnp.concatenate([frame_of(f + t) for f in outs], axis=0) for t in taps]
        product = multiply(windows, weight_ref, taps).reshape(len(outs), height, ring, -1)
        for h, row in enumerate(row_sums(product)):
            shifted = column_sum(row)
            for i, f in enumerate(outs):
                add(f, h, shifted[i])


def piece_rows(height, sibling=False):
    crossed = (lax.axis_index("tm") % 2 == lax.axis_index("cols")) != sibling
    row = lax.axis_index("rows")
    return [row ^ jnp.where(crossed, a, b) for a, b in zip(band_order(height, True), band_order(height, False))]


def block_number():
    return lax.axis_index("tm") // 2 * 2 + 1 - lax.axis_index("cols")


def pack_first(rows, out_ref, breadth):
    half = lax.axis_index("tm") % 2
    frames, ring, width = rows[0].shape
    centers = [row[:, 0:breadth].reshape(frames * breadth, width) for row in rows]
    ends = [
        jnp.concatenate(
            [jnp.where(half == 0, row[f, breadth : breadth + 1], row[f, ring - 1 : ring]) for f in range(frames)], axis=0
        )
        for row in rows
    ]
    pack(jnp.concatenate(centers, axis=1), jnp.concatenate(ends, axis=1), out_ref)


def bias_part(bias_ref, row, weight_ref):
    return own_part(bias_ref[...].reshape(1, -1), row, weight_ref.shape[1] // TAPS // TAPS)


def fill_slots(padded, pieces, breadth):
    frames = padded.shape[0]
    picks = [(f, f) for f in range(frames)]
    for i, piece in enumerate(pieces):
        values = piece[...].astype(jnp.float32)
        center, ends = unpack(values, frames * breadth, frames * EDGE, padded.shape[3])
        fill_first(padded, (0, i), center, ends, picks, breadth)


def first_near_body(breadth, height, *refs):
    *pieces, weight_ref, total, padded = refs
    fill_slots(padded, pieces, breadth)
    total[...] = jnp.zeros_like(total)
    add_rows(padded, piece_rows(height)[:-1], weight_ref, total)


def first_late_body(breadth, height, piece_ref, near_ref, weight_ref, bias_ref, out_ref, total, padded):
    row = lax.axis_index("rows")
    fill_slots(padded, [piece_ref], breadth)
    add_rows(padded, piece_rows(height)[-1:], weight_ref, total)
    bias_row = bias_part(bias_ref, row, weight_ref)
    pack_first([total[h + 1] + bias_row for h in range(height)], out_ref, breadth)


def cut_body(count, kept, *refs):
    *pieces, out_ref = refs
    for k, piece in enumerate(pieces):
        blocks = piece.shape[0] // count
        for i in range(blocks):
            out_ref[k, i * kept : (i + 1) * kept] = piece[(i + 1) * count - kept : (i + 1) * count]
        out_ref[k, blocks * kept :] = piece[blocks * count :]


def first_early_body(breadth, height, frames, *refs):
    *pieces, past_ref, weight_ref, bias_ref, out_ref, padded = refs
    row = lax.axis_index("rows")
    for k, (own, other) in enumerate(zip(piece_rows(height), piece_rows(height, True))):
        past = past_ref[k].astype(jnp.float32)
        past = jnp.where(block_number() > 0, past, jnp.zeros_like(past))
        picks = [(j, frames - PAST + j) for j in range(PAST)]
        center, ends = unpack(past, PAST * breadth, frames * EDGE, padded.shape[3])
        fill_first(padded, (0, other), center, ends, picks, breadth)
        center, ends = unpack(pieces[k][...].astype(jnp.float32), frames * breadth, frames * EDGE, padded.shape[3])
        fill_first(padded, (PAST, own), center, ends, [(j, j) for j in range(PAST)], breadth)
    pack_first(conv_sum(padded, weight_ref, bias_part(bias_ref, row, weight_ref)), out_ref, breadth)


def regroup(pieces, gain_ref, held, breadth, frames, store):
    row = lax.axis_index("rows")
    half = lax.axis_index("tm") % 2
    height, channels = len(pieces), held.shape[2]
    width = channels // height
    count = frames * breadth
    for k, piece in enumerate(pieces):
        center, ends = unpack(piece[...].astype(jnp.float32), count, frames, channels)
        held[row ^ k, 0:count] = center
        held[row ^ k, count : count + frames] = ends
    gain_values = gain_ref[...].reshape(1, channels)
    for h in range(height):
        joined = [held[s, :, h * width : (h + 1) * width] for s in range(height)]
        values = activate(jnp.concatenate(joined, axis=1), gain_values)
        for f in range(frames):
            end = frames * breadth + f
            ring = ring_of(values[f * breadth : (f + 1) * breadth], values[end : end + 1], half)
            store(h, f, ring.astype(jnp.bfloat16))


def regroup_body(breadth, *refs):
    *pieces, gain_ref, out_ref, last_ref, held = refs
    middle, late = out_ref.shape[1], last_ref.shape[1]

    def store(h, f, ring):
        if f < middle:
            out_ref[h, f] = ring
        else:
            last_ref[h, f - middle] = ring

    regroup(pieces, gain_ref, held, breadth, middle + late, store)


def second_late_body(frames, middle_ref, last_ref, weight_ref, total):
    height, middle, ring, channels = middle_ref.shape

    def frame_of(p):
        p -= 2 * PAST
        values = middle_ref[:, p] if p < middle else last_ref[:, p - middle]
        return values.reshape(height * ring, channels)

    def add(f, h, values):
        total[h, f - PAST] = values

    frame_sums(frame_of, frames, lambda p: p >= 2 * PAST, weight_ref, height, ring, add)


def second_past_body(past_ref, weight_ref, total):
    height, _, ring, channels = past_ref.shape

    def frame_of(p):
        values = past_ref[:, p]
        return jnp.where(block_number() > 0, values, jnp.zeros_like(values)).reshape(height * ring, channels)

    def add(f, h, values):
        total[h, f] = values

    frame_sums(frame_of, PAST, lambda p: p < PAST, weight_ref, height, ring, add)


def second_body(breadth, *refs):
    height = (len(refs) - 8) // 2
    pieces, refs = refs[:height], refs[height:]
    late_ref, past_ref, gain_ref, weight_ref, bias_ref = refs[:5]
    outs, (early, held, branch) = refs[5 : 5 + height], refs[5 + height :]
    row = lax.axis_index("rows")

    def store(h, f, ring):
        early[f, h] = ring

    regroup(pieces, gain_ref, held, breadth, PAST, store)
    _, frames, ring, _ = late_ref.shape
    frames += PAST
    channels = early.shape[3]
    sums = {}

    def held_sum(f, h):
        return past_ref[h, f] if f < PAST else late_ref[h, f - PAST]

    def add(f, h, values):
        sums[f, h] = held_sum(f, h) + values

    def frame_of(p):
        return early[p - PAST].reshape(height * ring, channels)

    frame_sums(frame_of, frames, lambda p: PAST <= p < 2 * PAST, weight_ref, height, ring, add)
    bias_row = bias_part(bias_ref, row, weight_ref)
    for h in range(height):
        for f in range(frames):
            values = sums[f, h] if (f, h) in sums else held_sum(f, h)
            branch[h, f * breadth : (f + 1) * breadth] = values[0:breadth] + bias_row
    for k, out_ref in enumerate(outs):
        chosen = branch[row ^ k]
        rows = out_ref.shape[0]
        parts = [chosen[i * rows : (i + 1) * rows] for i in range(height)]
        out_ref[...] = jnp.concatenate(parts, axis=1).astype(jnp.bfloat16)


def last_body(latents_ref, *refs):
    *pieces, out_ref, held = refs
    row = lax.axis_index("rows")
    height = len(pieces)
    frames, breadth, channels = latents_ref.shape
    width = channels // height
    for k, piece in enumerate(pieces):
        values = piece[...].astype(jnp.float32)
        parts = [values[:, i * width : (i + 1) * width] for i in range(height)]
        held[row ^ k] = jnp.concatenate(parts, axis=0)
    branch = jnp.concatenate([held[s] for s in range(height)], axis=1)
    branch = branch[0 : frames * breadth].reshape(frames, breadth, channels)
    out_ref[...] = (latents_ref[...].astype(jnp.float32) + branch).astype(jnp.bfloat16)


def shards(shape, latents, gain_one, conv_one, bias_one, gain_two, conv_two, bias_two):
    rows, tm, cols = (shape[name] for name in AXES)
    frames, height, breadth, channels = latents.shape
    width = channels // rows
    ring = breadth + 8
    late, middle = frames - PAST, frames - 2 * PAST
    bf16, f32 = jnp.bfloat16, jnp.float32
    own = latents.reshape(frames, breadth, channels)
    every = [(z, x, c) for z in range(rows) for x in range(tm) for c in range(cols)]
    place = {device: i for i, device in enumerate(every)}

    def moved(values, target):
        return lax.ppermute(values, AXES, [(place[device], place[target(*device)]) for device in every])

    def turned(values, k):
        steps = {crosses: band_order(rows, crosses)[k] for crosses in (True, False)}
        return moved(values, lambda z, x, c: (z ^ steps[x % 2 != c], x // 2 * 2 + c, 1 - x % 2))

    def returned(values, k):
        return moved(values, lambda z, x, c: (z ^ k, x // 2 * 2 + 1 - c, x % 2))

    def following(values):
        return moved(values, lambda z, x, c: (z, x, 0) if c == 1 else (z, (x + 2) % tm, 1))

    def spread(values):
        parts = [values]
        for k in range(1, rows):
            parts.append(lax.ppermute(values, "rows", [(z, z ^ k) for z in range(rows)]))
        return parts

    def turn(values, way):
        parts = []
        for k in range(rows):
            parts.append(way(values[k], k))
        return parts

    other = lax.ppermute(own, "cols", [(0, 1), (1, 0)])
    weights = [w.reshape(TAPS, TAPS * TAPS * width, channels) for w in (conv_one, conv_two)]
    sds = jax.ShapeDtypeStruct
    size = frames * ring * channels
    work = 2 * ring * channels * rows * 27 * width

    def padded(count):
        return VMEM((count, rows, ring, channels), bf16)

    center, gain_one = call(
        own_body, [sds((frames * breadth * channels // LANES, LANES), bf16), sds(gain_one.shape, f32)],
        [VMEM((frames, breadth, channels), bf16), pltpu.SemaphoreType.DMA((2,))],
        10 * size, 6 * size, own, gain_one, far=(0, 1),
    )
    total = packed_rows(frames * breadth, EDGE * frames, channels)
    band = call(ends_body, sds((total, LANES), bf16), [], size, 4 * size, center, other, gain_one)
    pieces = turn([band] * rows, turned)
    small = (bias_one, gain_two, bias_two, weights[0])
    bias_one, gain_two, bias_two, near = call(
        stage_body, [sds(v.shape, v.dtype) for v in small], [pltpu.SemaphoreType.DMA((len(small),))],
        size, 4 * size, *small, far=range(len(small)),
    )
    past_rows = packed_rows(PAST * breadth, EDGE * frames, channels)
    past = call(
        functools.partial(cut_body, frames * breadth, PAST * breadth), sds((rows, past_rows, LANES), bf16), [],
        size, 4 * size, *pieces,
    )
    past = following(past)
    late_sent, early_sent = (packed_rows(count * breadth, count, channels) for count in (late, PAST))
    late_rows, early_rows = (padded_rows(count * (breadth + 1)) for count in (late, PAST))
    sums = sds((rows + 2, late, ring, width), f32)
    near_sums = call(
        functools.partial(first_near_body, breadth, rows), sums,
        [VMEM((frames, rows - 1, ring, channels), bf16)], late * work * (rows - 1) // rows, 10 * size,
        *pieces[:-1], near,
    )
    part, _ = call(
        functools.partial(first_late_body, breadth, rows), [sds((late_sent, LANES), bf16), sums],
        [VMEM((frames, 1, ring, channels), bf16)], late * work // rows, 10 * size,
        pieces[-1], near_sums, near, bias_one, aliases={1: 1},
    )
    late_parts = spread(part)
    part = call(
        functools.partial(first_early_body, breadth, rows, frames), sds((early_sent, LANES), bf16),
        [padded(2 * PAST)], PAST * work, 20 * size, *pieces, past, near, bias_one,
    )
    early_parts = spread(part)
    second, last = call(
        functools.partial(regroup_body, breadth),
        [sds((rows, middle, ring, channels), bf16), sds((rows, PAST, ring, channels), bf16)],
        [VMEM((rows, late_rows, channels), f32)], 10 * size * rows, 4 * size * rows, *late_parts, gain_two,
    )
    past = following(last)
    back_rows = padded_rows(-(-frames * breadth // rows))
    late_sums = call(
        functools.partial(second_late_body, frames), sds((rows, late, ring, width), f32), [],
        frames * work // 3, 10 * size, second, last, weights[1],
    )
    past_sums = call(
        second_past_body, sds((rows, PAST, ring, width), f32), [],
        frames * work // 5, 10 * size, past, weights[1],
    )
    branch = call(
        functools.partial(second_body, breadth), [sds((back_rows, channels), bf16)] * rows,
        [padded(PAST), VMEM((rows, early_rows, channels), f32), VMEM((rows, back_rows * rows, width), f32)],
        frames * work // 2, 20 * size, *early_parts, late_sums, past_sums, gain_two, weights[1], bias_two,
    )
    branch = turn(branch, returned)
    result = call(
        last_body, sds((frames, breadth, channels), bf16), [VMEM((rows, back_rows * rows, width), f32)],
        2 * size, 6 * size, own, *branch,
    )
    return result.reshape(frames, height, breadth, channels)


def band_order(rows, crosses):
    first = [k for k in range(rows - 1, 0, -1) if k != 2]
    order = first + [0] + [k for k in (2,) if k < rows]
    return [{1: 2, 2: 1}.get(k, k) if crosses and rows > 2 else k for k in order]


def solution(mesh):
    shape = dict(mesh.shape)
    return jax.shard_map(
        functools.partial(shards, shape),
        mesh=mesh,
        in_specs=(
            P(("groups", "tm"), "rows", "cols", None),
            P(),
            P(None, "rows", None),
            P(),
            P(),
            P(None, "rows", None),
            P(),
        ),
        out_specs=P(("groups", "tm"), "rows", "cols", None),
        check_vma=False,
    )
```

```python
import functools

import jax
import jax.numpy as jnp
from jax import lax
from jax.experimental import pallas as pl
from jax.experimental.pallas import tpu as pltpu
from jax.sharding import PartitionSpec as P


AXES = ("rows", "tm", "cols")
EDGE = 2
LANES = 128
LAST = 2
PAST = 2
TAPS = 3
VMEM = pltpu.VMEM


def activate(values, gain_values):
    values = values.astype(jnp.float32)
    mean_square = jnp.mean(values * values, axis=-1, keepdims=True)
    return jax.nn.silu(values * lax.rsqrt(mean_square + 1e-06) * gain_values)


def call(body, out_shape, scratch, flops, moved, *operands, far=(), aliases=None):
    operands = [pltpu.with_memory_space_constraint(v, pltpu.HBM) if i in far else v for i, v in enumerate(operands)]
    spaces = [pltpu.HBM if i in far else VMEM for i in range(len(operands))]
    return pl.pallas_call(
        body,
        out_shape=out_shape,
        in_specs=[pl.BlockSpec(memory_space=space) for space in spaces],
        out_specs=jax.tree.map(lambda _: pl.BlockSpec(memory_space=VMEM), out_shape),
        scratch_shapes=scratch,
        input_output_aliases=aliases or {},
        cost_estimate=pl.CostEstimate(flops=flops, bytes_accessed=moved, transcendentals=0),
        compiler_params=pltpu.CompilerParams(vmem_limit_bytes=48 << 20),
    )(*operands)


def ring_of(center, end, half):
    gap = jnp.zeros((8 - end.shape[0], center.shape[1]), center.dtype)
    after = jnp.concatenate([end, gap], axis=0)
    before = jnp.concatenate([gap, end], axis=0)
    return jnp.concatenate([center, jnp.where(half == 0, after, before)], axis=0)


def padded_rows(count):
    return -(-count // 8) * 8


def packed_rows(count, ends, channels):
    blocks = channels // LANES
    return count * blocks + padded_rows(ends * blocks)


def lane_blocks(values):
    return [values[:, i : i + LANES] for i in range(0, values.shape[1], LANES)]


def pack(center, ends, out_ref):
    parts = lane_blocks(center) + lane_blocks(ends)
    rest = out_ref.shape[0] - sum(part.shape[0] for part in parts)
    if rest:
        parts.append(jnp.zeros((rest, LANES), jnp.float32))
    out_ref[...] = jnp.concatenate(parts, axis=0).astype(jnp.bfloat16)


def unpack(values, count, ends, channels):
    blocks = channels // LANES
    center = jnp.concatenate([values[i * count : (i + 1) * count] for i in range(blocks)], axis=1)
    start = blocks * count
    return center, jnp.concatenate([values[start + i * ends : start + (i + 1) * ends] for i in range(blocks)], axis=1)


def own_part(vector, row, width):
    parts = vector.shape[1] // width
    return sum(jnp.where(row == s, vector[:, s * width : (s + 1) * width], 0.0) for s in range(parts))


def own_body(own_ref, far_gain_ref, out_ref, gain_ref, held, sems):
    copies = [
        pltpu.make_async_copy(own_ref, held, sems.at[0]),
        pltpu.make_async_copy(far_gain_ref, gain_ref, sems.at[1]),
    ]
    for copy in copies:
        copy.start()
    for copy in copies:
        copy.wait()
    frames, breadth, channels = held.shape
    values = activate(held[...], gain_ref[...].reshape(1, channels))
    blocks = lane_blocks(values.reshape(frames * breadth, channels))
    out_ref[...] = jnp.concatenate(blocks, axis=0).astype(jnp.bfloat16)


def ends_body(center_ref, other_ref, gain_ref, out_ref):
    frames, breadth, channels = other_ref.shape
    half = lax.axis_index("cols")
    chosen = jnp.where(half == 0, other_ref[:, 0:8].astype(jnp.float32), other_ref[:, breadth - 8 :].astype(jnp.float32))
    values = activate(chosen, gain_ref[...].reshape(1, channels))
    ends = [jnp.where(half == 0, values[f, 0:EDGE], values[f, 8 - EDGE : 8]) for f in range(frames)]
    blocks = lane_blocks(jnp.concatenate(ends, axis=0))
    count = center_ref.shape[0]
    rest = out_ref.shape[0] - count - len(blocks) * EDGE * frames
    if rest:
        blocks.append(jnp.zeros((rest, LANES), jnp.float32))
    out_ref[0:count] = center_ref[...]
    out_ref[count:] = jnp.concatenate(blocks, axis=0).astype(jnp.bfloat16)


def stage_body(*refs):
    count = len(refs) // 2
    far, near, sems = refs[:count], refs[count : 2 * count], refs[2 * count]
    copies = [pltpu.make_async_copy(a, b, sems.at[i]) for i, (a, b) in enumerate(zip(far, near))]
    for copy in copies:
        copy.start()
    for copy in copies:
        copy.wait()


def fill_first(padded, at, centers, ends, picks, breadth):
    half = lax.axis_index("tm") % 2
    for i, (frame, end) in enumerate(picks):
        center = centers[frame * breadth : (frame + 1) * breadth]
        padded[i + at[0], at[1]] = ring_of(center, ends[end * EDGE : (end + 1) * EDGE], half).astype(jnp.bfloat16)


def multiply(windows, weight_ref, taps):
    return lax.dot_general(
        jnp.concatenate(windows, axis=1),
        jnp.concatenate([weight_ref[t] for t in taps], axis=1),
        (((1,), (1,)), ((), ())),
        preferred_element_type=jnp.float32,
    )


def row_sums(product):
    height, wide = product.shape[1], product.shape[3] // TAPS
    rows = []
    for h in range(height):
        near = [product[:, h + r - 1, :, r * wide : (r + 1) * wide] for r in range(TAPS) if 0 <= h + r - 1 < height]
        rows.append(sum(near[1:], near[0]))
    return rows


def column_sum(row):
    ring, width = row.shape[1], row.shape[2] // TAPS
    before = pltpu.roll(row[:, :, 0:width], 1, 1)
    after = pltpu.roll(row[:, :, 2 * width : 3 * width], ring - 1, 1)
    return before + row[:, :, width : 2 * width] + after


def conv_sum(padded, weight_ref, bias_row):
    frames, height, ring, channels = padded.shape[0] - PAST, padded.shape[1], padded.shape[2], padded.shape[3]
    windows = [padded[t : t + frames].reshape(frames * height * ring, channels) for t in range(TAPS)]
    product = multiply(windows, weight_ref, range(TAPS)).reshape(frames, height, ring, -1)
    return [column_sum(row) + bias_row for row in row_sums(product)]


def add_rows(padded, rows, weight_ref, total):
    frames, height, ring, channels = padded.shape[0] - PAST, padded.shape[1], padded.shape[2], padded.shape[3]
    windows = [padded[t : t + frames].reshape(frames * height * ring, channels) for t in range(TAPS)]
    product = multiply(windows, weight_ref, range(TAPS)).reshape(frames, height, ring, -1)
    wide = product.shape[3] // TAPS
    for i, row in enumerate(rows):
        for r in range(TAPS):
            total[row + 2 - r] += column_sum(product[:, i, :, r * wide : (r + 1) * wide])


def frame_terms(frames, wanted):
    groups = {}
    for f in range(frames):
        taps = tuple(t for t in range(TAPS) if wanted(f + t))
        groups.setdefault(taps, []).append(f)
    return [(taps, outs) for taps, outs in groups.items() if taps]


def frame_sums(frame_of, frames, wanted, weight_ref, height, ring, add):
    for taps, outs in frame_terms(frames, wanted):
        windows = [jnp.concatenate([frame_of(f + t) for f in outs], axis=0) for t in taps]
        product = multiply(windows, weight_ref, taps).reshape(len(outs), height, ring, -1)
        for h, row in enumerate(row_sums(product)):
            shifted = column_sum(row)
            for i, f in enumerate(outs):
                add(f, h, shifted[i])


def piece_rows(height, sibling=False):
    crossed = (lax.axis_index("tm") % 2 == lax.axis_index("cols")) != sibling
    row = lax.axis_index("rows")
    return [row ^ jnp.where(crossed, a, b) for a, b in zip(band_order(height, True), band_order(height, False))]


def block_number():
    return lax.axis_index("tm") // 2 * 2 + 1 - lax.axis_index("cols")


def pack_first(rows, out_ref, breadth):
    half = lax.axis_index("tm") % 2
    frames, ring, width = rows[0].shape
    centers = [row[:, 0:breadth].reshape(frames * breadth, width) for row in rows]
    ends = [
        jnp.concatenate(
            [jnp.where(half == 0, row[f, breadth : breadth + 1], row[f, ring - 1 : ring]) for f in range(frames)], axis=0
        )
        for row in rows
    ]
    pack(jnp.concatenate(centers, axis=1), jnp.concatenate(ends, axis=1), out_ref)


def bias_part(bias_ref, row, weight_ref):
    return own_part(bias_ref[...].reshape(1, -1), row, weight_ref.shape[1] // TAPS // TAPS)


def fill_slots(padded, pieces, breadth):
    frames = padded.shape[0]
    picks = [(f, f) for f in range(frames)]
    for i, piece in enumerate(pieces):
        values = piece[...].astype(jnp.float32)
        center, ends = unpack(values, frames * breadth, frames * EDGE, padded.shape[3])
        fill_first(padded, (0, i), center, ends, picks, breadth)


def first_near_body(breadth, height, *refs):
    *pieces, weight_ref, total, padded = refs
    fill_slots(padded, pieces, breadth)
    total[...] = jnp.zeros_like(total)
    add_rows(padded, piece_rows(height)[:-LAST], weight_ref, total)


def first_late_body(breadth, height, *refs):
    *pieces, near_ref, weight_ref, bias_ref, out_ref, total, padded = refs
    row = lax.axis_index("rows")
    fill_slots(padded, pieces, breadth)
    add_rows(padded, piece_rows(height)[-LAST:], weight_ref, total)
    bias_row = bias_part(bias_ref, row, weight_ref)
    pack_first([total[h + 1] + bias_row for h in range(height)], out_ref, breadth)


def cut_body(count, kept, *refs):
    *pieces, out_ref = refs
    for k, piece in enumerate(pieces):
        blocks = piece.shape[0] // count
        for i in range(blocks):
            out_ref[k, i * kept : (i + 1) * kept] = piece[(i + 1) * count - kept : (i + 1) * count]
        out_ref[k, blocks * kept :] = piece[blocks * count :]


def first_early_body(breadth, height, frames, *refs):
    *pieces, past_ref, weight_ref, bias_ref, out_ref, padded = refs
    row = lax.axis_index("rows")
    for k, (own, other) in enumerate(zip(piece_rows(height), piece_rows(height, True))):
        past = past_ref[k].astype(jnp.float32)
        past = jnp.where(block_number() > 0, past, jnp.zeros_like(past))
        picks = [(j, frames - PAST + j) for j in range(PAST)]
        center, ends = unpack(past, PAST * breadth, frames * EDGE, padded.shape[3])
        fill_first(padded, (0, other), center, ends, picks, breadth)
        center, ends = unpack(pieces[k][...].astype(jnp.float32), frames * breadth, frames * EDGE, padded.shape[3])
        fill_first(padded, (PAST, own), center, ends, [(j, j) for j in range(PAST)], breadth)
    pack_first(conv_sum(padded, weight_ref, bias_part(bias_ref, row, weight_ref)), out_ref, breadth)


def regroup(pieces, gain_ref, held, breadth, frames, store):
    row = lax.axis_index("rows")
    half = lax.axis_index("tm") % 2
    height, channels = len(pieces), held.shape[2]
    width = channels // height
    count = frames * breadth
    for k, piece in enumerate(pieces):
        center, ends = unpack(piece[...].astype(jnp.float32), count, frames, channels)
        held[row ^ k, 0:count] = center
        held[row ^ k, count : count + frames] = ends
    gain_values = gain_ref[...].reshape(1, channels)
    for h in range(height):
        joined = [held[s, :, h * width : (h + 1) * width] for s in range(height)]
        values = activate(jnp.concatenate(joined, axis=1), gain_values)
        for f in range(frames):
            end = frames * breadth + f
            ring = ring_of(values[f * breadth : (f + 1) * breadth], values[end : end + 1], half)
            store(h, f, ring.astype(jnp.bfloat16))


def regroup_body(breadth, *refs):
    *pieces, gain_ref, out_ref, last_ref, held = refs
    middle, late = out_ref.shape[1], last_ref.shape[1]

    def store(h, f, ring):
        if f < middle:
            out_ref[h, f] = ring
        else:
            last_ref[h, f - middle] = ring

    regroup(pieces, gain_ref, held, breadth, middle + late, store)


def second_late_body(frames, middle_ref, last_ref, weight_ref, total):
    height, middle, ring, channels = middle_ref.shape

    def frame_of(p):
        p -= 2 * PAST
        values = middle_ref[:, p] if p < middle else last_ref[:, p - middle]
        return values.reshape(height * ring, channels)

    def add(f, h, values):
        total[h, f - PAST] = values

    frame_sums(frame_of, frames, lambda p: p >= 2 * PAST, weight_ref, height, ring, add)


def second_past_body(past_ref, weight_ref, total):
    height, _, ring, channels = past_ref.shape

    def frame_of(p):
        values = past_ref[:, p]
        return jnp.where(block_number() > 0, values, jnp.zeros_like(values)).reshape(height * ring, channels)

    def add(f, h, values):
        total[h, f] = values

    frame_sums(frame_of, PAST, lambda p: p < PAST, weight_ref, height, ring, add)


def second_body(breadth, *refs):
    height = (len(refs) - 8) // 2
    pieces, refs = refs[:height], refs[height:]
    late_ref, past_ref, gain_ref, weight_ref, bias_ref = refs[:5]
    outs, (early, held, branch) = refs[5 : 5 + height], refs[5 + height :]
    row = lax.axis_index("rows")

    def store(h, f, ring):
        early[f, h] = ring

    regroup(pieces, gain_ref, held, breadth, PAST, store)
    _, frames, ring, _ = late_ref.shape
    frames += PAST
    channels = early.shape[3]
    sums = {}

    def held_sum(f, h):
        return past_ref[h, f] if f < PAST else late_ref[h, f - PAST]

    def add(f, h, values):
        sums[f, h] = held_sum(f, h) + values

    def frame_of(p):
        return early[p - PAST].reshape(height * ring, channels)

    frame_sums(frame_of, frames, lambda p: PAST <= p < 2 * PAST, weight_ref, height, ring, add)
    bias_row = bias_part(bias_ref, row, weight_ref)
    for h in range(height):
        for f in range(frames):
            values = sums[f, h] if (f, h) in sums else held_sum(f, h)
            branch[h, f * breadth : (f + 1) * breadth] = values[0:breadth] + bias_row
    for k, out_ref in enumerate(outs):
        chosen = branch[row ^ k]
        rows = out_ref.shape[0]
        parts = [chosen[i * rows : (i + 1) * rows] for i in range(height)]
        out_ref[...] = jnp.concatenate(parts, axis=1).astype(jnp.bfloat16)


def last_body(latents_ref, *refs):
    *pieces, out_ref, held = refs
    row = lax.axis_index("rows")
    height = len(pieces)
    frames, breadth, channels = latents_ref.shape
    width = channels // height
    for k, piece in enumerate(pieces):
        values = piece[...].astype(jnp.float32)
        parts = [values[:, i * width : (i + 1) * width] for i in range(height)]
        held[row ^ k] = jnp.concatenate(parts, axis=0)
    branch = jnp.concatenate([held[s] for s in range(height)], axis=1)
    branch = branch[0 : frames * breadth].reshape(frames, breadth, channels)
    out_ref[...] = (latents_ref[...].astype(jnp.float32) + branch).astype(jnp.bfloat16)


def shards(shape, latents, gain_one, conv_one, bias_one, gain_two, conv_two, bias_two):
    rows, tm, cols = (shape[name] for name in AXES)
    frames, height, breadth, channels = latents.shape
    width = channels // rows
    ring = breadth + 8
    late, middle = frames - PAST, frames - 2 * PAST
    bf16, f32 = jnp.bfloat16, jnp.float32
    own = latents.reshape(frames, breadth, channels)
    every = [(z, x, c) for z in range(rows) for x in range(tm) for c in range(cols)]
    place = {device: i for i, device in enumerate(every)}

    def moved(values, target):
        return lax.ppermute(values, AXES, [(place[device], place[target(*device)]) for device in every])

    def turned(values, k):
        steps = {crosses: band_order(rows, crosses)[k] for crosses in (True, False)}
        return moved(values, lambda z, x, c: (z ^ steps[x % 2 != c], x // 2 * 2 + c, 1 - x % 2))

    def returned(values, k):
        return moved(values, lambda z, x, c: (z ^ k, x // 2 * 2 + 1 - c, x % 2))

    def following(values):
        return moved(values, lambda z, x, c: (z, x, 0) if c == 1 else (z, (x + 2) % tm, 1))

    def spread(values):
        parts = [values]
        for k in range(1, rows):
            parts.append(lax.ppermute(values, "rows", [(z, z ^ k) for z in range(rows)]))
        return parts

    def turn(values, way):
        parts = []
        for k in range(rows):
            parts.append(way(values[k], k))
        return parts

    other = lax.ppermute(own, "cols", [(0, 1), (1, 0)])
    weights = [w.reshape(TAPS, TAPS * TAPS * width, channels) for w in (conv_one, conv_two)]
    sds = jax.ShapeDtypeStruct
    size = frames * ring * channels
    work = 2 * ring * channels * rows * 27 * width

    def padded(count):
        return VMEM((count, rows, ring, channels), bf16)

    center, gain_one = call(
        own_body, [sds((frames * breadth * channels // LANES, LANES), bf16), sds(gain_one.shape, f32)],
        [VMEM((frames, breadth, channels), bf16), pltpu.SemaphoreType.DMA((2,))],
        10 * size, 6 * size, own, gain_one, far=(0, 1),
    )
    total = packed_rows(frames * breadth, EDGE * frames, channels)
    band = call(ends_body, sds((total, LANES), bf16), [], size, 4 * size, center, other, gain_one)
    pieces = turn([band] * rows, turned)
    small = (bias_one, gain_two, bias_two, weights[0])
    bias_one, gain_two, bias_two, near = call(
        stage_body, [sds(v.shape, v.dtype) for v in small], [pltpu.SemaphoreType.DMA((len(small),))],
        size, 4 * size, *small, far=range(len(small)),
    )
    past_rows = packed_rows(PAST * breadth, EDGE * frames, channels)
    past = call(
        functools.partial(cut_body, frames * breadth, PAST * breadth), sds((rows, past_rows, LANES), bf16), [],
        size, 4 * size, *pieces,
    )
    past = following(past)
    late_sent, early_sent = (packed_rows(count * breadth, count, channels) for count in (late, PAST))
    late_rows, early_rows = (padded_rows(count * (breadth + 1)) for count in (late, PAST))
    sums = sds((rows + 2, late, ring, width), f32)
    near_sums = call(
        functools.partial(first_near_body, breadth, rows), sums,
        [VMEM((frames, rows - LAST, ring, channels), bf16)], late * work * (rows - LAST) // rows, 10 * size,
        *pieces[:-LAST], near,
    )
    part, _ = call(
        functools.partial(first_late_body, breadth, rows), [sds((late_sent, LANES), bf16), sums],
        [VMEM((frames, LAST, ring, channels), bf16)], late * work * LAST // rows, 10 * size,
        *pieces[-LAST:], near_sums, near, bias_one, aliases={LAST: 1},
    )
    late_parts = spread(part)
    part = call(
        functools.partial(first_early_body, breadth, rows, frames), sds((early_sent, LANES), bf16),
        [padded(2 * PAST)], PAST * work, 20 * size, *pieces, past, near, bias_one,
    )
    early_parts = spread(part)
    second, last = call(
        functools.partial(regroup_body, breadth),
        [sds((rows, middle, ring, channels), bf16), sds((rows, PAST, ring, channels), bf16)],
        [VMEM((rows, late_rows, channels), f32)], 10 * size * rows, 4 * size * rows, *late_parts, gain_two,
    )
    past = following(last)
    back_rows = padded_rows(-(-frames * breadth // rows))
    late_sums = call(
        functools.partial(second_late_body, frames), sds((rows, late, ring, width), f32), [],
        frames * work // 3, 10 * size, second, last, weights[1],
    )
    past_sums = call(
        second_past_body, sds((rows, PAST, ring, width), f32), [],
        frames * work // 5, 10 * size, past, weights[1],
    )
    branch = call(
        functools.partial(second_body, breadth), [sds((back_rows, channels), bf16)] * rows,
        [padded(PAST), VMEM((rows, early_rows, channels), f32), VMEM((rows, back_rows * rows, width), f32)],
        frames * work // 2, 20 * size, *early_parts, late_sums, past_sums, gain_two, weights[1], bias_two,
    )
    branch = turn(branch, returned)
    result = call(
        last_body, sds((frames, breadth, channels), bf16), [VMEM((rows, back_rows * rows, width), f32)],
        2 * size, 6 * size, own, *branch,
    )
    return result.reshape(frames, height, breadth, channels)


def band_order(rows, crosses):
    return [*range(rows - 1, 2, -1), 0] + ([2, 1] if crosses else [1, 2])


def solution(mesh):
    shape = dict(mesh.shape)
    return jax.shard_map(
        functools.partial(shards, shape),
        mesh=mesh,
        in_specs=(
            P(("groups", "tm"), "rows", "cols", None),
            P(),
            P(None, "rows", None),
            P(),
            P(),
            P(None, "rows", None),
            P(),
        ),
        out_specs=P(("groups", "tm"), "rows", "cols", None),
        check_vma=False,
    )
```

```python
import functools

import jax
import jax.numpy as jnp
from jax import lax
from jax.experimental import pallas as pl
from jax.experimental.pallas import tpu as pltpu
from jax.sharding import PartitionSpec as P


AXES = ("rows", "tm", "cols")
EDGE = 2
LANES = 128
LAST = 2
PAST = 2
TAPS = 3
VMEM = pltpu.VMEM


def activate(values, gain_values):
    values = values.astype(jnp.float32)
    mean_square = jnp.mean(values * values, axis=-1, keepdims=True)
    return jax.nn.silu(values * lax.rsqrt(mean_square + 1e-06) * gain_values)


def call(body, out_shape, scratch, flops, moved, *operands, far=(), aliases=None):
    operands = [pltpu.with_memory_space_constraint(v, pltpu.HBM) if i in far else v for i, v in enumerate(operands)]
    spaces = [pltpu.HBM if i in far else VMEM for i in range(len(operands))]
    return pl.pallas_call(
        body,
        out_shape=out_shape,
        in_specs=[pl.BlockSpec(memory_space=space) for space in spaces],
        out_specs=jax.tree.map(lambda _: pl.BlockSpec(memory_space=VMEM), out_shape),
        scratch_shapes=scratch,
        input_output_aliases=aliases or {},
        cost_estimate=pl.CostEstimate(flops=flops, bytes_accessed=moved, transcendentals=0),
        compiler_params=pltpu.CompilerParams(vmem_limit_bytes=48 << 20),
    )(*operands)


def ring_of(center, end, half):
    gap = jnp.zeros((8 - end.shape[0], center.shape[1]), center.dtype)
    after = jnp.concatenate([end, gap], axis=0)
    before = jnp.concatenate([gap, end], axis=0)
    return jnp.concatenate([center, jnp.where(half == 0, after, before)], axis=0)


def padded_rows(count):
    return -(-count // 8) * 8


def packed_rows(count, ends, channels):
    blocks = channels // LANES
    return count * blocks + padded_rows(ends * blocks)


def lane_blocks(values):
    return [values[:, i : i + LANES] for i in range(0, values.shape[1], LANES)]


def pack(center, ends, out_ref):
    parts = lane_blocks(center) + lane_blocks(ends)
    rest = out_ref.shape[0] - sum(part.shape[0] for part in parts)
    if rest:
        parts.append(jnp.zeros((rest, LANES), jnp.float32))
    out_ref[...] = jnp.concatenate(parts, axis=0).astype(jnp.bfloat16)


def unpack(values, count, ends, channels):
    blocks = channels // LANES
    center = jnp.concatenate([values[i * count : (i + 1) * count] for i in range(blocks)], axis=1)
    start = blocks * count
    return center, jnp.concatenate([values[start + i * ends : start + (i + 1) * ends] for i in range(blocks)], axis=1)


def own_part(vector, row, width):
    parts = vector.shape[1] // width
    return sum(jnp.where(row == s, vector[:, s * width : (s + 1) * width], 0.0) for s in range(parts))


def own_body(own_ref, far_gain_ref, out_ref, gain_ref, held, sems):
    copies = [
        pltpu.make_async_copy(own_ref, held, sems.at[0]),
        pltpu.make_async_copy(far_gain_ref, gain_ref, sems.at[1]),
    ]
    for copy in copies:
        copy.start()
    for copy in copies:
        copy.wait()
    frames, breadth, channels = held.shape
    values = activate(held[...], gain_ref[...].reshape(1, channels))
    blocks = lane_blocks(values.reshape(frames * breadth, channels))
    out_ref[...] = jnp.concatenate(blocks, axis=0).astype(jnp.bfloat16)


def ends_body(center_ref, other_ref, gain_ref, out_ref):
    frames, breadth, channels = other_ref.shape
    half = lax.axis_index("cols")
    chosen = jnp.where(half == 0, other_ref[:, 0:8].astype(jnp.float32), other_ref[:, breadth - 8 :].astype(jnp.float32))
    values = activate(chosen, gain_ref[...].reshape(1, channels))
    ends = [jnp.where(half == 0, values[f, 0:EDGE], values[f, 8 - EDGE : 8]) for f in range(frames)]
    blocks = lane_blocks(jnp.concatenate(ends, axis=0))
    count = center_ref.shape[0]
    rest = out_ref.shape[0] - count - len(blocks) * EDGE * frames
    if rest:
        blocks.append(jnp.zeros((rest, LANES), jnp.float32))
    out_ref[0:count] = center_ref[...]
    out_ref[count:] = jnp.concatenate(blocks, axis=0).astype(jnp.bfloat16)


def stage_body(*refs):
    count = len(refs) // 2
    far, near, sems = refs[:count], refs[count : 2 * count], refs[2 * count]
    copies = [pltpu.make_async_copy(a, b, sems.at[i]) for i, (a, b) in enumerate(zip(far, near))]
    for copy in copies:
        copy.start()
    for copy in copies:
        copy.wait()


def fill_first(padded, at, centers, ends, picks, breadth):
    half = lax.axis_index("tm") % 2
    for i, (frame, end) in enumerate(picks):
        center = centers[frame * breadth : (frame + 1) * breadth]
        padded[i + at[0], at[1]] = ring_of(center, ends[end * EDGE : (end + 1) * EDGE], half).astype(jnp.bfloat16)


def multiply(windows, weight_ref, taps):
    return lax.dot_general(
        jnp.concatenate(windows, axis=1),
        jnp.concatenate([weight_ref[t] for t in taps], axis=1),
        (((1,), (1,)), ((), ())),
        preferred_element_type=jnp.float32,
    )


def row_sums(product):
    height, wide = product.shape[1], product.shape[3] // TAPS
    rows = []
    for h in range(height):
        near = [product[:, h + r - 1, :, r * wide : (r + 1) * wide] for r in range(TAPS) if 0 <= h + r - 1 < height]
        rows.append(sum(near[1:], near[0]))
    return rows


def column_sum(row):
    ring, width = row.shape[1], row.shape[2] // TAPS
    before = pltpu.roll(row[:, :, 0:width], 1, 1)
    after = pltpu.roll(row[:, :, 2 * width : 3 * width], ring - 1, 1)
    return before + row[:, :, width : 2 * width] + after


def conv_sum(padded, weight_ref, bias_row):
    frames, height, ring, channels = padded.shape[0] - PAST, padded.shape[1], padded.shape[2], padded.shape[3]
    windows = [padded[t : t + frames].reshape(frames * height * ring, channels) for t in range(TAPS)]
    product = multiply(windows, weight_ref, range(TAPS)).reshape(frames, height, ring, -1)
    return [column_sum(row) + bias_row for row in row_sums(product)]


def add_rows(padded, rows, weight_ref, total):
    frames, height, ring, channels = padded.shape[0] - PAST, padded.shape[1], padded.shape[2], padded.shape[3]
    windows = [padded[t : t + frames].reshape(frames * height * ring, channels) for t in range(TAPS)]
    product = multiply(windows, weight_ref, range(TAPS)).reshape(frames, height, ring, -1)
    wide = product.shape[3] // TAPS
    for i, row in enumerate(rows):
        for r in range(TAPS):
            total[row + 2 - r] += column_sum(product[:, i, :, r * wide : (r + 1) * wide])


def frame_terms(frames, wanted):
    groups = {}
    for f in range(frames):
        taps = tuple(t for t in range(TAPS) if wanted(f + t))
        groups.setdefault(taps, []).append(f)
    return [(taps, outs) for taps, outs in groups.items() if taps]


def frame_sums(frame_of, frames, wanted, weight_ref, height, ring, add):
    for taps, outs in frame_terms(frames, wanted):
        windows = [jnp.concatenate([frame_of(f + t) for f in outs], axis=0) for t in taps]
        product = multiply(windows, weight_ref, taps).reshape(len(outs), height, ring, -1)
        for h, row in enumerate(row_sums(product)):
            shifted = column_sum(row)
            for i, f in enumerate(outs):
                add(f, h, shifted[i])


def piece_rows(height, sibling=False):
    crossed = (lax.axis_index("tm") % 2 == lax.axis_index("cols")) != sibling
    row = lax.axis_index("rows")
    return [row ^ jnp.where(crossed, a, b) for a, b in zip(band_order(height, True), band_order(height, False))]


def block_number():
    return lax.axis_index("tm") // 2 * 2 + 1 - lax.axis_index("cols")


def pack_first(rows, out_ref, breadth):
    half = lax.axis_index("tm") % 2
    frames, ring, width = rows[0].shape
    centers = [row[:, 0:breadth].reshape(frames * breadth, width) for row in rows]
    ends = [
        jnp.concatenate(
            [jnp.where(half == 0, row[f, breadth : breadth + 1], row[f, ring - 1 : ring]) for f in range(frames)], axis=0
        )
        for row in rows
    ]
    pack(jnp.concatenate(centers, axis=1), jnp.concatenate(ends, axis=1), out_ref)


def bias_part(bias_ref, row, weight_ref):
    return own_part(bias_ref[...].reshape(1, -1), row, weight_ref.shape[1] // TAPS // TAPS)


def fill_slots(padded, pieces, breadth):
    frames = padded.shape[0]
    picks = [(f, f) for f in range(frames)]
    for i, piece in enumerate(pieces):
        values = piece[...].astype(jnp.float32)
        center, ends = unpack(values, frames * breadth, frames * EDGE, padded.shape[3])
        fill_first(padded, (0, i), center, ends, picks, breadth)


def first_near_body(breadth, height, *refs):
    *pieces, weight_ref, total, padded = refs
    fill_slots(padded, pieces, breadth)
    total[...] = jnp.zeros_like(total)
    add_rows(padded, piece_rows(height)[:-LAST], weight_ref, total)


def first_late_body(breadth, height, *refs):
    *pieces, near_ref, weight_ref, bias_ref, out_ref, total, padded = refs
    row = lax.axis_index("rows")
    fill_slots(padded, pieces, breadth)
    add_rows(padded, piece_rows(height)[-LAST:], weight_ref, total)
    bias_row = bias_part(bias_ref, row, weight_ref)
    pack_first([total[h + 1] + bias_row for h in range(height)], out_ref, breadth)


def cut_body(count, kept, *refs):
    *pieces, out_ref = refs
    for k, piece in enumerate(pieces):
        blocks = piece.shape[0] // count
        for i in range(blocks):
            out_ref[k, i * kept : (i + 1) * kept] = piece[(i + 1) * count - kept : (i + 1) * count]
        out_ref[k, blocks * kept :] = piece[blocks * count :]


def first_early_body(breadth, height, frames, *refs):
    *pieces, past_ref, weight_ref, bias_ref, out_ref, padded = refs
    row = lax.axis_index("rows")
    for k, (own, other) in enumerate(zip(piece_rows(height), piece_rows(height, True))):
        past = past_ref[k].astype(jnp.float32)
        past = jnp.where(block_number() > 0, past, jnp.zeros_like(past))
        picks = [(j, frames - PAST + j) for j in range(PAST)]
        center, ends = unpack(past, PAST * breadth, frames * EDGE, padded.shape[3])
        fill_first(padded, (0, other), center, ends, picks, breadth)
        center, ends = unpack(pieces[k][...].astype(jnp.float32), frames * breadth, frames * EDGE, padded.shape[3])
        fill_first(padded, (PAST, own), center, ends, [(j, j) for j in range(PAST)], breadth)
    pack_first(conv_sum(padded, weight_ref, bias_part(bias_ref, row, weight_ref)), out_ref, breadth)


def regroup(pieces, gain_ref, held, breadth, frames, store):
    row = lax.axis_index("rows")
    half = lax.axis_index("tm") % 2
    height, channels = len(pieces), held.shape[2]
    width = channels // height
    count = frames * breadth
    first = lax.axis_index("cols") == 0
    sources = [row] + [row ^ jnp.where(first, a, b) for a, b in zip(*send_orders(height))]
    for source, piece in zip(sources, pieces):
        center, ends = unpack(piece[...].astype(jnp.float32), count, frames, channels)
        held[source, 0:count] = center
        held[source, count : count + frames] = ends
    gain_values = gain_ref[...].reshape(1, channels)
    for h in range(height):
        joined = [held[s, :, h * width : (h + 1) * width] for s in range(height)]
        values = activate(jnp.concatenate(joined, axis=1), gain_values)
        for f in range(frames):
            end = frames * breadth + f
            ring = ring_of(values[f * breadth : (f + 1) * breadth], values[end : end + 1], half)
            store(h, f, ring.astype(jnp.bfloat16))


def regroup_body(breadth, *refs):
    *pieces, gain_ref, out_ref, last_ref, held = refs
    middle, late = out_ref.shape[1], last_ref.shape[1]

    def store(h, f, ring):
        if f < middle:
            out_ref[h, f] = ring
        else:
            last_ref[h, f - middle] = ring

    regroup(pieces, gain_ref, held, breadth, middle + late, store)


def second_late_body(frames, middle_ref, last_ref, weight_ref, total):
    height, middle, ring, channels = middle_ref.shape

    def frame_of(p):
        p -= 2 * PAST
        values = middle_ref[:, p] if p < middle else last_ref[:, p - middle]
        return values.reshape(height * ring, channels)

    def add(f, h, values):
        total[h, f - PAST] = values

    frame_sums(frame_of, frames, lambda p: p >= 2 * PAST, weight_ref, height, ring, add)


def second_past_body(past_ref, weight_ref, total):
    height, _, ring, channels = past_ref.shape

    def frame_of(p):
        values = past_ref[:, p]
        return jnp.where(block_number() > 0, values, jnp.zeros_like(values)).reshape(height * ring, channels)

    def add(f, h, values):
        total[h, f] = values

    frame_sums(frame_of, PAST, lambda p: p < PAST, weight_ref, height, ring, add)


def second_body(breadth, *refs):
    height = (len(refs) - 8) // 2
    pieces, refs = refs[:height], refs[height:]
    late_ref, past_ref, gain_ref, weight_ref, bias_ref = refs[:5]
    outs, (early, held, branch) = refs[5 : 5 + height], refs[5 + height :]
    row = lax.axis_index("rows")

    def store(h, f, ring):
        early[f, h] = ring

    regroup(pieces, gain_ref, held, breadth, PAST, store)
    _, frames, ring, _ = late_ref.shape
    frames += PAST
    channels = early.shape[3]
    sums = {}

    def held_sum(f, h):
        return past_ref[h, f] if f < PAST else late_ref[h, f - PAST]

    def add(f, h, values):
        sums[f, h] = held_sum(f, h) + values

    def frame_of(p):
        return early[p - PAST].reshape(height * ring, channels)

    frame_sums(frame_of, frames, lambda p: PAST <= p < 2 * PAST, weight_ref, height, ring, add)
    bias_row = bias_part(bias_ref, row, weight_ref)
    for h in range(height):
        for f in range(frames):
            values = sums[f, h] if (f, h) in sums else held_sum(f, h)
            branch[h, f * breadth : (f + 1) * breadth] = values[0:breadth] + bias_row
    for k, out_ref in enumerate(outs):
        chosen = branch[row ^ k]
        rows = out_ref.shape[0]
        parts = [chosen[i * rows : (i + 1) * rows] for i in range(height)]
        out_ref[...] = jnp.concatenate(parts, axis=1).astype(jnp.bfloat16)


def last_body(latents_ref, *refs):
    *pieces, out_ref, held = refs
    row = lax.axis_index("rows")
    height = len(pieces)
    frames, breadth, channels = latents_ref.shape
    width = channels // height
    for k, piece in enumerate(pieces):
        values = piece[...].astype(jnp.float32)
        parts = [values[:, i * width : (i + 1) * width] for i in range(height)]
        held[row ^ k] = jnp.concatenate(parts, axis=0)
    branch = jnp.concatenate([held[s] for s in range(height)], axis=1)
    branch = branch[0 : frames * breadth].reshape(frames, breadth, channels)
    out_ref[...] = (latents_ref[...].astype(jnp.float32) + branch).astype(jnp.bfloat16)


def shards(shape, latents, gain_one, conv_one, bias_one, gain_two, conv_two, bias_two):
    rows, tm, cols = (shape[name] for name in AXES)
    frames, height, breadth, channels = latents.shape
    width = channels // rows
    ring = breadth + 8
    late, middle = frames - PAST, frames - 2 * PAST
    bf16, f32 = jnp.bfloat16, jnp.float32
    own = latents.reshape(frames, breadth, channels)
    every = [(z, x, c) for z in range(rows) for x in range(tm) for c in range(cols)]
    place = {device: i for i, device in enumerate(every)}

    def moved(values, target):
        return lax.ppermute(values, AXES, [(place[device], place[target(*device)]) for device in every])

    def turned(values, k):
        steps = {crosses: band_order(rows, crosses)[k] for crosses in (True, False)}
        return moved(values, lambda z, x, c: (z ^ steps[x % 2 != c], x // 2 * 2 + c, 1 - x % 2))

    def returned(values, k):
        return moved(values, lambda z, x, c: (z ^ k, x // 2 * 2 + 1 - c, x % 2))

    def following(values):
        return moved(values, lambda z, x, c: (z, x, 0) if c == 1 else (z, (x + 2) % tm, 1))

    def spread(values):
        parts = [values]
        for steps in zip(*send_orders(rows)):
            pairs = [(z * cols + c, (z ^ steps[c]) * cols + c) for z in range(rows) for c in range(cols)]
            parts.append(lax.ppermute(values, ("rows", "cols"), pairs))
        return parts

    def turn(values, way):
        parts = []
        for k in range(rows):
            parts.append(way(values[k], k))
        return parts

    other = lax.ppermute(own, "cols", [(0, 1), (1, 0)])
    weights = [w.reshape(TAPS, TAPS * TAPS * width, channels) for w in (conv_one, conv_two)]
    sds = jax.ShapeDtypeStruct
    size = frames * ring * channels
    work = 2 * ring * channels * rows * 27 * width

    def padded(count):
        return VMEM((count, rows, ring, channels), bf16)

    center, gain_one = call(
        own_body, [sds((frames * breadth * channels // LANES, LANES), bf16), sds(gain_one.shape, f32)],
        [VMEM((frames, breadth, channels), bf16), pltpu.SemaphoreType.DMA((2,))],
        10 * size, 6 * size, own, gain_one, far=(0, 1),
    )
    total = packed_rows(frames * breadth, EDGE * frames, channels)
    band = call(ends_body, sds((total, LANES), bf16), [], size, 4 * size, center, other, gain_one)
    pieces = turn([band] * rows, turned)
    small = (bias_one, gain_two, bias_two, weights[0])
    bias_one, gain_two, bias_two, near = call(
        stage_body, [sds(v.shape, v.dtype) for v in small], [pltpu.SemaphoreType.DMA((len(small),))],
        size, 4 * size, *small, far=range(len(small)),
    )
    past_rows = packed_rows(PAST * breadth, EDGE * frames, channels)
    past = call(
        functools.partial(cut_body, frames * breadth, PAST * breadth), sds((rows, past_rows, LANES), bf16), [],
        size, 4 * size, *pieces,
    )
    past = following(past)
    late_sent, early_sent = (packed_rows(count * breadth, count, channels) for count in (late, PAST))
    late_rows, early_rows = (padded_rows(count * (breadth + 1)) for count in (late, PAST))
    sums = sds((rows + 2, late, ring, width), f32)
    near_sums = call(
        functools.partial(first_near_body, breadth, rows), sums,
        [VMEM((frames, rows - LAST, ring, channels), bf16)], late * work * (rows - LAST) // rows, 10 * size,
        *pieces[:-LAST], near,
    )
    part, _ = call(
        functools.partial(first_late_body, breadth, rows), [sds((late_sent, LANES), bf16), sums],
        [VMEM((frames, LAST, ring, channels), bf16)], late * work * LAST // rows, 10 * size,
        *pieces[-LAST:], near_sums, near, bias_one, aliases={LAST: 1},
    )
    late_parts = spread(part)
    part = call(
        functools.partial(first_early_body, breadth, rows, frames), sds((early_sent, LANES), bf16),
        [padded(2 * PAST)], PAST * work, 20 * size, *pieces, past, near, bias_one,
    )
    early_parts = spread(part)
    second, last = call(
        functools.partial(regroup_body, breadth),
        [sds((rows, middle, ring, channels), bf16), sds((rows, PAST, ring, channels), bf16)],
        [VMEM((rows, late_rows, channels), f32)], 10 * size * rows, 4 * size * rows, *late_parts, gain_two,
    )
    past = following(last)
    back_rows = padded_rows(-(-frames * breadth // rows))
    late_sums = call(
        functools.partial(second_late_body, frames), sds((rows, late, ring, width), f32), [],
        frames * work // 3, 10 * size, second, last, weights[1],
    )
    past_sums = call(
        second_past_body, sds((rows, PAST, ring, width), f32), [],
        frames * work // 5, 10 * size, past, weights[1],
    )
    branch = call(
        functools.partial(second_body, breadth), [sds((back_rows, channels), bf16)] * rows,
        [padded(PAST), VMEM((rows, early_rows, channels), f32), VMEM((rows, back_rows * rows, width), f32)],
        frames * work // 2, 20 * size, *early_parts, late_sums, past_sums, gain_two, weights[1], bias_two,
    )
    branch = turn(branch, returned)
    result = call(
        last_body, sds((frames, breadth, channels), bf16), [VMEM((rows, back_rows * rows, width), f32)],
        2 * size, 6 * size, own, *branch,
    )
    return result.reshape(frames, height, breadth, channels)


def band_order(rows, crosses):
    return [*range(rows - 1, 2, -1), 0] + ([2, 1] if crosses else [1, 2])


def send_orders(rows):
    return [*range(rows - 1, 0, -1)], [1, *range(rows - 1, 1, -1)]


def solution(mesh):
    shape = dict(mesh.shape)
    return jax.shard_map(
        functools.partial(shards, shape),
        mesh=mesh,
        in_specs=(
            P(("groups", "tm"), "rows", "cols", None),
            P(),
            P(None, "rows", None),
            P(),
            P(),
            P(None, "rows", None),
            P(),
        ),
        out_specs=P(("groups", "tm"), "rows", "cols", None),
        check_vma=False,
    )
```

```python
import functools

import jax
import jax.numpy as jnp
from jax import lax
from jax.experimental import pallas as pl
from jax.experimental.pallas import tpu as pltpu
from jax.sharding import PartitionSpec as P


AXES = ("rows", "tm", "cols")
EDGE = 2
LANES = 128
LAST = 2
PAST = 2
TAPS = 3
VMEM = pltpu.VMEM


def activate(values, gain_values):
    values = values.astype(jnp.float32)
    mean_square = jnp.mean(values * values, axis=-1, keepdims=True)
    return jax.nn.silu(values * lax.rsqrt(mean_square + 1e-06) * gain_values)


def call(body, out_shape, scratch, flops, moved, *operands, far=(), aliases=None):
    operands = [pltpu.with_memory_space_constraint(v, pltpu.HBM) if i in far else v for i, v in enumerate(operands)]
    spaces = [pltpu.HBM if i in far else VMEM for i in range(len(operands))]
    return pl.pallas_call(
        body,
        out_shape=out_shape,
        in_specs=[pl.BlockSpec(memory_space=space) for space in spaces],
        out_specs=jax.tree.map(lambda _: pl.BlockSpec(memory_space=VMEM), out_shape),
        scratch_shapes=scratch,
        input_output_aliases=aliases or {},
        cost_estimate=pl.CostEstimate(flops=flops, bytes_accessed=moved, transcendentals=0),
        compiler_params=pltpu.CompilerParams(vmem_limit_bytes=48 << 20),
    )(*operands)


def ring_of(center, end, half):
    gap = jnp.zeros((8 - end.shape[0], center.shape[1]), center.dtype)
    after = jnp.concatenate([end, gap], axis=0)
    before = jnp.concatenate([gap, end], axis=0)
    return jnp.concatenate([center, jnp.where(half == 0, after, before)], axis=0)


def padded_rows(count):
    return -(-count // 8) * 8


def packed_rows(count, ends, channels):
    blocks = channels // LANES
    return count * blocks + padded_rows(ends * blocks)


def lane_blocks(values):
    return [values[:, i : i + LANES] for i in range(0, values.shape[1], LANES)]


def pack(center, ends, out_ref):
    parts = lane_blocks(center) + lane_blocks(ends)
    rest = out_ref.shape[0] - sum(part.shape[0] for part in parts)
    if rest:
        parts.append(jnp.zeros((rest, LANES), jnp.float32))
    out_ref[...] = jnp.concatenate(parts, axis=0).astype(jnp.bfloat16)


def unpack(values, count, ends, channels):
    blocks = channels // LANES
    center = jnp.concatenate([values[i * count : (i + 1) * count] for i in range(blocks)], axis=1)
    start = blocks * count
    return center, jnp.concatenate([values[start + i * ends : start + (i + 1) * ends] for i in range(blocks)], axis=1)


def own_part(vector, row, width):
    parts = vector.shape[1] // width
    return sum(jnp.where(row == s, vector[:, s * width : (s + 1) * width], 0.0) for s in range(parts))


def own_body(own_ref, far_gain_ref, out_ref, gain_ref, held, sems):
    copies = [
        pltpu.make_async_copy(own_ref, held, sems.at[0]),
        pltpu.make_async_copy(far_gain_ref, gain_ref, sems.at[1]),
    ]
    for copy in copies:
        copy.start()
    for copy in copies:
        copy.wait()
    frames, breadth, channels = held.shape
    values = activate(held[...], gain_ref[...].reshape(1, channels))
    blocks = lane_blocks(values.reshape(frames * breadth, channels))
    out_ref[...] = jnp.concatenate(blocks, axis=0).astype(jnp.bfloat16)


def ends_body(center_ref, other_ref, gain_ref, out_ref):
    frames, breadth, channels = other_ref.shape
    half = lax.axis_index("cols")
    chosen = jnp.where(half == 0, other_ref[:, 0:8].astype(jnp.float32), other_ref[:, breadth - 8 :].astype(jnp.float32))
    values = activate(chosen, gain_ref[...].reshape(1, channels))
    ends = [jnp.where(half == 0, values[f, 0:EDGE], values[f, 8 - EDGE : 8]) for f in range(frames)]
    blocks = lane_blocks(jnp.concatenate(ends, axis=0))
    count = center_ref.shape[0]
    rest = out_ref.shape[0] - count - len(blocks) * EDGE * frames
    if rest:
        blocks.append(jnp.zeros((rest, LANES), jnp.float32))
    out_ref[0:count] = center_ref[...]
    out_ref[count:] = jnp.concatenate(blocks, axis=0).astype(jnp.bfloat16)


def stage_body(*refs):
    count = len(refs) // 2
    far, near, sems = refs[:count], refs[count : 2 * count], refs[2 * count]
    copies = [pltpu.make_async_copy(a, b, sems.at[i]) for i, (a, b) in enumerate(zip(far, near))]
    for copy in copies:
        copy.start()
    for copy in copies:
        copy.wait()


def fill_first(padded, at, centers, ends, picks, breadth):
    half = lax.axis_index("tm") % 2
    for i, (frame, end) in enumerate(picks):
        center = centers[frame * breadth : (frame + 1) * breadth]
        padded[i + at[0], at[1]] = ring_of(center, ends[end * EDGE : (end + 1) * EDGE], half).astype(jnp.bfloat16)


def multiply(windows, weight_ref, taps):
    return lax.dot_general(
        jnp.concatenate(windows, axis=1),
        jnp.concatenate([weight_ref[t] for t in taps], axis=1),
        (((1,), (1,)), ((), ())),
        preferred_element_type=jnp.float32,
    )


def row_sums(product):
    height, wide = product.shape[1], product.shape[3] // TAPS
    rows = []
    for h in range(height):
        near = [product[:, h + r - 1, :, r * wide : (r + 1) * wide] for r in range(TAPS) if 0 <= h + r - 1 < height]
        rows.append(sum(near[1:], near[0]))
    return rows


def column_sum(row):
    ring, width = row.shape[1], row.shape[2] // TAPS
    before = pltpu.roll(row[:, :, 0:width], 1, 1)
    after = pltpu.roll(row[:, :, 2 * width : 3 * width], ring - 1, 1)
    return before + row[:, :, width : 2 * width] + after


def conv_sum(padded, weight_ref, bias_row):
    frames, height, ring, channels = padded.shape[0] - PAST, padded.shape[1], padded.shape[2], padded.shape[3]
    windows = [padded[t : t + frames].reshape(frames * height * ring, channels) for t in range(TAPS)]
    product = multiply(windows, weight_ref, range(TAPS)).reshape(frames, height, ring, -1)
    return [column_sum(row) + bias_row for row in row_sums(product)]


def add_rows(padded, rows, weight_ref, total):
    frames, height, ring, channels = padded.shape[0] - PAST, padded.shape[1], padded.shape[2], padded.shape[3]
    windows = [padded[t : t + frames].reshape(frames * height * ring, channels) for t in range(TAPS)]
    product = multiply(windows, weight_ref, range(TAPS)).reshape(frames, height, ring, -1)
    wide = product.shape[3] // TAPS
    for i, row in enumerate(rows):
        for r in range(TAPS):
            total[row + 2 - r] += column_sum(product[:, i, :, r * wide : (r + 1) * wide])


def frame_terms(frames, wanted):
    groups = {}
    for f in range(frames):
        taps = tuple(t for t in range(TAPS) if wanted(f + t))
        groups.setdefault(taps, []).append(f)
    return [(taps, outs) for taps, outs in groups.items() if taps]


def frame_sums(frame_of, frames, wanted, weight_ref, height, ring, add):
    for taps, outs in frame_terms(frames, wanted):
        windows = [jnp.concatenate([frame_of(f + t) for f in outs], axis=0) for t in taps]
        product = multiply(windows, weight_ref, taps).reshape(len(outs), height, ring, -1)
        for h, row in enumerate(row_sums(product)):
            shifted = column_sum(row)
            for i, f in enumerate(outs):
                add(f, h, shifted[i])


def piece_rows(height, sibling=False):
    crossed = (lax.axis_index("tm") % 2 == lax.axis_index("cols")) != sibling
    row = lax.axis_index("rows")
    return [row ^ jnp.where(crossed, a, b) for a, b in zip(band_order(height, True), band_order(height, False))]


def block_number():
    return lax.axis_index("tm") // 2 * 2 + 1 - lax.axis_index("cols")


def pack_first(rows, out_ref, breadth):
    half = lax.axis_index("tm") % 2
    frames, ring, width = rows[0].shape
    centers = [row[:, 0:breadth].reshape(frames * breadth, width) for row in rows]
    ends = [
        jnp.concatenate(
            [jnp.where(half == 0, row[f, breadth : breadth + 1], row[f, ring - 1 : ring]) for f in range(frames)], axis=0
        )
        for row in rows
    ]
    pack(jnp.concatenate(centers, axis=1), jnp.concatenate(ends, axis=1), out_ref)


def bias_part(bias_ref, row, weight_ref):
    return own_part(bias_ref[...].reshape(1, -1), row, weight_ref.shape[1] // TAPS // TAPS)


def fill_slots(padded, pieces, breadth):
    frames = padded.shape[0]
    picks = [(f, f) for f in range(frames)]
    for i, piece in enumerate(pieces):
        values = piece[...].astype(jnp.float32)
        center, ends = unpack(values, frames * breadth, frames * EDGE, padded.shape[3])
        fill_first(padded, (0, i), center, ends, picks, breadth)


def first_near_body(breadth, height, *refs):
    *pieces, weight_ref, total, padded = refs
    fill_slots(padded, pieces, breadth)
    total[...] = jnp.zeros_like(total)
    add_rows(padded, piece_rows(height)[:-LAST], weight_ref, total)


def first_late_body(breadth, height, *refs):
    *pieces, near_ref, weight_ref, bias_ref, out_ref, total, padded = refs
    row = lax.axis_index("rows")
    fill_slots(padded, pieces, breadth)
    add_rows(padded, piece_rows(height)[-LAST:], weight_ref, total)
    bias_row = bias_part(bias_ref, row, weight_ref)
    pack_first([total[h + 1] + bias_row for h in range(height)], out_ref, breadth)


def cut_body(count, kept, *refs):
    *pieces, out_ref = refs
    for k, piece in enumerate(pieces):
        blocks = piece.shape[0] // count
        for i in range(blocks):
            out_ref[k, i * kept : (i + 1) * kept] = piece[(i + 1) * count - kept : (i + 1) * count]
        out_ref[k, blocks * kept :] = piece[blocks * count :]


def first_early_body(breadth, height, frames, *refs):
    *pieces, past_ref, weight_ref, bias_ref, out_ref, padded = refs
    row = lax.axis_index("rows")
    for k, (own, other) in enumerate(zip(piece_rows(height), piece_rows(height, True))):
        past = past_ref[k].astype(jnp.float32)
        past = jnp.where(block_number() > 0, past, jnp.zeros_like(past))
        picks = [(j, frames - PAST + j) for j in range(PAST)]
        center, ends = unpack(past, PAST * breadth, frames * EDGE, padded.shape[3])
        fill_first(padded, (0, other), center, ends, picks, breadth)
        center, ends = unpack(pieces[k][...].astype(jnp.float32), frames * breadth, frames * EDGE, padded.shape[3])
        fill_first(padded, (PAST, own), center, ends, [(j, j) for j in range(PAST)], breadth)
    pack_first(conv_sum(padded, weight_ref, bias_part(bias_ref, row, weight_ref)), out_ref, breadth)


def regroup(pieces, gain_ref, held, breadth, frames, store, name):
    row = lax.axis_index("rows")
    half = lax.axis_index("tm") % 2
    height, channels = len(pieces), held.shape[2]
    width = channels // height
    count = frames * breadth
    first = lax.axis_index("cols") == 0
    sources = [row] + [row ^ jnp.where(first, a, b) for a, b in zip(*send_orders(height, name))]
    for source, piece in zip(sources, pieces):
        center, ends = unpack(piece[...].astype(jnp.float32), count, frames, channels)
        held[source, 0:count] = center
        held[source, count : count + frames] = ends
    gain_values = gain_ref[...].reshape(1, channels)
    for h in range(height):
        joined = [held[s, :, h * width : (h + 1) * width] for s in range(height)]
        values = activate(jnp.concatenate(joined, axis=1), gain_values)
        for f in range(frames):
            end = frames * breadth + f
            ring = ring_of(values[f * breadth : (f + 1) * breadth], values[end : end + 1], half)
            store(h, f, ring.astype(jnp.bfloat16))


def regroup_body(breadth, *refs):
    *pieces, gain_ref, out_ref, last_ref, held = refs
    middle, late = out_ref.shape[1], last_ref.shape[1]

    def store(h, f, ring):
        if f < middle:
            out_ref[h, f] = ring
        else:
            last_ref[h, f - middle] = ring

    regroup(pieces, gain_ref, held, breadth, middle + late, store, "late")


def second_late_body(frames, middle_ref, last_ref, weight_ref, total):
    height, middle, ring, channels = middle_ref.shape

    def frame_of(p):
        p -= 2 * PAST
        values = middle_ref[:, p] if p < middle else last_ref[:, p - middle]
        return values.reshape(height * ring, channels)

    def add(f, h, values):
        total[h, f - PAST] = values

    frame_sums(frame_of, frames, lambda p: p >= 2 * PAST, weight_ref, height, ring, add)


def second_past_body(past_ref, weight_ref, total):
    height, _, ring, channels = past_ref.shape

    def frame_of(p):
        values = past_ref[:, p]
        return jnp.where(block_number() > 0, values, jnp.zeros_like(values)).reshape(height * ring, channels)

    def add(f, h, values):
        total[h, f] = values

    frame_sums(frame_of, PAST, lambda p: p < PAST, weight_ref, height, ring, add)


def second_body(breadth, *refs):
    height = (len(refs) - 8) // 2
    pieces, refs = refs[:height], refs[height:]
    late_ref, past_ref, gain_ref, weight_ref, bias_ref = refs[:5]
    outs, (early, held, branch) = refs[5 : 5 + height], refs[5 + height :]
    row = lax.axis_index("rows")

    def store(h, f, ring):
        early[f, h] = ring

    regroup(pieces, gain_ref, held, breadth, PAST, store, "early")
    _, frames, ring, _ = late_ref.shape
    frames += PAST
    channels = early.shape[3]
    sums = {}

    def held_sum(f, h):
        return past_ref[h, f] if f < PAST else late_ref[h, f - PAST]

    def add(f, h, values):
        sums[f, h] = held_sum(f, h) + values

    def frame_of(p):
        return early[p - PAST].reshape(height * ring, channels)

    frame_sums(frame_of, frames, lambda p: PAST <= p < 2 * PAST, weight_ref, height, ring, add)
    bias_row = bias_part(bias_ref, row, weight_ref)
    for h in range(height):
        for f in range(frames):
            values = sums[f, h] if (f, h) in sums else held_sum(f, h)
            branch[h, f * breadth : (f + 1) * breadth] = values[0:breadth] + bias_row
    for k, out_ref in enumerate(outs):
        chosen = branch[row ^ k]
        rows = out_ref.shape[0]
        parts = [chosen[i * rows : (i + 1) * rows] for i in range(height)]
        out_ref[...] = jnp.concatenate(parts, axis=1).astype(jnp.bfloat16)


def last_body(latents_ref, *refs):
    *pieces, out_ref, held = refs
    row = lax.axis_index("rows")
    height = len(pieces)
    frames, breadth, channels = latents_ref.shape
    width = channels // height
    for k, piece in enumerate(pieces):
        values = piece[...].astype(jnp.float32)
        parts = [values[:, i * width : (i + 1) * width] for i in range(height)]
        held[row ^ k] = jnp.concatenate(parts, axis=0)
    branch = jnp.concatenate([held[s] for s in range(height)], axis=1)
    branch = branch[0 : frames * breadth].reshape(frames, breadth, channels)
    out_ref[...] = (latents_ref[...].astype(jnp.float32) + branch).astype(jnp.bfloat16)


def shards(shape, latents, gain_one, conv_one, bias_one, gain_two, conv_two, bias_two):
    rows, tm, cols = (shape[name] for name in AXES)
    frames, height, breadth, channels = latents.shape
    width = channels // rows
    ring = breadth + 8
    late, middle = frames - PAST, frames - 2 * PAST
    bf16, f32 = jnp.bfloat16, jnp.float32
    own = latents.reshape(frames, breadth, channels)
    every = [(z, x, c) for z in range(rows) for x in range(tm) for c in range(cols)]
    place = {device: i for i, device in enumerate(every)}

    def moved(values, target):
        return lax.ppermute(values, AXES, [(place[device], place[target(*device)]) for device in every])

    def turned(values, k):
        steps = {crosses: band_order(rows, crosses)[k] for crosses in (True, False)}
        return moved(values, lambda z, x, c: (z ^ steps[x % 2 != c], x // 2 * 2 + c, 1 - x % 2))

    def returned(values, k):
        return moved(values, lambda z, x, c: (z ^ k, x // 2 * 2 + 1 - c, x % 2))

    def following(values):
        return moved(values, lambda z, x, c: (z, x, 0) if c == 1 else (z, (x + 2) % tm, 1))

    def spread(values, name):
        parts = [values]
        for steps in zip(*send_orders(rows, name)):
            pairs = [(z * cols + c, (z ^ steps[c]) * cols + c) for z in range(rows) for c in range(cols)]
            parts.append(lax.ppermute(values, ("rows", "cols"), pairs))
        return parts

    def turn(values, way):
        parts = []
        for k in range(rows):
            parts.append(way(values[k], k))
        return parts

    other = lax.ppermute(own, "cols", [(0, 1), (1, 0)])
    weights = [w.reshape(TAPS, TAPS * TAPS * width, channels) for w in (conv_one, conv_two)]
    sds = jax.ShapeDtypeStruct
    size = frames * ring * channels
    work = 2 * ring * channels * rows * 27 * width

    def padded(count):
        return VMEM((count, rows, ring, channels), bf16)

    center, gain_one = call(
        own_body, [sds((frames * breadth * channels // LANES, LANES), bf16), sds(gain_one.shape, f32)],
        [VMEM((frames, breadth, channels), bf16), pltpu.SemaphoreType.DMA((2,))],
        10 * size, 6 * size, own, gain_one, far=(0, 1),
    )
    total = packed_rows(frames * breadth, EDGE * frames, channels)
    band = call(ends_body, sds((total, LANES), bf16), [], size, 4 * size, center, other, gain_one)
    pieces = turn([band] * rows, turned)
    small = (bias_one, gain_two, bias_two, weights[0])
    bias_one, gain_two, bias_two, near = call(
        stage_body, [sds(v.shape, v.dtype) for v in small], [pltpu.SemaphoreType.DMA((len(small),))],
        size, 4 * size, *small, far=range(len(small)),
    )
    past_rows = packed_rows(PAST * breadth, EDGE * frames, channels)
    past = call(
        functools.partial(cut_body, frames * breadth, PAST * breadth), sds((rows, past_rows, LANES), bf16), [],
        size, 4 * size, *pieces,
    )
    past = following(past)
    late_sent, early_sent = (packed_rows(count * breadth, count, channels) for count in (late, PAST))
    late_rows, early_rows = (padded_rows(count * (breadth + 1)) for count in (late, PAST))
    sums = sds((rows + 2, late, ring, width), f32)
    near_sums = call(
        functools.partial(first_near_body, breadth, rows), sums,
        [VMEM((frames, rows - LAST, ring, channels), bf16)], late * work * (rows - LAST) // rows, 10 * size,
        *pieces[:-LAST], near,
    )
    part, _ = call(
        functools.partial(first_late_body, breadth, rows), [sds((late_sent, LANES), bf16), sums],
        [VMEM((frames, LAST, ring, channels), bf16)], late * work * LAST // rows, 10 * size,
        *pieces[-LAST:], near_sums, near, bias_one, aliases={LAST: 1},
    )
    late_parts = spread(part, "late")
    part = call(
        functools.partial(first_early_body, breadth, rows, frames), sds((early_sent, LANES), bf16),
        [padded(2 * PAST)], PAST * work, 20 * size, *pieces, past, near, bias_one,
    )
    early_parts = spread(part, "early")
    second, last = call(
        functools.partial(regroup_body, breadth),
        [sds((rows, middle, ring, channels), bf16), sds((rows, PAST, ring, channels), bf16)],
        [VMEM((rows, late_rows, channels), f32)], 10 * size * rows, 4 * size * rows, *late_parts, gain_two,
    )
    past = following(last)
    back_rows = padded_rows(-(-frames * breadth // rows))
    late_sums = call(
        functools.partial(second_late_body, frames), sds((rows, late, ring, width), f32), [],
        frames * work // 3, 10 * size, second, last, weights[1],
    )
    past_sums = call(
        second_past_body, sds((rows, PAST, ring, width), f32), [],
        frames * work // 5, 10 * size, past, weights[1],
    )
    branch = call(
        functools.partial(second_body, breadth), [sds((back_rows, channels), bf16)] * rows,
        [padded(PAST), VMEM((rows, early_rows, channels), f32), VMEM((rows, back_rows * rows, width), f32)],
        frames * work // 2, 20 * size, *early_parts, late_sums, past_sums, gain_two, weights[1], bias_two,
    )
    branch = turn(branch, returned)
    result = call(
        last_body, sds((frames, breadth, channels), bf16), [VMEM((rows, back_rows * rows, width), f32)],
        2 * size, 6 * size, own, *branch,
    )
    return result.reshape(frames, height, breadth, channels)


def band_order(rows, crosses):
    return [*range(rows - 1, 2, -1), 0] + ([2, 1] if crosses else [1, 2])


def send_orders(rows, name):
    far = list(range(rows - 1, 0, -1))
    return far, far if name == "late" else far[-1:] + far[:-1]


def solution(mesh):
    shape = dict(mesh.shape)
    return jax.shard_map(
        functools.partial(shards, shape),
        mesh=mesh,
        in_specs=(
            P(("groups", "tm"), "rows", "cols", None),
            P(),
            P(None, "rows", None),
            P(),
            P(),
            P(None, "rows", None),
            P(),
        ),
        out_specs=P(("groups", "tm"), "rows", "cols", None),
        check_vma=False,
    )
```

```python
import functools

import jax
import jax.numpy as jnp
from jax import lax
from jax.experimental import pallas as pl
from jax.experimental.pallas import tpu as pltpu
from jax.sharding import PartitionSpec as P


AXES = ("rows", "tm", "cols")
EDGE = 2
LANES = 128
PAST = 2
TAPS = 3
VMEM = pltpu.VMEM


def activate(values, gain_values):
    values = values.astype(jnp.float32)
    mean_square = jnp.mean(values * values, axis=-1, keepdims=True)
    return jax.nn.silu(values * lax.rsqrt(mean_square + 1e-06) * gain_values)


def call(body, out_shape, scratch, flops, moved, *operands, far=(), aliases=None):
    operands = [pltpu.with_memory_space_constraint(v, pltpu.HBM) if i in far else v for i, v in enumerate(operands)]
    spaces = [pltpu.HBM if i in far else VMEM for i in range(len(operands))]
    return pl.pallas_call(
        body,
        out_shape=out_shape,
        in_specs=[pl.BlockSpec(memory_space=space) for space in spaces],
        out_specs=jax.tree.map(lambda _: pl.BlockSpec(memory_space=VMEM), out_shape),
        scratch_shapes=scratch,
        input_output_aliases=aliases or {},
        cost_estimate=pl.CostEstimate(flops=flops, bytes_accessed=moved, transcendentals=0),
        compiler_params=pltpu.CompilerParams(vmem_limit_bytes=48 << 20),
    )(*operands)


def ring_of(center, end, half):
    gap = jnp.zeros((8 - end.shape[0], center.shape[1]), center.dtype)
    after = jnp.concatenate([end, gap], axis=0)
    before = jnp.concatenate([gap, end], axis=0)
    return jnp.concatenate([center, jnp.where(half == 0, after, before)], axis=0)


def padded_rows(count):
    return -(-count // 8) * 8


def packed_rows(count, ends, channels):
    blocks = channels // LANES
    return count * blocks + padded_rows(ends * blocks)


def lane_blocks(values):
    return [values[:, i : i + LANES] for i in range(0, values.shape[1], LANES)]


def pack(center, ends, out_ref):
    parts = lane_blocks(center) + lane_blocks(ends)
    rest = out_ref.shape[0] - sum(part.shape[0] for part in parts)
    if rest:
        parts.append(jnp.zeros((rest, LANES), jnp.float32))
    out_ref[...] = jnp.concatenate(parts, axis=0).astype(jnp.bfloat16)


def unpack(values, count, ends, channels):
    blocks = channels // LANES
    center = jnp.concatenate([values[i * count : (i + 1) * count] for i in range(blocks)], axis=1)
    start = blocks * count
    return center, jnp.concatenate([values[start + i * ends : start + (i + 1) * ends] for i in range(blocks)], axis=1)


def own_part(vector, row, width):
    parts = vector.shape[1] // width
    return sum(jnp.where(row == s, vector[:, s * width : (s + 1) * width], 0.0) for s in range(parts))


def own_body(own_ref, far_gain_ref, out_ref, gain_ref, held, sems):
    copies = [
        pltpu.make_async_copy(own_ref, held, sems.at[0]),
        pltpu.make_async_copy(far_gain_ref, gain_ref, sems.at[1]),
    ]
    for copy in copies:
        copy.start()
    for copy in copies:
        copy.wait()
    frames, breadth, channels = held.shape
    values = activate(held[...], gain_ref[...].reshape(1, channels))
    blocks = lane_blocks(values.reshape(frames * breadth, channels))
    out_ref[...] = jnp.concatenate(blocks, axis=0).astype(jnp.bfloat16)


def ends_body(center_ref, other_ref, gain_ref, out_ref):
    frames, breadth, channels = other_ref.shape
    half = lax.axis_index("cols")
    chosen = jnp.where(half == 0, other_ref[:, 0:8].astype(jnp.float32), other_ref[:, breadth - 8 :].astype(jnp.float32))
    values = activate(chosen, gain_ref[...].reshape(1, channels))
    ends = [jnp.where(half == 0, values[f, 0:EDGE], values[f, 8 - EDGE : 8]) for f in range(frames)]
    blocks = lane_blocks(jnp.concatenate(ends, axis=0))
    count = center_ref.shape[0]
    rest = out_ref.shape[0] - count - len(blocks) * EDGE * frames
    if rest:
        blocks.append(jnp.zeros((rest, LANES), jnp.float32))
    out_ref[0:count] = center_ref[...]
    out_ref[count:] = jnp.concatenate(blocks, axis=0).astype(jnp.bfloat16)


def stage_body(*refs):
    count = len(refs) // 2
    far, near, sems = refs[:count], refs[count : 2 * count], refs[2 * count]
    copies = [pltpu.make_async_copy(a, b, sems.at[i]) for i, (a, b) in enumerate(zip(far, near))]
    for copy in copies:
        copy.start()
    for copy in copies:
        copy.wait()


def fill_first(padded, at, centers, ends, picks, breadth):
    half = lax.axis_index("tm") % 2
    for i, (frame, end) in enumerate(picks):
        center = centers[frame * breadth : (frame + 1) * breadth]
        padded[i + at[0], at[1]] = ring_of(center, ends[end * EDGE : (end + 1) * EDGE], half).astype(jnp.bfloat16)


def multiply(windows, weight_ref, taps):
    return lax.dot_general(
        jnp.concatenate(windows, axis=1),
        jnp.concatenate([weight_ref[t] for t in taps], axis=1),
        (((1,), (1,)), ((), ())),
        preferred_element_type=jnp.float32,
    )


def row_sums(product):
    height, wide = product.shape[1], product.shape[3] // TAPS
    rows = []
    for h in range(height):
        near = [product[:, h + r - 1, :, r * wide : (r + 1) * wide] for r in range(TAPS) if 0 <= h + r - 1 < height]
        rows.append(sum(near[1:], near[0]))
    return rows


def column_sum(row):
    ring, width = row.shape[1], row.shape[2] // TAPS
    before = pltpu.roll(row[:, :, 0:width], 1, 1)
    after = pltpu.roll(row[:, :, 2 * width : 3 * width], ring - 1, 1)
    return before + row[:, :, width : 2 * width] + after


def conv_sum(padded, weight_ref, bias_row):
    frames, height, ring, channels = padded.shape[0] - PAST, padded.shape[1], padded.shape[2], padded.shape[3]
    windows = [padded[t : t + frames].reshape(frames * height * ring, channels) for t in range(TAPS)]
    product = multiply(windows, weight_ref, range(TAPS)).reshape(frames, height, ring, -1)
    return [column_sum(row) + bias_row for row in row_sums(product)]


def add_rows(padded, rows, weight_ref, total):
    frames, height, ring, channels = padded.shape[0] - PAST, padded.shape[1], padded.shape[2], padded.shape[3]
    windows = [padded[t : t + frames].reshape(frames * height * ring, channels) for t in range(TAPS)]
    product = multiply(windows, weight_ref, range(TAPS)).reshape(frames, height, ring, -1)
    wide = product.shape[3] // TAPS
    for i, row in enumerate(rows):
        for r in range(TAPS):
            total[row + 2 - r] += column_sum(product[:, i, :, r * wide : (r + 1) * wide])


def frame_terms(frames, wanted):
    groups = {}
    for f in range(frames):
        taps = tuple(t for t in range(TAPS) if wanted(f + t))
        groups.setdefault(taps, []).append(f)
    return [(taps, outs) for taps, outs in groups.items() if taps]


def frame_sums(frame_of, frames, wanted, weight_ref, height, ring, add):
    for taps, outs in frame_terms(frames, wanted):
        windows = [jnp.concatenate([frame_of(f + t) for f in outs], axis=0) for t in taps]
        product = multiply(windows, weight_ref, taps).reshape(len(outs), height, ring, -1)
        for h, row in enumerate(row_sums(product)):
            shifted = column_sum(row)
            for i, f in enumerate(outs):
                add(f, h, shifted[i])


def block_number():
    return lax.axis_index("tm") // 2 * 2 + 1 - lax.axis_index("cols")


def pack_first(rows, out_ref, breadth):
    half = lax.axis_index("tm") % 2
    frames, ring, width = rows[0].shape
    centers = [row[:, 0:breadth].reshape(frames * breadth, width) for row in rows]
    ends = [
        jnp.concatenate(
            [jnp.where(half == 0, row[f, breadth : breadth + 1], row[f, ring - 1 : ring]) for f in range(frames)], axis=0
        )
        for row in rows
    ]
    pack(jnp.concatenate(centers, axis=1), jnp.concatenate(ends, axis=1), out_ref)


def bias_part(bias_ref, row, weight_ref):
    return own_part(bias_ref[...].reshape(1, -1), row, weight_ref.shape[1] // TAPS // TAPS)


def fill_slots(padded, pieces, breadth):
    frames = padded.shape[0]
    picks = [(f, f) for f in range(frames)]
    for i, piece in enumerate(pieces):
        values = piece[...].astype(jnp.float32)
        center, ends = unpack(values, frames * breadth, frames * EDGE, padded.shape[3])
        fill_first(padded, (0, i), center, ends, picks, breadth)


def first_near_body(breadth, ks, *refs):
    *pieces, weight_ref, total, padded = refs
    row = lax.axis_index("rows")
    fill_slots(padded, pieces, breadth)
    total[...] = jnp.zeros_like(total)
    add_rows(padded, [row ^ k for k in ks], weight_ref, total)


def first_late_body(breadth, k, piece_ref, near_ref, weight_ref, bias_ref, out_ref, total, padded):
    row = lax.axis_index("rows")
    fill_slots(padded, [piece_ref], breadth)
    add_rows(padded, [row ^ k], weight_ref, total)
    bias_row = bias_part(bias_ref, row, weight_ref)
    pack_first([total[h + 1] + bias_row for h in range(total.shape[0] - 2)], out_ref, breadth)


def cut_body(count, kept, *refs):
    *pieces, out_ref = refs
    for k, piece in enumerate(pieces):
        blocks = piece.shape[0] // count
        for i in range(blocks):
            out_ref[k, i * kept : (i + 1) * kept] = piece[(i + 1) * count - kept : (i + 1) * count]
        out_ref[k, blocks * kept :] = piece[blocks * count :]


def first_early_body(breadth, height, frames, *refs):
    *pieces, past_ref, weight_ref, bias_ref, out_ref, padded = refs
    row = lax.axis_index("rows")
    for k in range(height):
        past = past_ref[k].astype(jnp.float32)
        past = jnp.where(block_number() > 0, past, jnp.zeros_like(past))
        picks = [(j, frames - PAST + j) for j in range(PAST)]
        center, ends = unpack(past, PAST * breadth, frames * EDGE, padded.shape[3])
        fill_first(padded, (0, row ^ k), center, ends, picks, breadth)
        center, ends = unpack(pieces[k][...].astype(jnp.float32), frames * breadth, frames * EDGE, padded.shape[3])
        fill_first(padded, (PAST, row ^ k), center, ends, [(j, j) for j in range(PAST)], breadth)
    pack_first(conv_sum(padded, weight_ref, bias_part(bias_ref, row, weight_ref)), out_ref, breadth)


def regroup(pieces, gain_ref, held, breadth, frames, store):
    row = lax.axis_index("rows")
    half = lax.axis_index("tm") % 2
    height, channels = len(pieces), held.shape[2]
    width = channels // height
    count = frames * breadth
    for k, piece in enumerate(pieces):
        center, ends = unpack(piece[...].astype(jnp.float32), count, frames, channels)
        held[row ^ k, 0:count] = center
        held[row ^ k, count : count + frames] = ends
    gain_values = gain_ref[...].reshape(1, channels)
    for h in range(height):
        joined = [held[s, :, h * width : (h + 1) * width] for s in range(height)]
        values = activate(jnp.concatenate(joined, axis=1), gain_values)
        for f in range(frames):
            end = frames * breadth + f
            ring = ring_of(values[f * breadth : (f + 1) * breadth], values[end : end + 1], half)
            store(h, f, ring.astype(jnp.bfloat16))


def regroup_body(breadth, *refs):
    *pieces, gain_ref, out_ref, last_ref, held = refs
    middle, late = out_ref.shape[1], last_ref.shape[1]

    def store(h, f, ring):
        if f < middle:
            out_ref[h, f] = ring
        else:
            last_ref[h, f - middle] = ring

    regroup(pieces, gain_ref, held, breadth, middle + late, store)


def second_late_body(frames, middle_ref, last_ref, weight_ref, total):
    height, middle, ring, channels = middle_ref.shape

    def frame_of(p):
        p -= 2 * PAST
        values = middle_ref[:, p] if p < middle else last_ref[:, p - middle]
        return values.reshape(height * ring, channels)

    def add(f, h, values):
        total[h, f - PAST] = values

    frame_sums(frame_of, frames, lambda p: p >= 2 * PAST, weight_ref, height, ring, add)


def second_past_body(past_ref, weight_ref, total):
    height, _, ring, channels = past_ref.shape

    def frame_of(p):
        values = past_ref[:, p]
        return jnp.where(block_number() > 0, values, jnp.zeros_like(values)).reshape(height * ring, channels)

    def add(f, h, values):
        total[h, f] = values

    frame_sums(frame_of, PAST, lambda p: p < PAST, weight_ref, height, ring, add)


def second_body(breadth, *refs):
    height = (len(refs) - 8) // 2
    pieces, refs = refs[:height], refs[height:]
    late_ref, past_ref, gain_ref, weight_ref, bias_ref = refs[:5]
    outs, (early, held, branch) = refs[5 : 5 + height], refs[5 + height :]
    row = lax.axis_index("rows")

    def store(h, f, ring):
        early[f, h] = ring

    regroup(pieces, gain_ref, held, breadth, PAST, store)
    _, frames, ring, _ = late_ref.shape
    frames += PAST
    channels = early.shape[3]
    sums = {}

    def held_sum(f, h):
        return past_ref[h, f] if f < PAST else late_ref[h, f - PAST]

    def add(f, h, values):
        sums[f, h] = held_sum(f, h) + values

    def frame_of(p):
        return early[p - PAST].reshape(height * ring, channels)

    frame_sums(frame_of, frames, lambda p: PAST <= p < 2 * PAST, weight_ref, height, ring, add)
    bias_row = bias_part(bias_ref, row, weight_ref)
    for h in range(height):
        for f in range(frames):
            values = sums[f, h] if (f, h) in sums else held_sum(f, h)
            branch[h, f * breadth : (f + 1) * breadth] = values[0:breadth] + bias_row
    for k, out_ref in enumerate(outs):
        chosen = branch[row ^ k]
        rows = out_ref.shape[0]
        parts = [chosen[i * rows : (i + 1) * rows] for i in range(height)]
        out_ref[...] = jnp.concatenate(parts, axis=1).astype(jnp.bfloat16)


def last_body(latents_ref, *refs):
    *pieces, out_ref, held = refs
    row = lax.axis_index("rows")
    height = len(pieces)
    frames, breadth, channels = latents_ref.shape
    width = channels // height
    for k, piece in enumerate(pieces):
        values = piece[...].astype(jnp.float32)
        parts = [values[:, i * width : (i + 1) * width] for i in range(height)]
        held[row ^ k] = jnp.concatenate(parts, axis=0)
    branch = jnp.concatenate([held[s] for s in range(height)], axis=1)
    branch = branch[0 : frames * breadth].reshape(frames, breadth, channels)
    out_ref[...] = (latents_ref[...].astype(jnp.float32) + branch).astype(jnp.bfloat16)


def shards(shape, latents, gain_one, conv_one, bias_one, gain_two, conv_two, bias_two):
    rows, tm, cols = (shape[name] for name in AXES)
    frames, height, breadth, channels = latents.shape
    width = channels // rows
    ring = breadth + 8
    late, middle = frames - PAST, frames - 2 * PAST
    bf16, f32 = jnp.bfloat16, jnp.float32
    own = latents.reshape(frames, breadth, channels)
    every = [(z, x, c) for z in range(rows) for x in range(tm) for c in range(cols)]
    place = {device: i for i, device in enumerate(every)}

    def moved(values, target):
        return lax.ppermute(values, AXES, [(place[device], place[target(*device)]) for device in every])

    def turned(values, k):
        return moved(values, lambda z, x, c: (z ^ k, x // 2 * 2 + c, 1 - x % 2))

    def returned(values, k):
        return moved(values, lambda z, x, c: (z ^ k, x // 2 * 2 + 1 - c, x % 2))

    def following(values):
        return moved(values, lambda z, x, c: (z, x, 0) if c == 1 else (z, (x + 2) % tm, 1))

    def handed(values, k):
        return lax.ppermute(values, "rows", [(z, z ^ k) for z in range(rows)])

    def spread(values):
        parts = [values]
        for k in range(1, rows):
            parts.append(handed(values, k))
        return parts

    def turn(values, way):
        parts = []
        for k in range(rows):
            parts.append(way(values[k], k))
        return parts

    def gather(values):
        parts = []
        for k in range(rows):
            parts.append(handed(parts[k - 1], 1) if k % 2 and k > 1 else turned(values, k))
        return parts

    other = lax.ppermute(own, "cols", [(0, 1), (1, 0)])
    weights = [w.reshape(TAPS, TAPS * TAPS * width, channels) for w in (conv_one, conv_two)]
    sds = jax.ShapeDtypeStruct
    size = frames * ring * channels
    work = 2 * ring * channels * rows * 27 * width

    def padded(count):
        return VMEM((count, rows, ring, channels), bf16)

    center, gain_one = call(
        own_body, [sds((frames * breadth * channels // LANES, LANES), bf16), sds(gain_one.shape, f32)],
        [VMEM((frames, breadth, channels), bf16), pltpu.SemaphoreType.DMA((2,))],
        10 * size, 6 * size, own, gain_one, far=(0, 1),
    )
    total = packed_rows(frames * breadth, EDGE * frames, channels)
    band = call(ends_body, sds((total, LANES), bf16), [], size, 4 * size, center, other, gain_one)
    pieces = gather(band)
    small = (bias_one, gain_two, bias_two, weights[0])
    bias_one, gain_two, bias_two, near = call(
        stage_body, [sds(v.shape, v.dtype) for v in small], [pltpu.SemaphoreType.DMA((len(small),))],
        size, 4 * size, *small, far=range(len(small)),
    )
    past_rows = packed_rows(PAST * breadth, EDGE * frames, channels)
    past = call(
        functools.partial(cut_body, frames * breadth, PAST * breadth), sds((rows, past_rows, LANES), bf16), [],
        size, 4 * size, *pieces,
    )
    past = following(past)
    late_sent, early_sent = (packed_rows(count * breadth, count, channels) for count in (late, PAST))
    late_rows, early_rows = (padded_rows(count * (breadth + 1)) for count in (late, PAST))
    *ks, last_k = band_order(rows)
    sums = sds((rows + 2, late, ring, width), f32)
    near_sums = call(
        functools.partial(first_near_body, breadth, ks), sums,
        [VMEM((frames, rows - 1, ring, channels), bf16)], late * work * (rows - 1) // rows, 10 * size,
        *[pieces[k] for k in ks], near,
    )
    part, _ = call(
        functools.partial(first_late_body, breadth, last_k), [sds((late_sent, LANES), bf16), sums],
        [VMEM((frames, 1, ring, channels), bf16)], late * work // rows, 10 * size,
        pieces[last_k], near_sums, near, bias_one, aliases={1: 1},
    )
    late_parts = spread(part)
    part = call(
        functools.partial(first_early_body, breadth, rows, frames), sds((early_sent, LANES), bf16),
        [padded(2 * PAST)], PAST * work, 20 * size, *pieces, past, near, bias_one,
    )
    early_parts = spread(part)
    second, last = call(
        functools.partial(regroup_body, breadth),
        [sds((rows, middle, ring, channels), bf16), sds((rows, PAST, ring, channels), bf16)],
        [VMEM((rows, late_rows, channels), f32)], 10 * size * rows, 4 * size * rows, *late_parts, gain_two,
    )
    past = following(last)
    back_rows = padded_rows(-(-frames * breadth // rows))
    late_sums = call(
        functools.partial(second_late_body, frames), sds((rows, late, ring, width), f32), [],
        frames * work // 3, 10 * size, second, last, weights[1],
    )
    past_sums = call(
        second_past_body, sds((rows, PAST, ring, width), f32), [],
        frames * work // 5, 10 * size, past, weights[1],
    )
    branch = call(
        functools.partial(second_body, breadth), [sds((back_rows, channels), bf16)] * rows,
        [padded(PAST), VMEM((rows, early_rows, channels), f32), VMEM((rows, back_rows * rows, width), f32)],
        frames * work // 2, 20 * size, *early_parts, late_sums, past_sums, gain_two, weights[1], bias_two,
    )
    branch = turn(branch, returned)
    result = call(
        last_body, sds((frames, breadth, channels), bf16), [VMEM((rows, back_rows * rows, width), f32)],
        2 * size, 6 * size, own, *branch,
    )
    return result.reshape(frames, height, breadth, channels)


def band_order(rows):
    return [1, *range(rows - 2, 0, -2), 0, *range(3, rows, 2)]


def solution(mesh):
    shape = dict(mesh.shape)
    return jax.shard_map(
        functools.partial(shards, shape),
        mesh=mesh,
        in_specs=(
            P(("groups", "tm"), "rows", "cols", None),
            P(),
            P(None, "rows", None),
            P(),
            P(),
            P(None, "rows", None),
            P(),
        ),
        out_specs=P(("groups", "tm"), "rows", "cols", None),
        check_vma=False,
    )
```
